256 devices in a mesh: row: 8 (over z_hi, core), col: 32 (over z_lo, y, x).
Axes of the slice: x: 4, y: 4, z: 8 (z_hi: 4, z_lo: 2; z = z_hi * 2 + z_lo), core: 2. Of those that a mesh axis runs over, the one named last changes fastest.
Arguments:
- object_in: float32 [2, 2, 2048, 8192], P(None, None, 'row', 'col'), may hold values from -4 to 4
- probe_in: float32 [2, 256, 256], replicated, may hold values from -5 to 5
- positions: int32 [8, 32, 2, 2], P('row', 'col'), may hold values from -32 to 32
- intensity: float32 [8, 32, 2, 256, 256], P('row', 'col'), may hold values from 0.1 to 8.2
Outputs:
- object_out: float32 [2, 2, 2048, 8192], P(None, None, 'row', 'col')
- probe_out: float32 [2, 256, 256], replicated
The draws below stay inside these ranges and needn't reach their ends.
Inputs may be any that keep to these rules, and one draw needn't show every extreme that they name: positions[r, c, p] = (dy, dx) places the probe of position p on object rows r * 256 + dy to r * 256 + dy + 255 and columns c * 256 + dx to c * 256 + dx + 255.
All inputs are finite; a program needn't handle non-finite values.
Results may differ from the reference program's by a relative error of at most 0.0003.
Values sent between devices are 32-bit elements; how exact they have to be, the bound alone decides.
A program may use at most 64 MiB of HBM per device.

```python
import math
import jax
import jax.numpy as jnp
from jax import lax

PR = 256
CORE = 256
RIM = 32
NPOS = 2
ITERS = 1
TROWS = 8
TCOLS = 32
TILES = 256
NY = 2048
NX = 8192


def draw_intensity(key, part):
    shape_all = (TROWS, TCOLS, NPOS, PR, PR)
    tile_number = (jnp.arange(TROWS, dtype=jnp.int32)[:, None] * TCOLS + jnp.arange(TCOLS, dtype=jnp.int32)[None, :]).astype(jnp.float32)
    rising = 1.0 + 2.0 * tile_number / max(TILES - 1, 1)
    base_values = jnp.exp(jax.random.uniform(key, shape_all, jnp.float32, -2.0, 1.0))
    return (base_values * rising[:, :, None, None, None]).astype(jnp.float32)


def touch_ends(entries, stream_key, least, top_value):
    shape = entries.shape
    spot = [jax.random.randint(jax.random.fold_in(stream_key, axis), (), 0, shape[axis]) for axis in range(len(shape))]
    entries = entries.at[tuple(spot)].set(least)
    longest = shape.index(max(shape))
    spot[longest] = (spot[longest] + 1) % shape[longest]
    return entries.at[tuple(spot)].set(top_value)


def shard_levels(stream_key, shape, cuts, least, high):
    def one(axis_at, blocks):
        heights = jax.random.uniform(jax.random.fold_in(jax.random.fold_in(stream_key, 6), axis_at), (blocks,), jnp.float32, least / len(cuts), high / len(cuts))
        return jnp.repeat(jnp.exp(heights), shape[axis_at] // blocks).reshape((-1,) + (1,) * (len(shape) - axis_at - 1))

    factor_of = one(*cuts[0])
    for cut in cuts[1:]:
        factor_of = factor_of * one(*cut)
    return factor_of


def normal_values(stream_key, shape, spread, reach, cuts=(), kind=jnp.bfloat16):
    values = spread * jax.random.normal(stream_key, shape, jnp.float32)
    if cuts:
        values = values * shard_levels(stream_key, shape, cuts, -0.22, 0.18)
    return jnp.clip(values, -reach, reach).astype(kind)


def setup_inputs(seed: int = 0) -> dict:
    arg_keys = jax.random.split(jax.random.key(seed), 5)
    return {
        "object_in": normal_values(arg_keys[0], (2, 2, NY, NX), 0.7, 4.0, ((2, 8), (3, 32)), jnp.float32),
        "probe_in": normal_values(arg_keys[1], (2, PR, PR), 1.0, 5.0, (), jnp.float32),
        "positions": touch_ends(jax.random.randint(arg_keys[2], (TROWS, TCOLS, NPOS, 2), -RIM, RIM + 1), jax.random.fold_in(arg_keys[2], 1), -RIM, RIM).astype(jnp.int32),
        "intensity": draw_intensity(jax.random.fold_in(arg_keys[4], 71), 0),
    }


def tables(extent):
    line_idx = jnp.arange(extent, dtype=jnp.int32)
    turn_count = line_idx[:, None] * line_idx[None, :] % extent
    angles = turn_count.astype(jnp.float32) * (2.0 * math.pi / extent)
    factor = 1.0 / math.sqrt(extent)
    cosine = jnp.cos(angles) * factor
    sine_tab = jnp.sin(angles) * factor
    frequency = ((line_idx + extent // 2) % extent - extent // 2).astype(jnp.float32)
    phases = -math.pi * 8.0 / (extent * extent) * (frequency[:, None] ** 2 + frequency[None, :] ** 2)
    return (cosine, sine_tab, jnp.cos(phases), jnp.sin(phases))

def matrices(cosine, sine_tab, orient):
    return (cosine, sine_tab, float(orient))

def transform(real_part, imag_part, tables_pair):
    cosine, sine_tab, orient = tables_pair
    high = lax.Precision.HIGHEST
    rc = jnp.einsum('byx,xk->byk', real_part, cosine, precision=high)
    rs = jnp.einsum('byx,xk->byk', real_part, sine_tab, precision=high)
    ic = jnp.einsum('byx,xk->byk', imag_part, cosine, precision=high)
    isn = jnp.einsum('byx,xk->byk', imag_part, sine_tab, precision=high)
    mid_re = rc + orient * isn
    mid_im = ic - orient * rs
    out_re = jnp.einsum('ky,byx->bkx', cosine, mid_re, precision=high) + orient * jnp.einsum('ky,byx->bkx', sine_tab, mid_im, precision=high)
    out_im = jnp.einsum('ky,byx->bkx', cosine, mid_im, precision=high) - orient * jnp.einsum('ky,byx->bkx', sine_tab, mid_re, precision=high)
    return (out_re, out_im)

def times_plain(first_re, first_im, second_re, second_im):
    return (first_re * second_re - first_im * second_im, first_re * second_im + first_im * second_re)

def times_conj(first_re, first_im, second_re, second_im):
    return (first_re * second_re + first_im * second_im, first_re * second_im - first_im * second_re)

def tile_gradient(window, probe, offsets, measured, constants):
    cosine, sine_tab, kern_re, kern_im = constants
    forward = matrices(cosine, sine_tab, 1)
    backward = matrices(cosine, sine_tab, -1)
    extent = probe.shape[-1]
    zero_idx = jnp.zeros((), jnp.int32)

    def cut_patch(offset):
        return lax.dynamic_slice(window, (zero_idx, zero_idx, (offset[0] + RIM).astype(jnp.int32), (offset[1] + RIM).astype(jnp.int32)), (2, 2, extent, extent))
    patches = jax.vmap(cut_patch)(offsets)
    first_re, first_im = (patches[:, 0, 0], patches[:, 0, 1])
    second_re, second_im = (patches[:, 1, 0], patches[:, 1, 1])
    probe_re, probe_im = (probe[0], probe[1])
    wave_re, wave_im = times_plain(probe_re, probe_im, first_re, first_im)
    spec_re, spec_im = transform(wave_re, wave_im, forward)
    spec_re, spec_im = times_plain(kern_re, kern_im, spec_re, spec_im)
    prop_re, prop_im = transform(spec_re, spec_im, backward)
    exit_re, exit_im = times_plain(prop_re, prop_im, second_re, second_im)
    far_re, far_im = transform(exit_re, exit_im, forward)
    excess = 2.0 * (far_re * far_re + far_im * far_im - measured)
    back_re, back_im = transform(excess * far_re, excess * far_im, backward)
    grad2_re, grad2_im = times_conj(prop_re, prop_im, back_re, back_im)
    lift_re, lift_im = times_conj(second_re, second_im, back_re, back_im)
    lift_re, lift_im = transform(lift_re, lift_im, forward)
    lift_re, lift_im = times_conj(kern_re, kern_im, lift_re, lift_im)
    enter_re, enter_im = transform(lift_re, lift_im, backward)
    grad1_re, grad1_im = times_conj(probe_re, probe_im, enter_re, enter_im)
    probe_re_g, probe_im_g = times_conj(first_re, first_im, enter_re, enter_im)
    probe_grad = jnp.stack([lax.optimization_barrier(jnp.sum(probe_re_g, 0)), lax.optimization_barrier(jnp.sum(probe_im_g, 0))], 0)
    pieces = jnp.stack([jnp.stack([grad1_re, grad1_im], 1), jnp.stack([grad2_re, grad2_im], 1)], 1)
    gradient = jnp.zeros(window.shape, window.dtype)
    for position in range(offsets.shape[0]):
        start_at = (zero_idx, zero_idx, (offsets[position, 0] + RIM).astype(jnp.int32), (offsets[position, 1] + RIM).astype(jnp.int32))
        current = lax.dynamic_slice(gradient, start_at, pieces.shape[1:])
        gradient = lax.dynamic_update_slice(gradient, current + pieces[position], start_at)
    return (gradient, probe_grad)

def reference(object_in, probe_in, positions, intensity):
    constants = tables(PR)
    current = object_in
    probe = probe_in
    offsets_all = positions.reshape(TILES, NPOS, 2)
    measured_all = intensity.reshape(TILES, NPOS, PR, PR)
    span = CORE + 2 * RIM
    zero_idx = jnp.zeros((), jnp.int32)
    for iteration in range(ITERS):
        padded = jnp.pad(current, ((0, 0), (0, 0), (RIM, RIM), (RIM, RIM)))

        def visit(tile, carry):
            accum, probe_total = carry
            tile_idx = jnp.asarray(tile).astype(jnp.int32)
            row_idx = tile_idx // TCOLS
            col_idx = tile_idx % TCOLS
            start_at = (zero_idx, zero_idx, (row_idx * CORE).astype(jnp.int32), (col_idx * CORE).astype(jnp.int32))
            window = lax.dynamic_slice(padded, start_at, (2, 2, span, span))
            offsets = lax.dynamic_index_in_dim(offsets_all, tile_idx, 0, keepdims=False)
            measured = lax.dynamic_index_in_dim(measured_all, tile_idx, 0, keepdims=False)
            gradient, probe_grad = tile_gradient(window, probe, offsets, measured, constants)
            placed = lax.dynamic_slice(accum, start_at, (2, 2, span, span)) + gradient
            return (lax.dynamic_update_slice(accum, placed, start_at), probe_total + probe_grad.astype(probe_total.dtype))
        accum, probe_total = lax.fori_loop(0, TILES, visit, (jnp.zeros(padded.shape, padded.dtype), jnp.zeros(probe.shape, probe.dtype)))
        descent = accum[:, :, RIM:RIM + NY, RIM:RIM + NX]
        largest = jnp.max(descent[:, 0] ** 2 + descent[:, 1] ** 2)
        current = current - 0.3 * descent / (jnp.sqrt(largest) + 1e-06)
        probe = probe - 2.0 / TILES * probe_total
    return (current, probe)
```

```python
import functools
import math

import jax
import jax.numpy as jnp
import numpy as np
from jax import lax
from jax.experimental import pallas as pl
from jax.experimental.pallas import tpu as pltpu
from jax.sharding import PartitionSpec as P

RIM = 32
MESH = pl.DeviceIdType.MESH
VMEM = pltpu.VMEM
AROUND = ((-1, 0), (1, 0), (0, -1), (0, 1), (-1, -1), (-1, 1), (1, -1), (1, 1))
CORES = 2
NYX = (4, 4)


def split_of(matrix):
    high = matrix.astype(jnp.bfloat16)
    low = (matrix - high.astype(np.float64)).astype(jnp.bfloat16)
    return np.stack([np.asarray(high), np.asarray(low)])


def stacked(weight):
    real, imag = weight.real, weight.imag
    return np.block([[real, imag], [-imag, real]])


def weights(extent):
    half = extent // 2
    idx = np.arange(extent)
    freq = ((idx + half) % extent - half).astype(np.float64)
    turn = np.exp(-2j * np.pi * ((idx[:, None] * idx[None, :]) % extent) / extent)
    phase = np.exp(-8j * np.pi * freq**2 / extent**2)
    band = (np.conj(turn) * phase[None, :]) @ turn / extent
    left, right = band[:half, :half], band[:half, half:]
    even = turn[:half, 0::2] / math.sqrt(extent)
    odd = turn[:half, 1::2] / math.sqrt(extent)
    plus, minus = stacked((left + right) / 2), stacked((left - right) / 2)
    ev, od = stacked(even), stacked(odd)
    table = np.stack([split_of(m) for m in (plus, minus, ev, od, od.T)])
    order = np.concatenate([idx[0::2], idx[1::2]])
    perm = np.zeros((extent, extent), np.float32)
    perm[order, idx] = 1.0
    return table, perm.astype(jnp.bfloat16)


def parts(x):
    high = x.astype(jnp.bfloat16)
    return high, (x - high.astype(jnp.float32)).astype(jnp.bfloat16)


def dot(a, b):
    return jnp.dot(a, b, preferred_element_type=jnp.float32)


def times_right(x, w_ref, k):
    high, low = parts(x)
    wh, wl = w_ref[k, 0], w_ref[k, 1]
    return dot(jnp.concatenate([high, low, high], 1), jnp.concatenate([wh, wh, wl], 0))


def times_left(x, w_ref, k):
    high, low = parts(x)
    wh, wl = w_ref[k, 0], w_ref[k, 1]
    return dot(jnp.concatenate([wh, wh, wl], 1), jnp.concatenate([high, low, high], 0))


def fold(x):
    h = x.shape[0] // 2
    s, d = x[:h] + x[h:], x[:h] - x[h:]
    return [[s[:, :h] + s[:, h:], s[:, :h] - s[:, h:]], [d[:, :h] + d[:, h:], d[:, :h] - d[:, h:]]]


def unfold(b):
    top_s, top_d = b[0][0] + b[0][1], b[0][0] - b[0][1]
    bot_s, bot_d = b[1][0] + b[1][1], b[1][0] - b[1][1]
    s = jnp.concatenate([top_s, top_d], 1)
    d = jnp.concatenate([bot_s, bot_d], 1)
    return jnp.concatenate([s + d, s - d], 0)


def sandwich(re, im, w_ref, right, left):
    h = re[0][0].shape[0]
    out = [None, None]
    for j in (0, 1):
        k, swap = right[j]
        first, second = (im, re) if swap else (re, im)
        x = jnp.concatenate(
            [jnp.concatenate([first[i][j], second[i][j]], 1) for i in (0, 1)], 0
        )
        y = times_right(x, w_ref, k)
        a, b = y[:, :h], y[:, h:]
        out[j] = (b, a) if swap else (a, b)
    res_re, res_im = [None, None], [None, None]
    for i in (0, 1):
        k, swap = left[i]
        rows = slice(i * h, (i + 1) * h)
        r = jnp.concatenate([out[0][0][rows], out[1][0][rows]], 1)
        m = jnp.concatenate([out[0][1][rows], out[1][1][rows]], 1)
        y = times_left(jnp.concatenate([m, r] if swap else [r, m], 0), w_ref, k)
        a, b = y[:h], y[h:]
        r, m = (b, a) if swap else (a, b)
        res_re[i] = [r[:, :h], r[:, h:]]
        res_im[i] = [m[:, :h], m[:, h:]]
    return res_re, res_im


PROP = (((0, False), (1, False)), ((0, True), (1, True)))
PROP_CONJ = (((0, True), (1, True)), ((0, False), (1, False)))
FORWARD = (((2, False), (3, False)), ((2, True), (4, False)))
BACKWARD = (((2, True), (4, False)), ((2, False), (3, False)))


def tile_kernel(
    pos_ref, obj_ref, top_ref, bottom_ref, left_ref, right_ref, probe_ref, meas_ref, w_ref, perm_ref,
    core_ref, gt_ref, gb_ref, gl_ref, gr_ref, gp_ref,
    win, cut, mid, pad, seen,
):
    n = probe_ref.shape[-1]
    h = n // 2
    npos = cut.shape[0]
    lane = lax.broadcasted_iota(jnp.int32, (8, 128), 1)

    for q in range(4):
        for t in (0, 1):
            cols = slice(128 * t, 128 * t + 128)
            win[q, t + 1, RIM : RIM + n, :] = obj_ref[q, :, cols]
            win[q, t + 1, :RIM, :] = top_ref[q, :, cols]
            win[q, t + 1, RIM + n :, :] = bottom_ref[q, :, cols]
        win[q, 0] = pltpu.roll(left_ref[...], (96 - 32 * q) % 128, 1)
        win[q, 3] = pltpu.roll(right_ref[...], (128 - 32 * q) % 128, 1) if q else right_ref[...]
    zeros = jnp.zeros((64, 128), jnp.float32)
    for p in range(npos):
        for q in range(4):
            for t in (0, 1):
                pad[p, q, t, 0:64, :] = zeros
                pad[p, q, t, 64 + n :, :] = zeros

    def keep(p, q, value):
        pad[p, q, 0, 64 : 64 + n, :] = value[:, :128]
        pad[p, q, 1, 64 : 64 + n, :] = value[:, 128:]

    offs = [(pos_ref[2 * p], pos_ref[2 * p + 1]) for p in range(npos)]

    def cut_rows(i, carry):
        at = pl.multiple_of(i * 8, 8)
        for p in range(npos):
            dy, dx = offs[p]
            shift = lax.rem(128 - dx, 128)
            high, low = lane >= 128 - dx, lane < -dx
            for q in range(4):
                rows = pl.ds(RIM + dy + i * 8, 8)
                r = [pltpu.roll(win[q, t, rows, :], shift, 1) for t in range(4)]
                for t in (1, 2):
                    cut[p, q, pl.ds(at, 8), 128 * (t - 1) : 128 * t] = jnp.where(
                        high, r[t + 1], jnp.where(low, r[t - 1], r[t])
                    )
        return carry

    lax.fori_loop(0, n // 8, cut_rows, 0)

    for p in range(npos):
        pr, pi = probe_ref[0], probe_ref[1]
        ar, ai = cut[p, 0], cut[p, 1]
        re, im = sandwich(fold(pr * ar - pi * ai), fold(pr * ai + pi * ar), w_ref, *PROP)
        qr, qi = unfold(re), unfold(im)
        mid[p, 0], mid[p, 1] = qr, qi
        br, bi = cut[p, 2], cut[p, 3]
        re, im = sandwich(fold(qr * br - qi * bi), fold(qr * bi + qi * br), w_ref, *FORWARD)
        for t in (0, 1):
            seen[p, t] = meas_ref[p, :, 128 * t : 128 * t + 128]
        meas = jnp.concatenate(
            [
                jnp.concatenate([seen[p, t, pl.ds(i, h, stride=2), :] for t in (0, 1)], 1)
                for i in (0, 1)
            ],
            0,
        )
        mh, ml = parts(meas)
        meas = dot(jnp.concatenate([mh, ml], 1), jnp.concatenate([perm_ref[...], perm_ref[...]], 0))
        for i in (0, 1):
            for j in (0, 1):
                fr, fi = re[i][j], im[i][j]
                ex = 2.0 * (fr * fr + fi * fi - meas[i * h : (i + 1) * h, j * h : (j + 1) * h])
                re[i][j], im[i][j] = ex * fr, ex * fi
        re, im = sandwich(re, im, w_ref, *BACKWARD)
        hr, hi = unfold(re), unfold(im)
        qr, qi = mid[p, 0], mid[p, 1]
        keep(p, 2, qr * hr + qi * hi)
        keep(p, 3, qr * hi - qi * hr)
        br, bi = cut[p, 2], cut[p, 3]
        re, im = sandwich(fold(br * hr + bi * hi), fold(br * hi - bi * hr), w_ref, *PROP_CONJ)
        er, ei = unfold(re), unfold(im)
        pr, pi = probe_ref[0], probe_ref[1]
        keep(p, 0, pr * er + pi * ei)
        keep(p, 1, pr * ei - pi * er)
        ar, ai = cut[p, 0], cut[p, 1]
        if p == 0:
            gp_ref[0] = ar * er + ai * ei
            gp_ref[1] = ar * ei - ai * er
        else:
            gp_ref[0] += ar * er + ai * ei
            gp_ref[1] += ar * ei - ai * er

    quarter = lax.div(lane, 32)

    def place(i, mid_ref, first):
        at = pl.multiple_of((i - first) * 8, 8)
        left = right = None
        for q in range(4):
            sums = None
            for p in range(npos):
                dy, dx = offs[p]
                shift = lax.rem(128 + dx, 128)
                low, high = lane < dx, lane >= 128 + dx
                rows = pl.ds(RIM - dy + i * 8, 8)
                a, b = (pltpu.roll(pad[p, q, t, rows, :], shift, 1) for t in (0, 1))
                o = jnp.zeros_like(a)
                got = [
                    jnp.where(high, a, o),
                    jnp.where(low, o, jnp.where(high, b, a)),
                    jnp.where(low, a, jnp.where(high, o, b)),
                    jnp.where(low, b, o),
                ]
                sums = got if sums is None else [u + v for u, v in zip(sums, got)]
            mid_ref[q, pl.ds(at, 8), 0:128] = sums[1]
            mid_ref[q, pl.ds(at, 8), 128:256] = sums[2]
            lft = pltpu.roll(sums[0], (32 * q + 32) % 128, 1)
            rgt = pltpu.roll(sums[3], 32 * q, 1) if q else sums[3]
            left = lft if left is None else jnp.where(quarter == q, lft, left)
            right = rgt if right is None else jnp.where(quarter == q, rgt, right)
        row = pl.multiple_of(i * 8, 8)
        gl_ref[pl.ds(row, 8), :] = left
        gr_ref[pl.ds(row, 8), :] = right

    k = RIM // 8

    def loop(lo, hi, ref):
        def step(i, carry):
            place(i, ref, lo)
            return carry

        lax.fori_loop(lo, hi, step, 0)

    loop(0, k, gt_ref)
    loop(k, k + n // 8, core_ref)
    loop(k + n // 8, 2 * k + n // 8, gb_ref)


def place_of():
    return lax.axis_index("row"), lax.axis_index("col")


def neighbours(rows, cols):
    r, c = place_of()
    out = []
    for dr, dc in AROUND:
        ok = None
        if dr:
            ok = r > 0 if dr < 0 else r < rows - 1
        if dc:
            side = c > 0 if dc < 0 else c < cols - 1
            ok = side if ok is None else jnp.logical_and(ok, side)
        out.append((ok, (r + dr, c + dc)))
    return out


def opposite(d):
    dr, dc = AROUND[d]
    return AROUND.index((-dr, -dc))


def greet(rows, cols, extra=()):
    barrier = pltpu.get_barrier_semaphore()
    r, c = place_of()
    for ok, where in neighbours(rows, cols):

        @pl.when(ok)
        def _(where=where):
            pl.semaphore_signal(barrier, inc=1, device_id=where, device_id_type=MESH)

    for where in extra:
        pl.semaphore_signal(barrier, inc=1, device_id=where, device_id_type=MESH)
    tall = 1 + jnp.where(r > 0, 1, 0) + jnp.where(r < rows - 1, 1, 0)
    wide = 1 + jnp.where(c > 0, 1, 0) + jnp.where(c < cols - 1, 1, 0)
    pl.semaphore_wait(barrier, tall * wide - 1 + len(extra))


def swap_rims(rows, cols, sources, targets, send_sem, recv_sem):
    for d, (ok, where) in enumerate(neighbours(rows, cols)):
        copy = pltpu.make_async_remote_copy(
            src_ref=sources[d],
            dst_ref=targets[opposite(d)],
            send_sem=send_sem.at[d],
            recv_sem=recv_sem.at[opposite(d)],
            device_id=where,
            device_id_type=MESH,
        )
        pl.when(ok)(copy.start)
        target = targets[d]

        @pl.when(jnp.logical_not(ok))
        def _(target=target):
            target[...] = jnp.zeros(target.shape, target.dtype)


def finish_rims(rows, cols, sources, targets, send_sem, recv_sem):
    for d, (ok, where) in enumerate(neighbours(rows, cols)):
        sent = pltpu.make_async_remote_copy(
            src_ref=sources[d],
            dst_ref=targets[d],
            send_sem=send_sem.at[d],
            recv_sem=recv_sem.at[d],
            device_id=where,
            device_id_type=MESH,
        )
        pl.when(ok)(sent.wait)


def halo_kernel(rows, cols, obj_ref, top_ref, bottom_ref, left_ref, right_ref, pl_buf, pr_buf, send_sem, recv_sem):
    n = obj_ref.shape[-1]
    lane = lax.broadcasted_iota(jnp.int32, (n, 128), 1)
    quarter = lax.div(lane, 32)
    left = obj_ref[0, :, 0:128]
    right = pltpu.roll(obj_ref[0, :, n - 128 :], 32, 1)
    for q in range(1, 4):
        left = jnp.where(quarter == q, pltpu.roll(obj_ref[q, :, 0:128], 32 * q, 1), left)
        right = jnp.where(
            quarter == q, pltpu.roll(obj_ref[q, :, n - 128 :], (32 * q + 32) % 128, 1), right
        )
    pl_buf[...] = left
    pr_buf[...] = right
    greet(rows, cols)
    lo, hi = pl.ds(0, RIM), pl.ds(n - RIM, RIM)
    sources = [
        obj_ref.at[:, lo, :], obj_ref.at[:, hi, :], pl_buf, pr_buf,
        pl_buf.at[lo, :], pr_buf.at[lo, :], pl_buf.at[hi, :], pr_buf.at[hi, :],
    ]
    first, core, last = pl.ds(0, RIM), pl.ds(RIM, n), pl.ds(RIM + n, RIM)
    targets = [
        top_ref, bottom_ref, left_ref.at[core, :], right_ref.at[core, :],
        left_ref.at[first, :], right_ref.at[first, :], left_ref.at[last, :], right_ref.at[last, :],
    ]
    swap_rims(rows, cols, sources, targets, send_sem, recv_sem)
    finish_rims(rows, cols, sources, targets, send_sem, recv_sem)


def sum_kernel(
    rows, cols, nyx,
    gp_ref, core_ref, gt_ref, gb_ref, gl_ref, gr_ref,
    total_ref, descent_ref, peak_ref,
    theirs, ours, slots, zslots, mine, zpeak, xpeak, ppeak,
    rt, rb, rl, rr, corners,
    send_rim, recv_rim, send_pair, recv_pair, send_xy, recv_xy, send_z, recv_z,
    send_zm, recv_zm, send_xm, recv_xm, send_all, recv_all, send_back, recv_back, send_pm, recv_pm,
):
    n = gp_ref.shape[-1]
    ny, nx = nyx
    nxy = ny * nx
    nzl = cols // nxy
    nz = nzl * (rows // CORES)
    step = n // nxy
    r, c = place_of()
    core, zh = lax.rem(r, CORES), lax.div(r, CORES)
    zl, here = lax.div(c, nxy), lax.rem(c, nxy)
    y, x = lax.div(here, nx), lax.rem(here, nx)
    z = zh * nzl + zl
    partner = (zh * CORES + 1 - core, c)

    def peer(d):
        oy, ox = lax.div(d, nx), lax.rem(d, nx)
        q = lax.rem(y + oy, ny) * nx + lax.rem(x + ox, nx)
        return q, (r, zl * nxy + q)

    def source_of(d):
        oy, ox = lax.div(d, nx), lax.rem(d, nx)
        return lax.rem(y + ny - oy, ny) * nx + lax.rem(x + nx - ox, nx)

    def zpeer(d):
        k = lax.rem(z + d, nz)
        return k, (lax.div(k, nzl) * CORES + core, lax.rem(k, nzl) * nxy + here)

    extra = [partner]
    extra += [peer(jnp.int32(d))[1] for d in range(1, nxy)]
    extra += [zpeer(jnp.int32(d))[1] for d in range(1, nz)]
    greet(rows, cols, extra)

    def remote(src, dst, ssem, rsem, where):
        return pltpu.make_async_remote_copy(
            src_ref=src, dst_ref=dst, send_sem=ssem, recv_sem=rsem, device_id=where, device_id_type=MESH
        )

    def band(q):
        return pl.ds(pl.multiple_of(q * step, step), step)

    def pair(d):
        q, _ = peer(d)
        return remote(
            gp_ref.at[1 - core, band(q), :], theirs.at[band(q), :], send_pair.at[d], recv_pair.at[d], partner
        )

    def spread(d):
        q, where = peer(d)
        return remote(ours.at[band(q), :], slots.at[d], send_xy.at[d], recv_xy.at[d], where)

    def each(count, body, low=0):
        def go(i, carry):
            body(count - 1 - i)
            return carry

        lax.fori_loop(0, count - low, go, 0)

    each(nxy, lambda d: pair(d).start())

    lo, hi = pl.ds(0, RIM), pl.ds(RIM + n, RIM)
    mid = pl.ds(RIM, n)
    sources = [
        gt_ref, gb_ref, gl_ref.at[mid, :], gr_ref.at[mid, :],
        gl_ref.at[lo, :], gr_ref.at[lo, :], gl_ref.at[hi, :], gr_ref.at[hi, :],
    ]
    targets = [rt, rb, rl, rr, corners.at[0], corners.at[1], corners.at[2], corners.at[3]]
    swap_rims(rows, cols, sources, targets, send_rim, recv_rim)

    def pass_on(d):
        q, _ = peer(d)
        pair(d).wait_recv()
        ours[band(q), :] = gp_ref[core, band(q), :] + theirs[band(q), :]

    def pass_and_send(d):
        pass_on(d)
        spread(d).start()

    each(nxy, pass_and_send, 1)
    pass_on(jnp.int32(0))

    finish_rims(rows, cols, sources, targets, send_rim, recv_rim)
    lane = lax.broadcasted_iota(jnp.int32, (RIM, 128), 1)
    first, final = lane < 32, lane >= 96

    def rows_of(at, up, low):
        zero = jnp.zeros((RIM, 128), jnp.float32)
        best = None
        for s in (0, 1):
            planes = []
            for q in (2 * s, 2 * s + 1):
                a = core_ref[q, pl.ds(at, RIM), 0:128]
                b = core_ref[q, pl.ds(at, RIM), 128:256]
                lft, rgt = rl[pl.ds(at, RIM), :], rr[pl.ds(at, RIM), :]
                if up is not None:
                    lft, rgt = lft + corners[up], rgt + corners[up + 1]
                if low is not None:
                    a, b = a + low[q, :, 0:128], b + low[q, :, 128:256]
                lft = pltpu.roll(lft, (128 - 32 * q) % 128, 1) if q else lft
                rgt = pltpu.roll(rgt, (96 - 32 * q) % 128, 1) if q < 3 else rgt
                a = a + jnp.where(first, lft, zero)
                b = b + jnp.where(final, rgt, zero)
                descent_ref[q, pl.ds(at, RIM), 0:128] = a
                descent_ref[q, pl.ds(at, RIM), 128:256] = b
                planes.append((a, b))
            for t in (0, 1):
                v = planes[0][t] * planes[0][t] + planes[1][t] * planes[1][t]
                best = v if best is None else jnp.maximum(best, v)
        return functools.reduce(jnp.maximum, [best[8 * k : 8 * k + 8] for k in range(RIM // 8)])

    peak = jnp.maximum(rows_of(0, 0, rt), rows_of(n - RIM, 2, rb))
    peak = lax.fori_loop(
        1, n // RIM - 1, lambda i, m: jnp.maximum(m, rows_of(pl.multiple_of(i * RIM, RIM), None, None)), peak
    )
    zpeak[pl.ds(z, 1)] = peak[None]

    def to_z(d):
        return remote(mine, zslots.at[z], send_z.at[d], recv_z.at[d], zpeer(d)[1])

    def peak_to_z(d):
        return remote(zpeak.at[z], zpeak.at[z], send_zm.at[d], recv_zm.at[d], zpeer(d)[1])

    each(nz, lambda d: peak_to_z(d).start(), 1)
    each(nxy, lambda d: spread(d).wait_recv(), 1)
    acc = ours[band(here), :]
    for d in range(1, nxy):
        acc = acc + slots[d]
    mine[...] = acc
    zslots[pl.ds(z, 1)] = acc[None]
    each(nz, lambda d: to_z(d).start(), 1)

    def z_arrived(d):
        to_z(d).wait_recv()
        peak_to_z(d).wait_recv()

    each(nz, z_arrived, 1)
    acc = zslots[0]
    peak = zpeak[0]
    for k in range(1, nz):
        acc = acc + zslots[k]
        peak = jnp.maximum(peak, zpeak[k])
    total_ref[pl.ds(core, 1), band(here), :] = acc[None]
    xpeak[0] = peak

    def to_all(d):
        block = total_ref.at[core, band(here), :]
        return remote(block, block, send_all.at[d], recv_all.at[d], peer(d)[1])

    def peak_to_all(d):
        return remote(xpeak.at[0], xpeak.at[d], send_xm.at[d], recv_xm.at[d], peer(d)[1])

    def back(d):
        q = source_of(d)
        block = total_ref.at[core, band(q), :]
        return remote(block, block, send_back.at[d], recv_back.at[d], partner)

    def start_all(d):
        to_all(d).start()
        peak_to_all(d).start()

    def arrived(d):
        q = source_of(d)
        block = total_ref.at[core, band(q), :]
        remote(block, block, send_all.at[d], recv_all.at[d], partner).wait_recv()
        back(d).start()

    each(nxy, start_all, 1)
    back(jnp.int32(0)).start()

    lax.fori_loop(1, nxy, lambda d, carry: (arrived(d), carry)[1], 0)
    each(nxy, lambda d: peak_to_all(d).wait_recv(), 1)
    peak = xpeak[0]
    for d in range(1, nxy):
        peak = jnp.maximum(peak, xpeak[d])
    ppeak[0] = peak
    last = remote(ppeak.at[0], ppeak.at[1], send_pm, recv_pm, partner)
    last.start()
    last.wait()
    peak_ref[...] = jnp.maximum(ppeak[0], ppeak[1])

    def drain(d):
        pair(d).wait_send()
        back(d).wait()

    def drain_xy(d):
        spread(d).wait_send()
        to_all(d).wait_send()
        peak_to_all(d).wait_send()

    def drain_z(d):
        to_z(d).wait_send()
        peak_to_z(d).wait_send()

    each(nxy, drain)
    each(nxy, drain_xy, 1)
    each(nz, drain_z, 1)


def local(rows, cols, nyx, table, perm, object_in, probe_in, positions, intensity):
    n = probe_in.shape[-1]
    npos = positions.shape[2]
    f32 = jnp.float32
    obj = object_in.reshape(4, n, n)
    vmem = pl.BlockSpec(memory_space=pltpu.VMEM)
    smem = pl.BlockSpec(memory_space=pltpu.SMEM)
    dma = pltpu.SemaphoreType.DMA
    rim = jax.ShapeDtypeStruct((4, RIM, n), f32)
    side = jax.ShapeDtypeStruct((n + 2 * RIM, 128), f32)
    field = jax.ShapeDtypeStruct((4, n, n), f32)
    wave = jax.ShapeDtypeStruct((2, n, n), f32)
    top, bottom, left, right = pl.pallas_call(
        functools.partial(halo_kernel, rows, cols),
        out_shape=(rim, rim, side, side),
        in_specs=[vmem],
        out_specs=(vmem,) * 4,
        scratch_shapes=[VMEM((n, 128), f32), VMEM((n, 128), f32), dma((8,)), dma((8,))],
        compiler_params=pltpu.CompilerParams(collective_id=0, has_side_effects=True),
        name="halo",
    )(obj)
    core, gt, gb, gl, gr, gp = pl.pallas_call(
        tile_kernel,
        out_shape=(field, rim, rim, side, side, wave),
        in_specs=[smem] + [vmem] * 9,
        out_specs=(vmem,) * 6,
        scratch_shapes=[
            VMEM((4, 4, n + 2 * RIM, 128), f32),
            VMEM((npos, 4, n, n), f32),
            VMEM((npos, 2, n, n), f32),
            VMEM((npos, 4, 2, n + 128, 128), f32),
            VMEM((npos, 2, n, 128), f32),
        ],
        compiler_params=pltpu.CompilerParams(vmem_limit_bytes=48 * 2**20),
        name="tile",
    )(
        positions.reshape(-1), obj, top, bottom, left, right, probe_in, intensity.reshape(npos, n, n),
        jnp.asarray(table), jnp.asarray(perm),
    )
    nxy = nyx[0] * nyx[1]
    nz = rows * cols // (CORES * nxy)
    step = n // nxy
    total, descent, peak = pl.pallas_call(
        functools.partial(sum_kernel, rows, cols, nyx),
        out_shape=(wave, field, jax.ShapeDtypeStruct((8, 128), f32)),
        in_specs=[vmem] * 6,
        out_specs=(vmem,) * 3,
        scratch_shapes=[
            VMEM((n, n), f32), VMEM((n, n), f32), VMEM((nxy, step, n), f32), VMEM((nz, step, n), f32),
            VMEM((step, n), f32), VMEM((nz, 8, 128), f32), VMEM((nxy, 8, 128), f32), VMEM((2, 8, 128), f32),
            VMEM((4, RIM, n), f32), VMEM((4, RIM, n), f32), VMEM((n, 128), f32), VMEM((n, 128), f32),
            VMEM((4, RIM, 128), f32),
            dma((8,)), dma((8,)), dma((nxy,)), dma((nxy,)), dma((nxy,)), dma((nxy,)), dma((nz,)), dma((nz,)),
            dma((nz,)), dma((nz,)), dma((nxy,)), dma((nxy,)), dma((nxy,)), dma((nxy,)), dma((nxy,)), dma((nxy,)),
            dma, dma,
        ],
        compiler_params=pltpu.CompilerParams(collective_id=1, has_side_effects=True),
        name="sums",
    )(gp, core, gt, gb, gl, gr)
    tiles = rows * cols
    largest = jnp.max(peak)
    descent = descent.reshape(object_in.shape)
    object_out = object_in - 0.3 * descent / (jnp.sqrt(largest) + 1e-06)
    probe_out = probe_in - (2.0 / tiles) * total
    return object_out, probe_out


def solution(mesh):
    rows, cols = mesh.shape["row"], mesh.shape["col"]
    table, perm = weights(256)
    spec = (P(None, None, "row", "col"), P(), P("row", "col", None, None), P("row", "col", None, None, None))
    return jax.shard_map(
        functools.partial(local, rows, cols, NYX, table, perm),
        mesh=mesh,
        in_specs=spec,
        out_specs=(P(None, None, "row", "col"), P()),
        check_vma=False,
    )
```

```python
import functools
import math

import jax
import jax.numpy as jnp
import numpy as np
from jax import lax
from jax.experimental import pallas as pl
from jax.experimental.pallas import tpu as pltpu
from jax.sharding import PartitionSpec as P

RIM = 32
MESH = pl.DeviceIdType.MESH
VMEM = pltpu.VMEM
AROUND = ((-1, 0), (1, 0), (0, -1), (0, 1), (-1, -1), (-1, 1), (1, -1), (1, 1))
CORES = 2
NYX = (4, 4)
SUBS = 2


def split_of(matrix):
    high = matrix.astype(jnp.bfloat16)
    low = (matrix - high.astype(np.float64)).astype(jnp.bfloat16)
    return np.stack([np.asarray(high), np.asarray(low)])


def stacked(weight):
    real, imag = weight.real, weight.imag
    return np.block([[real, imag], [-imag, real]])


def weights(extent):
    half = extent // 2
    idx = np.arange(extent)
    freq = ((idx + half) % extent - half).astype(np.float64)
    turn = np.exp(-2j * np.pi * ((idx[:, None] * idx[None, :]) % extent) / extent)
    phase = np.exp(-8j * np.pi * freq**2 / extent**2)
    band = (np.conj(turn) * phase[None, :]) @ turn / extent
    left, right = band[:half, :half], band[:half, half:]
    even = turn[:half, 0::2] / math.sqrt(extent)
    odd = turn[:half, 1::2] / math.sqrt(extent)
    plus, minus = stacked((left + right) / 2), stacked((left - right) / 2)
    ev, od = stacked(even), stacked(odd)
    table = np.stack([split_of(m) for m in (plus, minus, ev, od, od.T)])
    order = np.concatenate([idx[0::2], idx[1::2]])
    perm = np.zeros((extent, extent), np.float32)
    perm[order, idx] = 1.0
    return table, perm.astype(jnp.bfloat16)


def parts(x):
    high = x.astype(jnp.bfloat16)
    return high, (x - high.astype(jnp.float32)).astype(jnp.bfloat16)


def dot(a, b):
    return jnp.dot(a, b, preferred_element_type=jnp.float32)


def times_right(x, w_ref, k):
    high, low = parts(x)
    wh, wl = w_ref[k, 0], w_ref[k, 1]
    return dot(jnp.concatenate([high, low, high], 1), jnp.concatenate([wh, wh, wl], 0))


def times_left(x, w_ref, k):
    high, low = parts(x)
    wh, wl = w_ref[k, 0], w_ref[k, 1]
    return dot(jnp.concatenate([wh, wh, wl], 1), jnp.concatenate([high, low, high], 0))


def fold(x):
    h = x.shape[0] // 2
    s, d = x[:h] + x[h:], x[:h] - x[h:]
    return [[s[:, :h] + s[:, h:], s[:, :h] - s[:, h:]], [d[:, :h] + d[:, h:], d[:, :h] - d[:, h:]]]


def unfold(b):
    top_s, top_d = b[0][0] + b[0][1], b[0][0] - b[0][1]
    bot_s, bot_d = b[1][0] + b[1][1], b[1][0] - b[1][1]
    s = jnp.concatenate([top_s, top_d], 1)
    d = jnp.concatenate([bot_s, bot_d], 1)
    return jnp.concatenate([s + d, s - d], 0)


def sandwich(re, im, w_ref, right, left):
    h = re[0][0].shape[0]
    out = [None, None]
    for j in (0, 1):
        k, swap = right[j]
        first, second = (im, re) if swap else (re, im)
        x = jnp.concatenate(
            [jnp.concatenate([first[i][j], second[i][j]], 1) for i in (0, 1)], 0
        )
        y = times_right(x, w_ref, k)
        a, b = y[:, :h], y[:, h:]
        out[j] = (b, a) if swap else (a, b)
    res_re, res_im = [None, None], [None, None]
    for i in (0, 1):
        k, swap = left[i]
        rows = slice(i * h, (i + 1) * h)
        r = jnp.concatenate([out[0][0][rows], out[1][0][rows]], 1)
        m = jnp.concatenate([out[0][1][rows], out[1][1][rows]], 1)
        y = times_left(jnp.concatenate([m, r] if swap else [r, m], 0), w_ref, k)
        a, b = y[:h], y[h:]
        r, m = (b, a) if swap else (a, b)
        res_re[i] = [r[:, :h], r[:, h:]]
        res_im[i] = [m[:, :h], m[:, h:]]
    return res_re, res_im


PROP = (((0, False), (1, False)), ((0, True), (1, True)))
PROP_CONJ = (((0, True), (1, True)), ((0, False), (1, False)))
FORWARD = (((2, False), (3, False)), ((2, True), (4, False)))
BACKWARD = (((2, True), (4, False)), ((2, False), (3, False)))


def rows_at(start, size):
    return pl.ds(pl.multiple_of(start, size), size)


def place_of():
    return lax.axis_index("row"), lax.axis_index("col")


def neighbours(rows, cols):
    r, c = place_of()
    out = []
    for dr, dc in AROUND:
        ok = None
        if dr:
            ok = r > 0 if dr < 0 else r < rows - 1
        if dc:
            side = c > 0 if dc < 0 else c < cols - 1
            ok = side if ok is None else jnp.logical_and(ok, side)
        out.append((ok, (r + dr, c + dc)))
    return out


def opposite(d):
    dr, dc = AROUND[d]
    return AROUND.index((-dr, -dc))


def remote(src, dst, ssem, rsem, where):
    return pltpu.make_async_remote_copy(
        src_ref=src, dst_ref=dst, send_sem=ssem, recv_sem=rsem, device_id=where, device_id_type=MESH
    )


def greet(around, extra):
    barrier = pltpu.get_barrier_semaphore()
    for ok, where in around:

        @pl.when(ok)
        def _(where=where):
            pl.semaphore_signal(barrier, inc=1, device_id=where, device_id_type=MESH)

    for where in extra:
        pl.semaphore_signal(barrier, inc=1, device_id=where, device_id_type=MESH)


def await_greetings(rows, cols, extra):
    r, c = place_of()
    tall = 1 + jnp.where(r > 0, 1, 0) + jnp.where(r < rows - 1, 1, 0)
    wide = 1 + jnp.where(c > 0, 1, 0) + jnp.where(c < cols - 1, 1, 0)
    pl.semaphore_wait(pltpu.get_barrier_semaphore(), tall * wide - 1 + len(extra))


def swap_rims(around, sources, targets, send_sem, recv_sem):
    for d, (ok, where) in enumerate(around):
        o = opposite(d)
        copy = remote(sources[d], targets[o], send_sem.at[d], recv_sem.at[o], where)
        pl.when(ok)(copy.start)
        target = targets[d]

        @pl.when(jnp.logical_not(ok))
        def _(target=target):
            target[...] = jnp.zeros(target.shape, target.dtype)


def finish_rims(around, sources, targets, send_sem, recv_sem):
    for d, (ok, where) in enumerate(around):
        pl.when(ok)(remote(sources[d], targets[d], send_sem.at[d], recv_sem.at[d], where).wait)


def both(ref, *at):
    return jnp.concatenate([ref[(*at, 0)], ref[(*at, 1)]], 1)


def pack_sides(first, last, quarter):
    left, right = first(0), pltpu.roll(last(0), 32, 1)
    for q in range(1, 4):
        left = jnp.where(quarter == q, pltpu.roll(first(q), 32 * q, 1), left)
        right = jnp.where(quarter == q, pltpu.roll(last(q), (32 * q + 32) % 128, 1), right)
    return left, right


def kernel(
    rows, cols, nyx,
    pos_ref, obj_ref, probe_in, meas_in, table_in, perm_in,
    obj_out, probe_out,
    probe_ref, meas_ref, w_ref, perm_ref,
    win, pl_buf, pr_buf, hl, hr,
    cut, mid, pad, seen,
    grad, gl, gr, gp_ref, fresh,
    theirs, ours, slots, mine, zslots, zpeak, xpeak, ppeak, total_ref,
    rt, rb, rl, rr, corners,
    load_sem, store_sem,
    send_halo, recv_halo, send_rim, recv_rim, send_pair, recv_pair, send_xy, recv_xy, send_z, recv_z,
    send_zm, recv_zm, send_xm, recv_xm, send_all, recv_all, send_back, recv_back, send_pm, recv_pm,
):
    n = probe_ref.shape[-1]
    h = n // 2
    npos = cut.shape[0]
    ny, nx = nyx
    nxy = ny * nx
    nzl = cols // nxy
    nz = nzl * (rows // CORES)
    step = n // nxy // SUBS
    r, c = place_of()
    core, zh = lax.rem(r, CORES), lax.div(r, CORES)
    zl, here = lax.div(c, nxy), lax.rem(c, nxy)
    y, x = lax.div(here, nx), lax.rem(here, nx)
    z = zh * nzl + zl
    partner = (zh * CORES + 1 - core, c)

    def peer(d):
        oy, ox = lax.div(d, nx), lax.rem(d, nx)
        q = lax.rem(y + oy, ny) * nx + lax.rem(x + ox, nx)
        return q, (r, zl * nxy + q)

    def source_of(d):
        oy, ox = lax.div(d, nx), lax.rem(d, nx)
        return lax.rem(y + ny - oy, ny) * nx + lax.rem(x + nx - ox, nx)

    def zpeer(d):
        k = lax.rem(z + d, nz)
        return lax.div(k, nzl) * CORES + core, lax.rem(k, nzl) * nxy + here

    def each(count, body, low=0):
        def go(i, carry):
            body(count - 1 - i)
            return carry

        lax.fori_loop(0, count - low, go, 0)

    around = neighbours(rows, cols)
    extra = [partner]
    extra += [peer(jnp.int32(d))[1] for d in range(1, nxy)]
    extra += [zpeer(jnp.int32(d)) for d in range(1, nz)]
    greet(around, extra)

    inner = pl.ds(RIM, n)
    loads = [
        (obj_ref.at[:, :, pl.ds(0, 128)], win.at[:, 1, inner, :]),
        (obj_ref.at[:, :, pl.ds(128, 128)], win.at[:, 2, inner, :]),
        (meas_in, meas_ref),
        (perm_in, perm_ref),
        (probe_in, probe_ref),
        (table_in, w_ref),
    ]
    loads = [pltpu.make_async_copy(a, b, load_sem.at[i]) for i, (a, b) in enumerate(loads)]
    for load in loads:
        load.start()
    loads[0].wait()
    loads[1].wait()
    quarter = lax.div(lax.broadcasted_iota(jnp.int32, (n, 128), 1), 32)
    pl_buf[...], pr_buf[...] = pack_sides(
        lambda q: win[q, 1, RIM : RIM + n, :], lambda q: win[q, 2, RIM : RIM + n, :], quarter
    )
    await_greetings(rows, cols, extra)

    ups, tops = pl.ds(0, RIM), pl.ds(RIM, RIM)
    lows, downs = pl.ds(n, RIM), pl.ds(n + RIM, RIM)
    lo, hi = pl.ds(0, RIM), pl.ds(n - RIM, RIM)
    halo = (
        around,
        [
            win.at[:, 1:3, tops, :], win.at[:, 1:3, lows, :], pl_buf, pr_buf,
            pl_buf.at[lo, :], pr_buf.at[lo, :], pl_buf.at[hi, :], pr_buf.at[hi, :],
        ],
        [
            win.at[:, 1:3, ups, :], win.at[:, 1:3, downs, :], hl.at[inner, :], hr.at[inner, :],
            hl.at[ups, :], hr.at[ups, :], hl.at[downs, :], hr.at[downs, :],
        ],
        send_halo,
        recv_halo,
    )
    swap_rims(*halo)

    zeros = jnp.zeros((64, 128), jnp.float32)
    for p in range(npos):
        for q in range(4):
            for t in (0, 1):
                pad[p, q, t, 0:64, :] = zeros
                pad[p, q, t, 64 + n :, :] = zeros
    loads[2].wait()
    loads[3].wait()
    for p in range(npos):
        for t in (0, 1):
            seen[p, t] = meas_ref[p, :, 128 * t : 128 * t + 128]
        meas = jnp.concatenate(
            [
                jnp.concatenate([seen[p, t, pl.ds(i, h, stride=2), :] for t in (0, 1)], 1)
                for i in (0, 1)
            ],
            0,
        )
        mh, ml = parts(meas)
        meas_ref[p] = dot(
            jnp.concatenate([mh, ml], 1), jnp.concatenate([perm_ref[...], perm_ref[...]], 0)
        )
    loads[4].wait()
    loads[5].wait()
    finish_rims(*halo)
    for q in range(4):
        win[q, 0] = pltpu.roll(hl[...], (96 - 32 * q) % 128, 1)
        win[q, 3] = pltpu.roll(hr[...], (128 - 32 * q) % 128, 1) if q else hr[...]

    offs = [(pos_ref[2 * p], pos_ref[2 * p + 1]) for p in range(npos)]
    lane = lax.broadcasted_iota(jnp.int32, (RIM, 128), 1)

    def cut_rows(i, carry):
        for p in range(npos):
            dy, dx = offs[p]
            shift = lax.rem(128 - dx, 128)
            high, low = lane >= 128 - dx, lane < -dx
            for q in range(4):
                at = pl.ds(RIM + dy + i * RIM, RIM)
                t0, t1, t2, t3 = [pltpu.roll(win[q, t, at, :], shift, 1) for t in range(4)]
                to = rows_at(i * RIM, RIM)
                cut[p, q, 0, to, :] = jnp.where(high, t2, jnp.where(low, t0, t1))
                cut[p, q, 1, to, :] = jnp.where(high, t3, jnp.where(low, t1, t2))
        return carry

    lax.fori_loop(0, n // RIM, cut_rows, 0)

    def keep(p, q, value):
        pad[p, q, 0, 64 : 64 + n, :] = value[:, :128]
        pad[p, q, 1, 64 : 64 + n, :] = value[:, 128:]

    for p in range(npos):
        pr, pi = probe_ref[0], probe_ref[1]
        ar, ai = both(cut, p, 0), both(cut, p, 1)
        re, im = sandwich(fold(pr * ar - pi * ai), fold(pr * ai + pi * ar), w_ref, *PROP)
        qr, qi = unfold(re), unfold(im)
        mid[p, 0], mid[p, 1] = qr, qi
        br, bi = both(cut, p, 2), both(cut, p, 3)
        re, im = sandwich(fold(qr * br - qi * bi), fold(qr * bi + qi * br), w_ref, *FORWARD)
        for i in (0, 1):
            for j in (0, 1):
                fr, fi = re[i][j], im[i][j]
                seen_at = meas_ref[p, i * h : (i + 1) * h, j * h : (j + 1) * h]
                ex = 2.0 * (fr * fr + fi * fi - seen_at)
                re[i][j], im[i][j] = ex * fr, ex * fi
        re, im = sandwich(re, im, w_ref, *BACKWARD)
        hr_, hi_ = unfold(re), unfold(im)
        qr, qi = mid[p, 0], mid[p, 1]
        keep(p, 2, qr * hr_ + qi * hi_)
        keep(p, 3, qr * hi_ - qi * hr_)
        br, bi = both(cut, p, 2), both(cut, p, 3)
        re, im = sandwich(fold(br * hr_ + bi * hi_), fold(br * hi_ - bi * hr_), w_ref, *PROP_CONJ)
        er, ei = unfold(re), unfold(im)
        pr, pi = probe_ref[0], probe_ref[1]
        keep(p, 0, pr * er + pi * ei)
        keep(p, 1, pr * ei - pi * er)
        ar, ai = both(cut, p, 0), both(cut, p, 1)
        if p == 0:
            gp_ref[0] = ar * er + ai * ei
            gp_ref[1] = ar * ei - ai * er
        else:
            gp_ref[0] += ar * er + ai * ei
            gp_ref[1] += ar * ei - ai * er

    def band(q, s):
        return rows_at((q * SUBS + s) * step, step)

    def pair(s, d):
        at = band(peer(d)[0], s)
        return remote(
            gp_ref.at[1 - core, at, :], theirs.at[at, :], send_pair.at[s, d], recv_pair.at[s, d], partner
        )

    def spread(s, d):
        q, where = peer(d)
        return remote(
            ours.at[band(q, s), :], slots.at[s, d], send_xy.at[s, d], recv_xy.at[s, d], where
        )

    for s in range(SUBS):
        each(nxy, lambda d, s=s: pair(s, d).start())

    quarter = lax.div(lane, 32)

    def place(i):
        to = rows_at(i * RIM, RIM)
        ends = []
        for q in range(4):
            sums = None
            for p in range(npos):
                dy, dx = offs[p]
                shift = lax.rem(128 + dx, 128)
                low, high = lane < dx, lane >= 128 + dx
                at = pl.ds(RIM - dy + i * RIM, RIM)
                a, b = (pltpu.roll(pad[p, q, t, at, :], shift, 1) for t in (0, 1))
                o = jnp.zeros_like(a)
                got = [
                    jnp.where(high, a, o),
                    jnp.where(low, o, jnp.where(high, b, a)),
                    jnp.where(low, a, jnp.where(high, o, b)),
                    jnp.where(low, b, o),
                ]
                sums = got if sums is None else [u + v for u, v in zip(sums, got)]
            grad[q, 0, to, :] = sums[1]
            grad[q, 1, to, :] = sums[2]
            ends.append((sums[0], sums[3]))
        gr[to, :], gl[to, :] = pack_sides(lambda q: ends[q][1], lambda q: ends[q][0], quarter)

    def pass_on(s, d):
        at = band(peer(d)[0], s)
        pair(s, d).wait_recv()
        ours[at, :] = gp_ref[core, at, :] + theirs[at, :]

    def pass_and_send(s, d):
        pass_on(s, d)
        spread(s, d).start()

    for s in range(SUBS):
        each(nxy, lambda d, s=s: pass_and_send(s, d), 1)
        pass_on(s, jnp.int32(0))

    each(n // RIM + 2, place)
    rims = (
        around,
        [
            grad.at[:, :, ups, :], grad.at[:, :, downs, :], gl.at[inner, :], gr.at[inner, :],
            gl.at[ups, :], gr.at[ups, :], gl.at[downs, :], gr.at[downs, :],
        ],
        [rt, rb, rl, rr, corners.at[0], corners.at[1], corners.at[2], corners.at[3]],
        send_rim,
        recv_rim,
    )
    swap_rims(*rims)

    def to_z(s, d):
        return remote(mine.at[s], zslots.at[s, z], send_z.at[s, d], recv_z.at[s, d], zpeer(d))

    def peak_to_z(d):
        return remote(zpeak.at[z], zpeak.at[z], send_zm.at[d], recv_zm.at[d], zpeer(d))

    for s in range(SUBS):
        each(nxy, lambda d, s=s: spread(s, d).wait_recv(), 1)
        acc = ours[band(here, s), :]
        for d in range(1, nxy):
            acc = acc + slots[s, d]
        mine[s] = acc
        zslots[s, pl.ds(z, 1)] = acc[None]
        each(nz, lambda d, s=s: to_z(s, d).start(), 1)

    finish_rims(*rims)
    first, final = lane < 32, lane >= 96

    def rows_of(i, up, low):
        at, to = rows_at(i * RIM, RIM), rows_at(i * RIM + RIM, RIM)
        zero = jnp.zeros((RIM, 128), jnp.float32)
        lft, rgt = rl[at, :], rr[at, :]
        if up is not None:
            lft, rgt = lft + corners[up], rgt + corners[up + 1]
        best = None
        for l in (0, 1):
            square = [None, None]
            for q in (2 * l, 2 * l + 1):
                ends = (
                    jnp.where(first, pltpu.roll(lft, (128 - 32 * q) % 128, 1) if q else lft, zero),
                    jnp.where(final, pltpu.roll(rgt, 96 - 32 * q, 1) if q < 3 else rgt, zero),
                )
                for t in (0, 1):
                    v = grad[q, t, to, :] + ends[t]
                    if low is not None:
                        v = v + low[q, t]
                    grad[q, t, to, :] = v
                    square[t] = v * v if square[t] is None else square[t] + v * v
            for v in square:
                best = v if best is None else jnp.maximum(best, v)
        return functools.reduce(jnp.maximum, [best[8 * k : 8 * k + 8] for k in range(RIM // 8)])

    blocks = n // RIM
    peak = jnp.maximum(rows_of(0, 0, rt), rows_of(blocks - 1, 2, rb))
    peak = lax.fori_loop(1, blocks - 1, lambda i, m: jnp.maximum(m, rows_of(i, None, None)), peak)
    zpeak[pl.ds(z, 1)] = peak[None]
    each(nz, lambda d: peak_to_z(d).start(), 1)

    def to_all(s, d):
        block = total_ref.at[core, band(here, s), :]
        return remote(block, block, send_all.at[s, d], recv_all.at[s, d], peer(d)[1])

    def peak_to_all(d):
        return remote(xpeak.at[0], xpeak.at[d], send_xm.at[d], recv_xm.at[d], peer(d)[1])

    def back(s, d):
        block = total_ref.at[core, band(source_of(d), s), :]
        return remote(block, block, send_back.at[s, d], recv_back.at[s, d], partner)

    for s in range(SUBS):
        each(nz, lambda d, s=s: to_z(s, d).wait_recv(), 1)
        acc = zslots[s, 0]
        for k in range(1, nz):
            acc = acc + zslots[s, k]
        total_ref[pl.ds(core, 1), band(here, s), :] = acc[None]
        each(nxy, lambda d, s=s: to_all(s, d).start(), 1)
        back(s, jnp.int32(0)).start()

    each(nz, lambda d: peak_to_z(d).wait_recv(), 1)
    peak = zpeak[0]
    for k in range(1, nz):
        peak = jnp.maximum(peak, zpeak[k])
    xpeak[0] = peak
    each(nxy, lambda d: peak_to_all(d).start(), 1)

    def arrived(s, d):
        block = total_ref.at[core, band(source_of(d), s), :]
        remote(block, block, send_all.at[s, d], recv_all.at[s, d], partner).wait_recv()
        back(s, d).start()

    def forward(s):
        lax.fori_loop(1, nxy, lambda d, carry: (arrived(s, d), carry)[1], 0)

    for s in range(SUBS - 1):
        forward(s)
    each(nxy, lambda d: peak_to_all(d).wait_recv(), 1)
    peak = xpeak[0]
    for d in range(1, nxy):
        peak = jnp.maximum(peak, xpeak[d])
    ppeak[0] = peak
    last = remote(ppeak.at[0], ppeak.at[1], send_pm, recv_pm, partner)
    last.start()
    forward(SUBS - 1)
    last.wait()

    largest = jnp.max(jnp.maximum(ppeak[0], ppeak[1]), axis=(0, 1), keepdims=True)
    scale = jnp.broadcast_to(0.3 / (jnp.sqrt(largest) + 1e-06), (RIM, 128))

    def next_rows(i, carry):
        at = rows_at(i * RIM + RIM, RIM)
        for q in range(4):
            for t in (0, 1):
                grad[q, t, at, :] = win[q, t + 1, at, :] - scale * grad[q, t, at, :]
        return carry

    lax.fori_loop(0, blocks, next_rows, 0)
    stores = [
        pltpu.make_async_copy(grad.at[:, t, inner, :], obj_out.at[:, :, pl.ds(128 * t, 128)], store_sem.at[t])
        for t in (0, 1)
    ]
    for store in stores:
        store.start()

    def drain(s, d):
        pair(s, d).wait_send()
        back(s, d).wait()

    def drain_xy(s, d):
        spread(s, d).wait_send()
        to_all(s, d).wait_send()

    for s in range(SUBS):
        each(nxy, lambda d, s=s: drain(s, d))
    fresh[...] = probe_ref[...] - (2.0 / (rows * cols)) * total_ref[...]
    stores.append(pltpu.make_async_copy(fresh, probe_out, store_sem.at[2]))
    stores[2].start()
    for s in range(SUBS):
        each(nxy, lambda d, s=s: drain_xy(s, d), 1)
        each(nz, lambda d, s=s: to_z(s, d).wait_send(), 1)
    each(nxy, lambda d: peak_to_all(d).wait_send(), 1)
    each(nz, lambda d: peak_to_z(d).wait_send(), 1)
    for store in stores:
        store.wait()


def local(rows, cols, nyx, table, perm, object_in, probe_in, positions, intensity):
    n = probe_in.shape[-1]
    npos = positions.shape[2]
    f32 = jnp.float32
    hbm = pl.BlockSpec(memory_space=pltpu.HBM)
    smem = pl.BlockSpec(memory_space=pltpu.SMEM)
    dma = pltpu.SemaphoreType.DMA
    nxy = nyx[0] * nyx[1]
    nz = rows * cols // (CORES * nxy)
    step = n // nxy // SUBS
    wide = n + 2 * RIM
    buffers = [
        (2, n, n), (npos, n, n), table.shape, perm.shape,
        (4, 4, wide, 128), (n, 128), (n, 128), (wide, 128), (wide, 128),
        (npos, 4, 2, n, 128), (npos, 2, n, n), (npos, 4, 2, n + 128, 128), (npos, 2, n, 128),
        (4, 2, wide, 128), (wide, 128), (wide, 128), (2, n, n), (2, n, n),
        (n, n), (n, n), (SUBS, nxy, step, n), (SUBS, step, n), (SUBS, nz, step, n),
        (nz, 8, 128), (nxy, 8, 128), (2, 8, 128), (2, n, n),
        (4, 2, RIM, 128), (4, 2, RIM, 128), (n, 128), (n, 128), (4, RIM, 128),
    ]
    scratch = [VMEM(shape, jnp.bfloat16 if i in (2, 3) else f32) for i, shape in enumerate(buffers)]
    scratch += [dma((6,)), dma((3,)), dma((8,)), dma((8,)), dma((8,)), dma((8,))]
    scratch += [dma((SUBS, nxy))] * 4 + [dma((SUBS, nz))] * 2 + [dma((nz,))] * 2 + [dma((nxy,))] * 2
    scratch += [dma((SUBS, nxy))] * 4 + [dma, dma]
    object_out, probe_out = pl.pallas_call(
        functools.partial(kernel, rows, cols, nyx),
        out_shape=(jax.ShapeDtypeStruct((4, n, n), f32), jax.ShapeDtypeStruct((2, n, n), f32)),
        in_specs=[smem] + [hbm] * 5,
        out_specs=(hbm, hbm),
        scratch_shapes=scratch,
        compiler_params=pltpu.CompilerParams(
            collective_id=0, has_side_effects=True, vmem_limit_bytes=48 * 2**20
        ),
        name="step",
    )(
        positions.reshape(-1), object_in.reshape(4, n, n), probe_in, intensity.reshape(npos, n, n),
        jnp.asarray(table), jnp.asarray(perm),
    )
    return object_out.reshape(object_in.shape), probe_out


def solution(mesh):
    rows, cols = mesh.shape["row"], mesh.shape["col"]
    table, perm = weights(256)
    spec = (P(None, None, "row", "col"), P(), P("row", "col", None, None), P("row", "col", None, None, None))
    return jax.shard_map(
        functools.partial(local, rows, cols, NYX, table, perm),
        mesh=mesh,
        in_specs=spec,
        out_specs=(P(None, None, "row", "col"), P()),
        check_vma=False,
    )
```

```python
import functools
import math

import jax
import jax.numpy as jnp
import numpy as np
from jax import lax
from jax.experimental import pallas as pl
from jax.experimental.pallas import tpu as pltpu
from jax.sharding import PartitionSpec as P

RIM = 32
MESH = pl.DeviceIdType.MESH
VMEM = pltpu.VMEM
AROUND = ((-1, 0), (1, 0), (0, -1), (0, 1), (-1, -1), (-1, 1), (1, -1), (1, 1))
CORES = 2
NYX = (4, 4)


def split_of(matrix):
    high = matrix.astype(jnp.bfloat16)
    low = (matrix - high.astype(np.float64)).astype(jnp.bfloat16)
    return np.stack([np.asarray(high), np.asarray(low)])


def stacked(weight):
    real, imag = weight.real, weight.imag
    return np.block([[real, imag], [-imag, real]])


def weights(extent):
    half = extent // 2
    idx = np.arange(extent)
    freq = ((idx + half) % extent - half).astype(np.float64)
    turn = np.exp(-2j * np.pi * ((idx[:, None] * idx[None, :]) % extent) / extent)
    phase = np.exp(-8j * np.pi * freq**2 / extent**2)
    band = (np.conj(turn) * phase[None, :]) @ turn / extent
    left, right = band[:half, :half], band[:half, half:]
    even = turn[:half, 0::2] / math.sqrt(extent)
    odd = turn[:half, 1::2] / math.sqrt(extent)
    plus, minus = stacked((left + right) / 2), stacked((left - right) / 2)
    ev, od = stacked(even), stacked(odd)
    table = np.stack([split_of(m) for m in (plus, minus, ev, od, od.T)])
    order = np.concatenate([idx[0::2], idx[1::2]])
    perm = np.zeros((extent, extent), np.float32)
    perm[order, idx] = 1.0
    return table, perm.astype(jnp.bfloat16)


def parts(x):
    high = x.astype(jnp.bfloat16)
    return high, (x - high.astype(jnp.float32)).astype(jnp.bfloat16)


def dot(a, b):
    return jnp.dot(a, b, preferred_element_type=jnp.float32)


def times_right(x, w_ref, k):
    high, low = parts(x)
    wh, wl = w_ref[k, 0], w_ref[k, 1]
    return dot(jnp.concatenate([high, low, high], 1), jnp.concatenate([wh, wh, wl], 0))


def times_left(x, w_ref, k):
    high, low = parts(x)
    wh, wl = w_ref[k, 0], w_ref[k, 1]
    return dot(jnp.concatenate([wh, wh, wl], 1), jnp.concatenate([high, low, high], 0))


def fold(x):
    h = x.shape[0] // 2
    s, d = x[:h] + x[h:], x[:h] - x[h:]
    return [[s[:, :h] + s[:, h:], s[:, :h] - s[:, h:]], [d[:, :h] + d[:, h:], d[:, :h] - d[:, h:]]]


def unfold(b):
    top_s, top_d = b[0][0] + b[0][1], b[0][0] - b[0][1]
    bot_s, bot_d = b[1][0] + b[1][1], b[1][0] - b[1][1]
    s = jnp.concatenate([top_s, top_d], 1)
    d = jnp.concatenate([bot_s, bot_d], 1)
    return jnp.concatenate([s + d, s - d], 0)


def sandwich(re, im, w_ref, right, left):
    h = re[0][0].shape[0]
    out = [None, None]
    for j in (0, 1):
        k, swap = right[j]
        first, second = (im, re) if swap else (re, im)
        x = jnp.concatenate(
            [jnp.concatenate([first[i][j], second[i][j]], 1) for i in (0, 1)], 0
        )
        y = times_right(x, w_ref, k)
        a, b = y[:, :h], y[:, h:]
        out[j] = (b, a) if swap else (a, b)
    res_re, res_im = [None, None], [None, None]
    for i in (0, 1):
        k, swap = left[i]
        rows = slice(i * h, (i + 1) * h)
        r = jnp.concatenate([out[0][0][rows], out[1][0][rows]], 1)
        m = jnp.concatenate([out[0][1][rows], out[1][1][rows]], 1)
        y = times_left(jnp.concatenate([m, r] if swap else [r, m], 0), w_ref, k)
        a, b = y[:h], y[h:]
        r, m = (b, a) if swap else (a, b)
        res_re[i] = [r[:, :h], r[:, h:]]
        res_im[i] = [m[:, :h], m[:, h:]]
    return res_re, res_im


PROP = (((0, False), (1, False)), ((0, True), (1, True)))
PROP_CONJ = (((0, True), (1, True)), ((0, False), (1, False)))
FORWARD = (((2, False), (3, False)), ((2, True), (4, False)))
BACKWARD = (((2, True), (4, False)), ((2, False), (3, False)))


def rows_at(start, size):
    return pl.ds(pl.multiple_of(start, size), size)


def place_of():
    return lax.axis_index("row"), lax.axis_index("col")


def neighbours(rows, cols):
    r, c = place_of()
    out = []
    for dr, dc in AROUND:
        ok = None
        if dr:
            ok = r > 0 if dr < 0 else r < rows - 1
        if dc:
            side = c > 0 if dc < 0 else c < cols - 1
            ok = side if ok is None else jnp.logical_and(ok, side)
        out.append((ok, (r + dr, c + dc)))
    return out


def opposite(d):
    dr, dc = AROUND[d]
    return AROUND.index((-dr, -dc))


def remote(src, dst, ssem, rsem, where):
    return pltpu.make_async_remote_copy(
        src_ref=src, dst_ref=dst, send_sem=ssem, recv_sem=rsem, device_id=where, device_id_type=MESH
    )


def greet(around, extra):
    barrier = pltpu.get_barrier_semaphore()
    for ok, where in around:

        @pl.when(ok)
        def _(where=where):
            pl.semaphore_signal(barrier, inc=1, device_id=where, device_id_type=MESH)

    for where in extra:
        pl.semaphore_signal(barrier, inc=1, device_id=where, device_id_type=MESH)


def await_greetings(rows, cols, extra):
    r, c = place_of()
    tall = 1 + jnp.where(r > 0, 1, 0) + jnp.where(r < rows - 1, 1, 0)
    wide = 1 + jnp.where(c > 0, 1, 0) + jnp.where(c < cols - 1, 1, 0)
    pl.semaphore_wait(pltpu.get_barrier_semaphore(), tall * wide - 1 + len(extra))


def swap_rims(around, sources, targets, send_sem, recv_sem):
    for d, (ok, where) in enumerate(around):
        o = opposite(d)
        copy = remote(sources[d], targets[o], send_sem.at[d], recv_sem.at[o], where)
        pl.when(ok)(copy.start)
        target = targets[d]

        @pl.when(jnp.logical_not(ok))
        def _(target=target):
            target[...] = jnp.zeros(target.shape, target.dtype)


def finish_rims(around, sources, targets, send_sem, recv_sem):
    for d, (ok, where) in enumerate(around):
        pl.when(ok)(remote(sources[d], targets[d], send_sem.at[d], recv_sem.at[d], where).wait)


def both(ref, *at):
    return jnp.concatenate([ref[(*at, 0)], ref[(*at, 1)]], 1)


def pack_sides(first, last, quarter):
    left, right = first(0), pltpu.roll(last(0), 32, 1)
    for q in range(1, 4):
        left = jnp.where(quarter == q, pltpu.roll(first(q), 32 * q, 1), left)
        right = jnp.where(quarter == q, pltpu.roll(last(q), (32 * q + 32) % 128, 1), right)
    return left, right


def kernel(
    rows, cols, nyx,
    pos_in, obj_ref, probe_in, meas_in, table_in, perm_in,
    obj_out, probe_out,
    pos_ref, probe_ref, meas_ref, w_ref, perm_ref,
    win, pl_buf, pr_buf, hl, hr,
    cut, mid, pad, seen,
    grad, gl, gr, gp_ref,
    theirs, ours, slots, mine, zslots, zpeak, xpeak, ppeak, total_ref,
    rt, rb, rl, rr, corners,
    load_sem,
    send_halo, recv_halo, send_rim, recv_rim, send_pair, recv_pair, send_xy, recv_xy, send_z, recv_z,
    send_zm, recv_zm, send_xm, recv_xm, send_all, recv_all, send_back, recv_back, send_pm, recv_pm,
):
    n = probe_ref.shape[-1]
    h = n // 2
    npos = cut.shape[0]
    ny, nx = nyx
    nxy = ny * nx
    nzl = cols // nxy
    nz = nzl * (rows // CORES)
    step = n // nxy
    r, c = place_of()
    core, zh = lax.rem(r, CORES), lax.div(r, CORES)
    zl, here = lax.div(c, nxy), lax.rem(c, nxy)
    y, x = lax.div(here, nx), lax.rem(here, nx)
    z = zh * nzl + zl
    partner = (zh * CORES + 1 - core, c)

    def peer(d):
        q = lax.rem(y + d // nx, ny) * nx + lax.rem(x + d % nx, nx)
        return q, (r, zl * nxy + q)

    def zpeer(d):
        k = lax.rem(z + d, nz)
        return lax.div(k, nzl) * CORES + core, lax.rem(k, nzl) * nxy + here

    far = sorted(range(1, nz), key=lambda d: -min(d, nz - d))

    around = neighbours(rows, cols)
    extra = [partner]
    extra += [peer(d)[1] for d in range(1, nxy)]
    extra += [zpeer(d) for d in range(1, nz)]
    greet(around, extra)

    inner = pl.ds(RIM, n)
    loads = [
        (obj_ref.at[:, :, pl.ds(0, 128)], win.at[:, 1, inner, :]),
        (obj_ref.at[:, :, pl.ds(128, 128)], win.at[:, 2, inner, :]),
        (meas_in, meas_ref),
        (perm_in, perm_ref),
        (probe_in, probe_ref),
        (table_in, w_ref),
        (pos_in, pos_ref),
    ]
    loads = [pltpu.make_async_copy(a, b, load_sem.at[i]) for i, (a, b) in enumerate(loads)]
    for load in loads:
        load.start()
    loads[0].wait()
    loads[1].wait()
    quarter = lax.div(lax.broadcasted_iota(jnp.int32, (n, 128), 1), 32)
    pl_buf[...], pr_buf[...] = pack_sides(
        lambda q: win[q, 1, RIM : RIM + n, :], lambda q: win[q, 2, RIM : RIM + n, :], quarter
    )
    await_greetings(rows, cols, extra)

    ups, tops = pl.ds(0, RIM), pl.ds(RIM, RIM)
    lows, downs = pl.ds(n, RIM), pl.ds(n + RIM, RIM)
    lo, hi = pl.ds(0, RIM), pl.ds(n - RIM, RIM)
    halo = (
        around,
        [
            win.at[:, 1:3, tops, :], win.at[:, 1:3, lows, :], pl_buf, pr_buf,
            pl_buf.at[lo, :], pr_buf.at[lo, :], pl_buf.at[hi, :], pr_buf.at[hi, :],
        ],
        [
            win.at[:, 1:3, ups, :], win.at[:, 1:3, downs, :], hl.at[inner, :], hr.at[inner, :],
            hl.at[ups, :], hr.at[ups, :], hl.at[downs, :], hr.at[downs, :],
        ],
        send_halo,
        recv_halo,
    )
    swap_rims(*halo)

    zeros = jnp.zeros((64, 128), jnp.float32)
    for p in range(npos):
        for q in range(4):
            for t in (0, 1):
                pad[p, q, t, 0:64, :] = zeros
                pad[p, q, t, 64 + n :, :] = zeros
    loads[2].wait()
    loads[3].wait()
    for p in range(npos):
        for t in (0, 1):
            seen[p, t] = meas_ref[p, :, 128 * t : 128 * t + 128]
        meas = jnp.concatenate(
            [
                jnp.concatenate([seen[p, t, pl.ds(i, h, stride=2), :] for t in (0, 1)], 1)
                for i in (0, 1)
            ],
            0,
        )
        mh, ml = parts(meas)
        meas_ref[p] = dot(
            jnp.concatenate([mh, ml], 1), jnp.concatenate([perm_ref[...], perm_ref[...]], 0)
        )
    loads[4].wait()
    loads[5].wait()
    loads[6].wait()
    finish_rims(*halo)
    for q in range(4):
        win[q, 0] = pltpu.roll(hl[...], (96 - 32 * q) % 128, 1)
        win[q, 3] = pltpu.roll(hr[...], (128 - 32 * q) % 128, 1) if q else hr[...]

    offs = [(pos_ref[0, 0, p, 0], pos_ref[0, 0, p, 1]) for p in range(npos)]
    lane = lax.broadcasted_iota(jnp.int32, (RIM, 128), 1)

    def cut_rows(i, carry):
        for p in range(npos):
            dy, dx = offs[p]
            shift = lax.rem(128 - dx, 128)
            high, low = lane >= 128 - dx, lane < -dx
            for q in range(4):
                at = pl.ds(RIM + dy + i * RIM, RIM)
                t0, t1, t2, t3 = [pltpu.roll(win[q, t, at, :], shift, 1) for t in range(4)]
                to = rows_at(i * RIM, RIM)
                cut[p, q, 0, to, :] = jnp.where(high, t2, jnp.where(low, t0, t1))
                cut[p, q, 1, to, :] = jnp.where(high, t3, jnp.where(low, t1, t2))
        return carry

    lax.fori_loop(0, n // RIM, cut_rows, 0)

    def keep(p, q, value):
        pad[p, q, 0, 64 : 64 + n, :] = value[:, :128]
        pad[p, q, 1, 64 : 64 + n, :] = value[:, 128:]

    for p in range(npos):
        pr, pi = probe_ref[0], probe_ref[1]
        ar, ai = both(cut, p, 0), both(cut, p, 1)
        re, im = sandwich(fold(pr * ar - pi * ai), fold(pr * ai + pi * ar), w_ref, *PROP)
        qr, qi = unfold(re), unfold(im)
        mid[p, 0], mid[p, 1] = qr, qi
        br, bi = both(cut, p, 2), both(cut, p, 3)
        re, im = sandwich(fold(qr * br - qi * bi), fold(qr * bi + qi * br), w_ref, *FORWARD)
        for i in (0, 1):
            for j in (0, 1):
                fr, fi = re[i][j], im[i][j]
                seen_at = meas_ref[p, i * h : (i + 1) * h, j * h : (j + 1) * h]
                ex = 2.0 * (fr * fr + fi * fi - seen_at)
                re[i][j], im[i][j] = ex * fr, ex * fi
        re, im = sandwich(re, im, w_ref, *BACKWARD)
        hr_, hi_ = unfold(re), unfold(im)
        qr, qi = mid[p, 0], mid[p, 1]
        keep(p, 2, qr * hr_ + qi * hi_)
        keep(p, 3, qr * hi_ - qi * hr_)
        br, bi = both(cut, p, 2), both(cut, p, 3)
        re, im = sandwich(fold(br * hr_ + bi * hi_), fold(br * hi_ - bi * hr_), w_ref, *PROP_CONJ)
        er, ei = unfold(re), unfold(im)
        pr, pi = probe_ref[0], probe_ref[1]
        keep(p, 0, pr * er + pi * ei)
        keep(p, 1, pr * ei - pi * er)
        ar, ai = both(cut, p, 0), both(cut, p, 1)
        if p == 0:
            gp_ref[0] = ar * er + ai * ei
            gp_ref[1] = ar * ei - ai * er
        else:
            gp_ref[0] += ar * er + ai * ei
            gp_ref[1] += ar * ei - ai * er

    def band(q):
        return rows_at(q * step, step)

    def stripe(row):
        return rows_at(row * step * nx, step * nx)

    def pair(oy):
        at = stripe(lax.rem(y + oy, ny))
        return at, remote(gp_ref.at[1 - core, at, :], theirs.at[at, :], send_pair, recv_pair.at[oy], partner)

    for oy in reversed(range(ny)):
        pair(oy)[1].start()

    quarter = lax.div(lane, 32)

    def place(i):
        to = rows_at(i * RIM, RIM)
        ends = []
        for q in range(4):
            sums = None
            for p in range(npos):
                dy, dx = offs[p]
                shift = lax.rem(128 + dx, 128)
                low, high = lane < dx, lane >= 128 + dx
                at = pl.ds(RIM - dy + i * RIM, RIM)
                a, b = (pltpu.roll(pad[p, q, t, at, :], shift, 1) for t in (0, 1))
                o = jnp.zeros_like(a)
                got = [
                    jnp.where(high, a, o),
                    jnp.where(low, o, jnp.where(high, b, a)),
                    jnp.where(low, a, jnp.where(high, o, b)),
                    jnp.where(low, b, o),
                ]
                sums = got if sums is None else [u + v for u, v in zip(sums, got)]
            grad[q, 0, to, :] = sums[1]
            grad[q, 1, to, :] = sums[2]
            ends.append((sums[0], sums[3]))
        gr[to, :], gl[to, :] = pack_sides(lambda q: ends[q][1], lambda q: ends[q][0], quarter)

    for oy in reversed(range(ny)):
        at, copy = pair(oy)
        copy.wait_recv()
        ours[at, :] = gp_ref[core, at, :] + theirs[at, :]
        for ox in reversed(range(nx)):
            d = oy * nx + ox
            if d:
                q, where = peer(d)
                remote(ours.at[band(q), :], slots.at[d], send_xy, recv_xy, where).start()

    lax.fori_loop(0, n // RIM + 2, lambda i, carry: (place(i), carry)[1], 0)
    rims = (
        around,
        [
            grad.at[:, :, ups, :], grad.at[:, :, downs, :], gl.at[inner, :], gr.at[inner, :],
            gl.at[ups, :], gr.at[ups, :], gl.at[downs, :], gr.at[downs, :],
        ],
        [rt, rb, rl, rr, corners.at[0], corners.at[1], corners.at[2], corners.at[3]],
        send_rim,
        recv_rim,
    )
    swap_rims(*rims)

    def landed(ref, sem):
        remote(ref, ref, sem, sem, partner).wait_recv()

    def left(ref, sem):
        remote(ref, ref, sem, sem, partner).wait_send()

    landed(slots.at[pl.ds(1, nxy - 1)], recv_xy)
    acc = ours[band(here), :]
    for d in range(1, nxy):
        acc = acc + slots[d]
    mine[...] = acc
    zslots[pl.ds(z, 1)] = acc[None]
    for d in far:
        remote(mine, zslots.at[z], send_z, recv_z, zpeer(d)).start()

    finish_rims(*rims)
    first, final = lane < 32, lane >= 96

    def rows_of(i, up, low):
        at, to = rows_at(i * RIM, RIM), rows_at(i * RIM + RIM, RIM)
        zero = jnp.zeros((RIM, 128), jnp.float32)
        lft, rgt = rl[at, :], rr[at, :]
        if up is not None:
            lft, rgt = lft + corners[up], rgt + corners[up + 1]
        best = None
        for l in (0, 1):
            square = [None, None]
            for q in (2 * l, 2 * l + 1):
                ends = (
                    jnp.where(first, pltpu.roll(lft, (128 - 32 * q) % 128, 1) if q else lft, zero),
                    jnp.where(final, pltpu.roll(rgt, 96 - 32 * q, 1) if q < 3 else rgt, zero),
                )
                for t in (0, 1):
                    v = grad[q, t, to, :] + ends[t]
                    if low is not None:
                        v = v + low[q, t]
                    grad[q, t, to, :] = v
                    square[t] = v * v if square[t] is None else square[t] + v * v
            for v in square:
                best = v if best is None else jnp.maximum(best, v)
        return functools.reduce(jnp.maximum, [best[8 * k : 8 * k + 8] for k in range(RIM // 8)])

    blocks = n // RIM
    peak = jnp.maximum(rows_of(0, 0, rt), rows_of(blocks - 1, 2, rb))
    peak = lax.fori_loop(1, blocks - 1, lambda i, m: jnp.maximum(m, rows_of(i, None, None)), peak)
    zpeak[pl.ds(z, 1)] = peak[None]
    for d in far:
        remote(zpeak.at[z], zpeak.at[z], send_zm, recv_zm, zpeer(d)).start()

    landed(zslots.at[pl.ds(0, nz - 1)], recv_z)
    acc = zslots[0]
    for k in range(1, nz):
        acc = acc + zslots[k]
    total_ref[pl.ds(core, 1), band(here), :] = acc[None]
    block = total_ref.at[core, band(here), :]
    for d in reversed(range(1, nxy)):
        remote(block, block, send_all, recv_all.at[d // nx], peer(d)[1]).start()

    landed(zpeak.at[pl.ds(0, nz - 1)], recv_zm)
    peak = zpeak[0]
    for k in range(1, nz):
        peak = jnp.maximum(peak, zpeak[k])
    xpeak[0] = peak
    for d in reversed(range(1, nxy)):
        remote(xpeak.at[0], xpeak.at[d], send_xm, recv_xm, peer(d)[1]).start()

    def forward(oy):
        at = stripe(lax.rem(y + ny - oy, ny))
        block = total_ref.at[core, at, :]
        count = nx - 1 if oy == 0 else nx
        landed(total_ref.at[core, pl.ds(0, count * step), :], recv_all.at[oy])
        remote(block, block, send_back, recv_back, partner).start()

    forward(0)
    landed(xpeak.at[pl.ds(1, nxy - 1)], recv_xm)
    peak = xpeak[0]
    for d in range(1, nxy):
        peak = jnp.maximum(peak, xpeak[d])
    ppeak[0] = peak
    last = remote(ppeak.at[0], ppeak.at[1], send_pm, recv_pm, partner)
    last.start()
    for oy in range(1, ny):
        forward(oy)
    last.wait()

    largest = jnp.max(jnp.maximum(ppeak[0], ppeak[1]), axis=(0, 1), keepdims=True)
    scale = jnp.broadcast_to(0.3 / (jnp.sqrt(largest) + 1e-06), (RIM, 128))

    def next_rows(i, carry):
        at = rows_at(i * RIM + RIM, RIM)
        for q in range(4):
            for t in (0, 1):
                obj_out[q, rows_at(i * RIM, RIM), 128 * t : 128 * t + 128] = (
                    win[q, t + 1, at, :] - scale * grad[q, t, at, :]
                )
        return carry

    lax.fori_loop(0, blocks, next_rows, 0)
    landed(total_ref.at[core], recv_back)
    probe_out[...] = probe_ref[...] - (2.0 / (rows * cols)) * total_ref[...]
    left(total_ref.at[core], send_back)
    left(total_ref.at[core], send_pair)
    left(slots.at[pl.ds(1, nxy - 1)], send_xy)
    left(slots.at[pl.ds(1, nxy - 1)], send_all)
    left(zslots.at[pl.ds(0, nz - 1)], send_z)
    left(zpeak.at[pl.ds(0, nz - 1)], send_zm)
    left(xpeak.at[pl.ds(1, nxy - 1)], send_xm)


def local(rows, cols, nyx, table, perm, object_in, probe_in, positions, intensity):
    n = probe_in.shape[-1]
    npos = positions.shape[2]
    f32 = jnp.float32
    hbm = pl.BlockSpec(memory_space=pltpu.HBM)
    vmem = pl.BlockSpec(memory_space=pltpu.VMEM)
    dma = pltpu.SemaphoreType.DMA
    nxy = nyx[0] * nyx[1]
    nz = rows * cols // (CORES * nxy)
    step = n // nxy
    wide = n + 2 * RIM
    buffers = [
        (2, n, n), (npos, n, n), table.shape, perm.shape,
        (4, 4, wide, 128), (n, 128), (n, 128), (wide, 128), (wide, 128),
        (npos, 4, 2, n, 128), (npos, 2, n, n), (npos, 4, 2, n + 128, 128), (npos, 2, n, 128),
        (4, 2, wide, 128), (wide, 128), (wide, 128), (2, n, n),
        (n, n), (n, n), (nxy, step, n), (step, n), (nz, step, n),
        (nz, 8, 128), (nxy, 8, 128), (2, 8, 128), (2, n, n),
        (4, 2, RIM, 128), (4, 2, RIM, 128), (n, 128), (n, 128), (4, RIM, 128),
    ]
    scratch = [pltpu.SMEM(positions.shape, jnp.int32)]
    scratch += [VMEM(shape, jnp.bfloat16 if i in (2, 3) else f32) for i, shape in enumerate(buffers)]
    scratch += [dma((7,)), dma((8,)), dma((8,)), dma((8,)), dma((8,))]
    scratch += [dma, dma((nyx[0],)), dma, dma, dma, dma]
    scratch += [dma] * 4 + [dma, dma((nyx[0],)), dma, dma, dma, dma]
    object_out, probe_out = pl.pallas_call(
        functools.partial(kernel, rows, cols, nyx),
        out_shape=(jax.ShapeDtypeStruct((4, n, n), f32), jax.ShapeDtypeStruct((2, n, n), f32)),
        in_specs=[hbm] * 6,
        out_specs=(vmem, vmem),
        scratch_shapes=scratch,
        compiler_params=pltpu.CompilerParams(
            collective_id=0, has_side_effects=True, vmem_limit_bytes=28 * 2**20
        ),
        name="step",
    )(
        *(
            pltpu.with_memory_space_constraint(a, pltpu.HBM)
            for a in (
                positions, object_in.reshape(4, n, n), probe_in, intensity.reshape(npos, n, n),
                jnp.asarray(table), jnp.asarray(perm),
            )
        )
    )
    return object_out.reshape(object_in.shape), probe_out


def solution(mesh):
    rows, cols = mesh.shape["row"], mesh.shape["col"]
    table, perm = weights(256)
    spec = (P(None, None, "row", "col"), P(), P("row", "col", None, None), P("row", "col", None, None, None))
    return jax.shard_map(
        functools.partial(local, rows, cols, NYX, table, perm),
        mesh=mesh,
        in_specs=spec,
        out_specs=(P(None, None, "row", "col"), P()),
        check_vma=False,
    )
```

```python
import functools
import math

import jax
import jax.numpy as jnp
import numpy as np
from jax import lax
from jax.experimental import pallas as pl
from jax.experimental.pallas import tpu as pltpu
from jax.sharding import PartitionSpec as P

RIM = 32
MESH = pl.DeviceIdType.MESH
VMEM = pltpu.VMEM
AROUND = ((-1, 0), (1, 0), (0, -1), (0, 1), (-1, -1), (-1, 1), (1, -1), (1, 1))
CORES = 2
NYX = (4, 4)


def split_of(matrix):
    high = matrix.astype(jnp.bfloat16)
    low = (matrix - high.astype(np.float64)).astype(jnp.bfloat16)
    return np.stack([np.asarray(high), np.asarray(low)])


def stacked(weight):
    real, imag = weight.real, weight.imag
    return np.block([[real, imag], [-imag, real]])


def weights(extent):
    half = extent // 2
    idx = np.arange(extent)
    freq = ((idx + half) % extent - half).astype(np.float64)
    turn = np.exp(-2j * np.pi * ((idx[:, None] * idx[None, :]) % extent) / extent)
    phase = np.exp(-8j * np.pi * freq**2 / extent**2)
    band = (np.conj(turn) * phase[None, :]) @ turn / extent
    left, right = band[:half, :half], band[:half, half:]
    even = turn[:half, 0::2] / math.sqrt(extent)
    odd = turn[:half, 1::2] / math.sqrt(extent)
    plus, minus = stacked((left + right) / 2), stacked((left - right) / 2)
    ev, od = stacked(even), stacked(odd)
    table = np.stack([split_of(m) for m in (plus, minus, ev, od, od.T)])
    order = np.concatenate([idx[0::2], idx[1::2]])
    perm = np.zeros((extent, extent), np.float32)
    perm[order, idx] = 1.0
    return table, perm.astype(jnp.bfloat16)


def parts(x):
    high = x.astype(jnp.bfloat16)
    return high, (x - high.astype(jnp.float32)).astype(jnp.bfloat16)


def dot(a, b):
    return jnp.dot(a, b, preferred_element_type=jnp.float32)


def times_right(x, w_ref, k):
    high, low = parts(x)
    wh, wl = w_ref[k, 0], w_ref[k, 1]
    return dot(jnp.concatenate([high, low, high], 1), jnp.concatenate([wh, wh, wl], 0))


def times_left(x, w_ref, k):
    high, low = parts(x)
    wh, wl = w_ref[k, 0], w_ref[k, 1]
    return dot(jnp.concatenate([wh, wh, wl], 1), jnp.concatenate([high, low, high], 0))


def fold(x):
    h = x.shape[0] // 2
    s, d = x[:h] + x[h:], x[:h] - x[h:]
    return [[s[:, :h] + s[:, h:], s[:, :h] - s[:, h:]], [d[:, :h] + d[:, h:], d[:, :h] - d[:, h:]]]


def unfold(b):
    top_s, top_d = b[0][0] + b[0][1], b[0][0] - b[0][1]
    bot_s, bot_d = b[1][0] + b[1][1], b[1][0] - b[1][1]
    s = jnp.concatenate([top_s, top_d], 1)
    d = jnp.concatenate([bot_s, bot_d], 1)
    return jnp.concatenate([s + d, s - d], 0)


def sandwich(re, im, w_ref, right, left):
    h = re[0][0].shape[0]
    out = [None, None]
    for j in (0, 1):
        k, swap = right[j]
        first, second = (im, re) if swap else (re, im)
        x = jnp.concatenate(
            [jnp.concatenate([first[i][j], second[i][j]], 1) for i in (0, 1)], 0
        )
        y = times_right(x, w_ref, k)
        a, b = y[:, :h], y[:, h:]
        out[j] = (b, a) if swap else (a, b)
    res_re, res_im = [None, None], [None, None]
    for i in (0, 1):
        k, swap = left[i]
        rows = slice(i * h, (i + 1) * h)
        r = jnp.concatenate([out[0][0][rows], out[1][0][rows]], 1)
        m = jnp.concatenate([out[0][1][rows], out[1][1][rows]], 1)
        y = times_left(jnp.concatenate([m, r] if swap else [r, m], 0), w_ref, k)
        a, b = y[:h], y[h:]
        r, m = (b, a) if swap else (a, b)
        res_re[i] = [r[:, :h], r[:, h:]]
        res_im[i] = [m[:, :h], m[:, h:]]
    return res_re, res_im


PROP = (((0, False), (1, False)), ((0, True), (1, True)))
PROP_CONJ = (((0, True), (1, True)), ((0, False), (1, False)))
FORWARD = (((2, False), (3, False)), ((2, True), (4, False)))
BACKWARD = (((2, True), (4, False)), ((2, False), (3, False)))


def rows_at(start, size):
    return pl.ds(pl.multiple_of(start, size), size)


def place_of():
    return lax.axis_index("row"), lax.axis_index("col")


def neighbours(rows, cols):
    r, c = place_of()
    out = []
    for dr, dc in AROUND:
        ok = None
        if dr:
            ok = r > 0 if dr < 0 else r < rows - 1
        if dc:
            side = c > 0 if dc < 0 else c < cols - 1
            ok = side if ok is None else jnp.logical_and(ok, side)
        out.append((ok, (r + dr, c + dc)))
    return out


def opposite(d):
    dr, dc = AROUND[d]
    return AROUND.index((-dr, -dc))


def remote(src, dst, ssem, rsem, where):
    return pltpu.make_async_remote_copy(
        src_ref=src, dst_ref=dst, send_sem=ssem, recv_sem=rsem, device_id=where, device_id_type=MESH
    )


def greet(around, extra):
    barrier = pltpu.get_barrier_semaphore()
    for ok, where in around:

        @pl.when(ok)
        def _(where=where):
            pl.semaphore_signal(barrier, inc=1, device_id=where, device_id_type=MESH)

    for where in extra:
        pl.semaphore_signal(barrier, inc=1, device_id=where, device_id_type=MESH)


def await_greetings(rows, cols, extra):
    r, c = place_of()
    tall = 1 + jnp.where(r > 0, 1, 0) + jnp.where(r < rows - 1, 1, 0)
    wide = 1 + jnp.where(c > 0, 1, 0) + jnp.where(c < cols - 1, 1, 0)
    pl.semaphore_wait(pltpu.get_barrier_semaphore(), tall * wide - 1 + len(extra))


def swap_rims(around, sources, targets, send_sem, recv_sem, wave):
    for d, (ok, where) in enumerate(around):
        o = opposite(d)
        copy = remote(sources[d], targets[o], send_sem.at[wave, d], recv_sem.at[wave, o], where)
        pl.when(ok)(copy.start)
        target = targets[d]

        @pl.when(jnp.logical_not(ok))
        def _(target=target):
            target[...] = jnp.zeros(target.shape, target.dtype)


def finish_rims(around, sources, targets, send_sem, recv_sem, wave):
    for d, (ok, where) in enumerate(around):
        copy = remote(sources[d], targets[d], send_sem.at[wave, d], recv_sem.at[wave, d], where)
        pl.when(ok)(copy.wait)


def both(ref, *at):
    return jnp.concatenate([ref[(*at, 0)], ref[(*at, 1)]], 1)


def turn(x, lanes):
    return pltpu.roll(x, lanes % 128, 1) if lanes % 128 else x


def pack_sides(first, last, quarter):
    left, right = first(0), turn(last(0), 32)
    for k in range(1, 4):
        left = jnp.where(quarter == k, turn(first(k), 32 * k), left)
        right = jnp.where(quarter == k, turn(last(k), 32 * k + 32), right)
    return left, right


def kernel(
    rows, cols, nyx,
    pos_in, obj_ref, probe_in, meas_in, table_in, perm_in,
    obj_out, probe_out,
    pos_ref, probe_ref, meas_ref, w_ref, perm_ref,
    win_a, win_b, pl_buf, pr_buf, hl, hr, hc,
    cut, mid, pad, seen,
    grad, gl, gr, gcl, gcr, gp_ref,
    theirs, ours, slots, mine, zslots, zpeak, xpeak, total_ref,
    rt, rb, rl, rr, corners,
    load_sem,
    send_halo, recv_halo, send_rim, recv_rim, send_pair, recv_pair, send_xy, recv_xy, send_z, recv_z,
    send_zm, recv_zm, send_xm, recv_xm, send_all, recv_all, send_back, recv_back,
):
    n = probe_ref.shape[-1]
    h = n // 2
    npos = cut.shape[0]
    ny, nx = nyx
    nxy = ny * nx
    nzl = cols // nxy
    nz = nzl * (rows // CORES)
    step = n // nxy
    r, c = place_of()
    core, zh = lax.rem(r, CORES), lax.div(r, CORES)
    zl, here = lax.div(c, nxy), lax.rem(c, nxy)
    y, x = lax.div(here, nx), lax.rem(here, nx)
    z = zh * nzl + zl
    partner = (zh * CORES + 1 - core, c)

    def peer(d):
        q = lax.rem(y + d // nx, ny) * nx + lax.rem(x + d % nx, nx)
        return q, (r, zl * nxy + q)

    def zpeer(d):
        k = lax.rem(z + d, nz)
        return lax.div(k, nzl) * CORES + core, lax.rem(k, nzl) * nxy + here

    def zother(d):
        k = lax.rem(z + d, nz)
        return lax.div(k, nzl) * CORES + 1 - core, lax.rem(k, nzl) * nxy + here

    far = sorted(range(1, nz), key=lambda d: -min(d, nz - d))

    around = neighbours(rows, cols)
    extra = [partner]
    extra += [peer(d)[1] for d in range(1, nxy)]
    extra += [zpeer(d) for d in range(1, nz)]
    extra += [zother(d) for d in range(1, nz)]
    greet(around, extra)

    win = (win_a, win_b)
    inner = pl.ds(RIM, n)
    loads = [
        (obj_ref.at[pl.ds(2 * l, 2), :, pl.ds(128 * t, 128)], win[l].at[:, t + 1, inner, :])
        for l in (0, 1)
        for t in (0, 1)
    ]
    loads += [
        (meas_in, meas_ref),
        (perm_in, perm_ref),
        (probe_in, probe_ref),
        (table_in, w_ref),
        (pos_in, pos_ref),
    ]
    loads = [pltpu.make_async_copy(a, b, load_sem.at[i]) for i, (a, b) in enumerate(loads)]
    for load in loads:
        load.start()
    quarter = lax.div(lax.broadcasted_iota(jnp.int32, (h, 128), 1), 32)
    for l in (0, 1):
        loads[2 * l].wait()
        loads[2 * l + 1].wait()

        def piece(t, k, l=l):
            return win[l][k % 2, t, RIM + h * (k // 2) : RIM + h * (k // 2) + h, :]

        pl_buf[l], pr_buf[l] = pack_sides(lambda k: piece(1, k), lambda k: piece(2, k), quarter)
    await_greetings(rows, cols, extra)

    ups, tops = pl.ds(0, RIM), pl.ds(RIM, RIM)
    lows, downs = pl.ds(n, RIM), pl.ds(n + RIM, RIM)
    lo, hi = pl.ds(0, RIM), pl.ds(h - RIM, RIM)
    halo = [
        (
            around,
            [
                win[l].at[:, 1:3, tops, :], win[l].at[:, 1:3, lows, :], pl_buf.at[l], pr_buf.at[l],
                pl_buf.at[l, lo, :], pr_buf.at[l, lo, :], pl_buf.at[l, hi, :], pr_buf.at[l, hi, :],
            ],
            [win[l].at[:, 1:3, ups, :], win[l].at[:, 1:3, downs, :], hl.at[l], hr.at[l]]
            + [hc.at[l, k] for k in range(4)],
            send_halo,
            recv_halo,
            l,
        )
        for l in (0, 1)
    ]
    for l in (0, 1):
        swap_rims(*halo[l])

    zeros = jnp.zeros((64, 128), jnp.float32)
    for p in range(npos):
        for q in range(4):
            for t in (0, 1):
                pad[p, q, t, 0:64, :] = zeros
                pad[p, q, t, 64 + n :, :] = zeros
    loads[4].wait()
    loads[5].wait()
    for p in range(npos):
        for t in (0, 1):
            seen[p, t] = meas_ref[p, :, 128 * t : 128 * t + 128]
        meas = jnp.concatenate(
            [
                jnp.concatenate([seen[p, t, pl.ds(i, h, stride=2), :] for t in (0, 1)], 1)
                for i in (0, 1)
            ],
            0,
        )
        mh, ml = parts(meas)
        meas_ref[p] = dot(
            jnp.concatenate([mh, ml], 1), jnp.concatenate([perm_ref[...], perm_ref[...]], 0)
        )
    for load in loads[6:]:
        load.wait()
    offs = [(pos_ref[0, 0, p, 0], pos_ref[0, 0, p, 1]) for p in range(npos)]
    lane = lax.broadcasted_iota(jnp.int32, (RIM, 128), 1)

    def cut_slice(l):
        finish_rims(*halo[l])
        for a in (0, 1):
            for k in (0, 1):
                at = slice(RIM + h * k, RIM + h * k + h)
                win[l][a, 0, at, :] = turn(hl[l], 96 - 32 * (2 * k + a))
                win[l][a, 3, at, :] = turn(hr[l], -32 * (2 * k + a))
            win[l][a, 0, 0:RIM, :] = turn(hc[l, 0], 96 - 32 * (2 + a))
            win[l][a, 3, 0:RIM, :] = turn(hc[l, 1], -32 * (2 + a))
            win[l][a, 0, RIM + n :, :] = turn(hc[l, 2], 96 - 32 * a)
            win[l][a, 3, RIM + n :, :] = turn(hc[l, 3], -32 * a)

        def cut_rows(i, carry):
            for p in range(npos):
                dy, dx = offs[p]
                shift = lax.rem(128 - dx, 128)
                high, low = lane >= 128 - dx, lane < -dx
                for a in (0, 1):
                    at = pl.ds(RIM + dy + i * RIM, RIM)
                    t0, t1, t2, t3 = [pltpu.roll(win[l][a, t, at, :], shift, 1) for t in range(4)]
                    to = rows_at(i * RIM, RIM)
                    cut[p, 2 * l + a, 0, to, :] = jnp.where(high, t2, jnp.where(low, t0, t1))
                    cut[p, 2 * l + a, 1, to, :] = jnp.where(high, t3, jnp.where(low, t1, t2))
            return carry

        lax.fori_loop(0, n // RIM, cut_rows, 0)

    def keep(p, q, value):
        pad[p, q, 0, 64 : 64 + n, :] = value[:, :128]
        pad[p, q, 1, 64 : 64 + n, :] = value[:, 128:]

    quarter = lax.div(lane, 32)

    def window_rows(l, a, start):
        sums = None
        for p in range(npos):
            dy, dx = offs[p]
            shift = lax.rem(128 + dx, 128)
            low, high = lane < dx, lane >= 128 + dx
            at = pl.ds(RIM - dy + start, RIM)
            u, v = (pltpu.roll(pad[p, 2 * l + a, t, at, :], shift, 1) for t in (0, 1))
            o = jnp.zeros_like(u)
            got = [
                jnp.where(high, u, o),
                jnp.where(low, o, jnp.where(high, v, u)),
                jnp.where(low, u, jnp.where(high, o, v)),
                jnp.where(low, v, o),
            ]
            sums = got if sums is None else [e + f for e, f in zip(sums, got)]
        return sums

    def place(l, starts):
        got = [window_rows(l, a, start) for start in starts for a in (0, 1)]
        for k, four in enumerate(got):
            to = rows_at(starts[k // 2], RIM)
            grad[2 * l + k % 2, 0, to, :] = four[1]
            grad[2 * l + k % 2, 1, to, :] = four[2]
        right, left = pack_sides(lambda k: got[k][3], lambda k: got[k][0], quarter)
        return left, right

    def place_slice(l):
        gcl[l], gcr[l] = place(l, (0, RIM + n))

        def go(i, carry):
            to = rows_at(i * RIM, RIM)
            gl[l, to, :], gr[l, to, :] = place(l, (i * RIM + RIM, i * RIM + RIM + h))
            return carry

        lax.fori_loop(0, h // RIM, go, 0)

    rims = [
        (
            around,
            [grad.at[pl.ds(2 * l, 2), :, ups, :], grad.at[pl.ds(2 * l, 2), :, downs, :], gl.at[l], gr.at[l]]
            + [gcl.at[l], gcr.at[l]] * 2,
            [rt.at[l], rb.at[l], rl.at[l], rr.at[l]] + [corners.at[l, k] for k in range(4)],
            send_rim,
            recv_rim,
            l,
        )
        for l in (0, 1)
    ]

    cut_slice(0)
    for p in range(npos):
        pr, pi = probe_ref[0], probe_ref[1]
        ar, ai = both(cut, p, 0), both(cut, p, 1)
        re, im = sandwich(fold(pr * ar - pi * ai), fold(pr * ai + pi * ar), w_ref, *PROP)
        mid[p, 0], mid[p, 1] = unfold(re), unfold(im)
    cut_slice(1)
    for p in range(npos):
        qr, qi = mid[p, 0], mid[p, 1]
        br, bi = both(cut, p, 2), both(cut, p, 3)
        re, im = sandwich(fold(qr * br - qi * bi), fold(qr * bi + qi * br), w_ref, *FORWARD)
        for i in (0, 1):
            for j in (0, 1):
                fr, fi = re[i][j], im[i][j]
                seen_at = meas_ref[p, i * h : (i + 1) * h, j * h : (j + 1) * h]
                ex = 2.0 * (fr * fr + fi * fi - seen_at)
                re[i][j], im[i][j] = ex * fr, ex * fi
        re, im = sandwich(re, im, w_ref, *BACKWARD)
        hr_, hi_ = unfold(re), unfold(im)
        qr, qi = mid[p, 0], mid[p, 1]
        keep(p, 2, qr * hr_ + qi * hi_)
        keep(p, 3, qr * hi_ - qi * hr_)
        br, bi = both(cut, p, 2), both(cut, p, 3)
        mid[p, 0], mid[p, 1] = br * hr_ + bi * hi_, br * hi_ - bi * hr_
    place_slice(1)
    swap_rims(*rims[1])
    for p in range(npos):
        re, im = sandwich(fold(mid[p, 0]), fold(mid[p, 1]), w_ref, *PROP_CONJ)
        er, ei = unfold(re), unfold(im)
        pr, pi = probe_ref[0], probe_ref[1]
        keep(p, 0, pr * er + pi * ei)
        keep(p, 1, pr * ei - pi * er)
        ar, ai = both(cut, p, 0), both(cut, p, 1)
        if p == 0:
            gp_ref[0] = ar * er + ai * ei
            gp_ref[1] = ar * ei - ai * er
        else:
            gp_ref[0] += ar * er + ai * ei
            gp_ref[1] += ar * ei - ai * er

    def band(q):
        return rows_at(q * step, step)

    def stripe(row):
        return rows_at(row * step * nx, step * nx)

    def pair(oy):
        at = stripe(lax.rem(y + oy, ny))
        return at, remote(gp_ref.at[1 - core, at, :], theirs.at[at, :], send_pair, recv_pair.at[oy], partner)

    for oy in reversed(range(ny)):
        pair(oy)[1].start()

    place_slice(0)
    swap_rims(*rims[0])

    for oy in reversed(range(ny)):
        at, copy = pair(oy)
        copy.wait_recv()
        ours[at, :] = gp_ref[core, at, :] + theirs[at, :]
        for ox in reversed(range(nx)):
            d = oy * nx + ox
            if d:
                q, where = peer(d)
                remote(ours.at[band(q), :], slots.at[d], send_xy, recv_xy, where).start()

    def landed(ref, sem):
        remote(ref, ref, sem, sem, partner).wait_recv()

    def left(ref, sem):
        remote(ref, ref, sem, sem, partner).wait_send()

    landed(slots.at[pl.ds(1, nxy - 1)], recv_xy)
    acc = ours[band(here), :]
    for d in range(1, nxy):
        acc = acc + slots[d]
    mine[...] = acc
    zslots[pl.ds(z, 1)] = acc[None]
    for d in far:
        remote(mine, zslots.at[z], send_z, recv_z, zpeer(d)).start()

    first, final = lane < 32, lane >= 96
    zero = jnp.zeros((RIM, 128), jnp.float32)

    def rows_of(l, k, i):
        at, to = rows_at(i * RIM, RIM), rows_at(h * k + i * RIM + RIM, RIM)
        square = [None, None]
        for a in (0, 1):
            lane_of = 32 * (2 * k + a)
            ends = (
                jnp.where(first, turn(rl[l, at, :], -lane_of), zero),
                jnp.where(final, turn(rr[l, at, :], 96 - lane_of), zero),
            )
            for t in (0, 1):
                v = grad[2 * l + a, t, to, :] + ends[t]
                grad[2 * l + a, t, to, :] = v
                square[t] = v * v if square[t] is None else square[t] + v * v
        best = jnp.maximum(square[0], square[1])
        return functools.reduce(jnp.maximum, [best[8 * b : 8 * b + 8] for b in range(RIM // 8)])

    def add_edges(l):
        for edge, (strip, to, c) in enumerate(((rt, RIM, 0), (rb, n, 2))):
            for a in (0, 1):
                lane_of = 32 * (2 * (1 - edge) + a)
                sides = (
                    jnp.where(first, turn(corners[l, c], -lane_of), zero),
                    jnp.where(final, turn(corners[l, c + 1], 96 - lane_of), zero),
                )
                for t in (0, 1):
                    grad[2 * l + a, t, to : to + RIM, :] += strip[l, a, t] + sides[t]

    def finish_slice(l):
        finish_rims(*rims[l])
        add_edges(l)
        peak = jnp.zeros((8, 128), jnp.float32)
        for k in (0, 1):
            peak = lax.fori_loop(
                0, h // RIM, lambda i, m, k=k: jnp.maximum(m, rows_of(l, k, i)), peak
            )
        return peak

    xpeak[0] = jnp.maximum(finish_slice(1), finish_slice(0))
    for d in reversed(range(1, nxy)):
        remote(xpeak.at[0], xpeak.at[d], send_xm, recv_xm, peer(d)[1]).start()

    landed(zslots.at[pl.ds(0, nz - 1)], recv_z)
    acc = zslots[0]
    for k in range(1, nz):
        acc = acc + zslots[k]
    total_ref[pl.ds(core, 1), band(here), :] = acc[None]
    block = total_ref.at[core, band(here), :]
    for d in reversed(range(1, nxy)):
        remote(block, block, send_all, recv_all.at[d // nx], peer(d)[1]).start()

    landed(xpeak.at[pl.ds(1, nxy - 1)], recv_xm)
    peak = xpeak[0]
    for d in range(1, nxy):
        peak = jnp.maximum(peak, xpeak[d])
    zpeak[0] = peak
    for d in far:
        remote(zpeak.at[0], zpeak.at[d], send_zm, recv_zm, zpeer(d)).start()
        remote(zpeak.at[0], zpeak.at[nz + d], send_zm, recv_zm, zother(d)).start()
    remote(zpeak.at[0], zpeak.at[nz], send_zm, recv_zm, partner).start()

    def forward(oy):
        at = stripe(lax.rem(y + ny - oy, ny))
        block = total_ref.at[core, at, :]
        count = nx - 1 if oy == 0 else nx
        landed(total_ref.at[core, pl.ds(0, count * step), :], recv_all.at[oy])
        remote(block, block, send_back, recv_back, partner).start()

    for oy in range(ny):
        forward(oy)
    landed(zpeak.at[pl.ds(1, 2 * nz - 1)], recv_zm)
    peak = zpeak[0]
    for d in range(1, 2 * nz):
        peak = jnp.maximum(peak, zpeak[d])

    largest = jnp.max(peak, axis=(0, 1), keepdims=True)
    scale = jnp.broadcast_to(0.3 / (jnp.sqrt(largest) + 1e-06), (RIM, 128))

    def next_rows(i, carry):
        at = rows_at(i * RIM + RIM, RIM)
        for q in range(4):
            for t in (0, 1):
                obj_out[q, rows_at(i * RIM, RIM), 128 * t : 128 * t + 128] = (
                    win[q // 2][q % 2, t + 1, at, :] - scale * grad[q, t, at, :]
                )
        return carry

    lax.fori_loop(0, n // RIM, next_rows, 0)
    landed(total_ref.at[core], recv_back)
    probe_out[...] = probe_ref[...] - (2.0 / (rows * cols)) * total_ref[...]
    left(total_ref.at[core], send_back)
    left(total_ref.at[core], send_pair)
    left(slots.at[pl.ds(1, nxy - 1)], send_xy)
    left(slots.at[pl.ds(1, nxy - 1)], send_all)
    left(zslots.at[pl.ds(0, nz - 1)], send_z)
    left(zpeak.at[pl.ds(1, 2 * nz - 1)], send_zm)
    left(xpeak.at[pl.ds(1, nxy - 1)], send_xm)


def local(rows, cols, nyx, table, perm, object_in, probe_in, positions, intensity):
    n = probe_in.shape[-1]
    npos = positions.shape[2]
    f32 = jnp.float32
    hbm = pl.BlockSpec(memory_space=pltpu.HBM)
    vmem = pl.BlockSpec(memory_space=pltpu.VMEM)
    dma = pltpu.SemaphoreType.DMA
    nxy = nyx[0] * nyx[1]
    nz = rows * cols // (CORES * nxy)
    step = n // nxy
    wide = n + 2 * RIM
    buffers = [
        (2, n, n), (npos, n, n), table.shape, perm.shape,
        (2, 4, wide, 128), (2, 4, wide, 128), (2, n // 2, 128), (2, n // 2, 128), (2, n // 2, 128), (2, n // 2, 128),
        (2, 4, RIM, 128),
        (npos, 4, 2, n, 128), (npos, 2, n, n), (npos, 4, 2, n + 128, 128), (npos, 2, n, 128),
        (4, 2, wide, 128), (2, n // 2, 128), (2, n // 2, 128), (2, RIM, 128), (2, RIM, 128), (2, n, n),
        (n, n), (n, n), (nxy, step, n), (step, n), (nz, step, n),
        (2 * nz, 8, 128), (nxy, 8, 128), (2, n, n),
        (2, 2, 2, RIM, 128), (2, 2, 2, RIM, 128), (2, n // 2, 128), (2, n // 2, 128), (2, 4, RIM, 128),
    ]
    scratch = [pltpu.SMEM(positions.shape, jnp.int32)]
    scratch += [VMEM(shape, jnp.bfloat16 if i in (2, 3) else f32) for i, shape in enumerate(buffers)]
    scratch += [dma((9,)), dma((2, 8)), dma((2, 8)), dma((2, 8)), dma((2, 8))]
    scratch += [dma, dma((nyx[0],)), dma, dma, dma, dma]
    scratch += [dma] * 4 + [dma, dma((nyx[0],)), dma, dma]
    object_out, probe_out = pl.pallas_call(
        functools.partial(kernel, rows, cols, nyx),
        out_shape=(jax.ShapeDtypeStruct((4, n, n), f32), jax.ShapeDtypeStruct((2, n, n), f32)),
        in_specs=[hbm] * 6,
        out_specs=(vmem, vmem),
        scratch_shapes=scratch,
        compiler_params=pltpu.CompilerParams(
            collective_id=0, has_side_effects=True, vmem_limit_bytes=28 * 2**20
        ),
        name="step",
    )(
        *(
            pltpu.with_memory_space_constraint(a, pltpu.HBM)
            for a in (
                positions, object_in.reshape(4, n, n), probe_in, intensity.reshape(npos, n, n),
                jnp.asarray(table), jnp.asarray(perm),
            )
        )
    )
    return object_out.reshape(object_in.shape), probe_out


def solution(mesh):
    rows, cols = mesh.shape["row"], mesh.shape["col"]
    table, perm = weights(256)
    spec = (P(None, None, "row", "col"), P(), P("row", "col", None, None), P("row", "col", None, None, None))
    return jax.shard_map(
        functools.partial(local, rows, cols, NYX, table, perm),
        mesh=mesh,
        in_specs=spec,
        out_specs=(P(None, None, "row", "col"), P()),
        check_vma=False,
    )
```

```python
import functools
import math

import jax
import jax.numpy as jnp
import numpy as np
from jax import lax
from jax.experimental import pallas as pl
from jax.experimental.pallas import tpu as pltpu
from jax.sharding import PartitionSpec as P

RIM = 32
MESH = pl.DeviceIdType.MESH
VMEM = pltpu.VMEM
AROUND = ((-1, 0), (1, 0), (0, -1), (0, 1), (-1, -1), (-1, 1), (1, -1), (1, 1))
CORES = 2
NYX = (4, 4)


def split_of(matrix):
    high = matrix.astype(jnp.bfloat16)
    low = (matrix - high.astype(np.float64)).astype(jnp.bfloat16)
    return np.stack([np.asarray(high), np.asarray(low)])


def stacked(weight):
    real, imag = weight.real, weight.imag
    return np.block([[real, imag], [-imag, real]])


def weights(extent):
    half = extent // 2
    idx = np.arange(extent)
    freq = ((idx + half) % extent - half).astype(np.float64)
    turn = np.exp(-2j * np.pi * ((idx[:, None] * idx[None, :]) % extent) / extent)
    phase = np.exp(-8j * np.pi * freq**2 / extent**2)
    band = (np.conj(turn) * phase[None, :]) @ turn / extent
    left, right = band[:half, :half], band[:half, half:]
    even = turn[:half, 0::2] / math.sqrt(extent)
    odd = turn[:half, 1::2] / math.sqrt(extent)
    plus, minus = stacked((left + right) / 2), stacked((left - right) / 2)
    ev, od = stacked(even), stacked(odd)
    table = np.stack([split_of(m) for m in (plus, minus, ev, od, od.T)])
    order = np.concatenate([idx[0::2], idx[1::2]])
    perm = np.zeros((extent, extent), np.float32)
    perm[order, idx] = 1.0
    return table, perm.astype(jnp.bfloat16)


def parts(x):
    high = x.astype(jnp.bfloat16)
    return high, (x - high.astype(jnp.float32)).astype(jnp.bfloat16)


def dot(a, b):
    return jnp.dot(a, b, preferred_element_type=jnp.float32)


def times_right(split, w_ref, k):
    high, low = split
    wh, wl = w_ref[k, 0], w_ref[k, 1]
    return dot(jnp.concatenate([high, low, high], 1), jnp.concatenate([wh, wh, wl], 0))


def times_left(split, w_ref, k):
    high, low = split
    wh, wl = w_ref[k, 0], w_ref[k, 1]
    return dot(jnp.concatenate([wh, wh, wl], 1), jnp.concatenate([high, low, high], 0))


def fold(x):
    h = x.shape[0] // 2
    s, d = x[:h] + x[h:], x[:h] - x[h:]
    return [[s[:, :h] + s[:, h:], s[:, :h] - s[:, h:]], [d[:, :h] + d[:, h:], d[:, :h] - d[:, h:]]]


def unfold(b):
    top_s, top_d = b[0][0] + b[0][1], b[0][0] - b[0][1]
    bot_s, bot_d = b[1][0] + b[1][1], b[1][0] - b[1][1]
    s = jnp.concatenate([top_s, top_d], 1)
    d = jnp.concatenate([bot_s, bot_d], 1)
    return jnp.concatenate([s + d, s - d], 0)


def sandwich(re, im, w_ref, right, left):
    h = re[0][0].shape[0]
    split = []
    for j in (0, 1):
        first, second = (im, re) if right[j][1] else (re, im)
        x = jnp.concatenate(
            [jnp.concatenate([first[i][j], second[i][j]], 1) for i in (0, 1)], 0
        )
        split.append(parts(x))
    yield
    out = []
    for j in (0, 1):
        k, swap = right[j]
        y = times_right(split[j], w_ref, k)
        a, b = y[:, :h], y[:, h:]
        out.append((b, a) if swap else (a, b))
    yield
    split = []
    for i in (0, 1):
        rows = slice(i * h, (i + 1) * h)
        r = jnp.concatenate([out[0][0][rows], out[1][0][rows]], 1)
        m = jnp.concatenate([out[0][1][rows], out[1][1][rows]], 1)
        split.append(parts(jnp.concatenate([m, r] if left[i][1] else [r, m], 0)))
    yield
    res_re, res_im = [None, None], [None, None]
    for i in (0, 1):
        k, swap = left[i]
        y = times_left(split[i], w_ref, k)
        a, b = y[:h], y[h:]
        r, m = (b, a) if swap else (a, b)
        res_re[i] = [r[:, :h], r[:, h:]]
        res_im[i] = [m[:, :h], m[:, h:]]
    yield
    return res_re, res_im


def staggered(*runs):
    live = list(enumerate(runs))
    turn_of = 0
    while live:
        for item in list(live):
            lag, run = item
            if turn_of >= lag:
                try:
                    next(run)
                except StopIteration:
                    live.remove(item)
        turn_of += 1


PROP = (((0, False), (1, False)), ((0, True), (1, True)))
PROP_CONJ = (((0, True), (1, True)), ((0, False), (1, False)))
FORWARD = (((2, False), (3, False)), ((2, True), (4, False)))
BACKWARD = (((2, True), (4, False)), ((2, False), (3, False)))


def rows_at(start, size):
    return pl.ds(pl.multiple_of(start, size), size)


def place_of():
    return lax.axis_index("row"), lax.axis_index("col")


def neighbours(rows, cols):
    r, c = place_of()
    return [(lax.rem(r + dr + rows, rows), lax.rem(c + dc + cols, cols)) for dr, dc in AROUND]


def opposite(d):
    dr, dc = AROUND[d]
    return AROUND.index((-dr, -dc))


def remote(src, dst, ssem, rsem, where):
    return pltpu.make_async_remote_copy(
        src_ref=src, dst_ref=dst, send_sem=ssem, recv_sem=rsem, device_id=where, device_id_type=MESH
    )


def greet(peers):
    for where in peers:
        pl.semaphore_signal(pltpu.get_barrier_semaphore(), inc=1, device_id=where, device_id_type=MESH)


CORNERS, STRAIGHT, ALONG, ACROSS = (4, 5, 6, 7), (0, 1, 2, 3), (0, 1), (2, 3)


def swap_rims(around, sources, targets, send_sem, recv_sem, these):
    for d in these:
        o = opposite(d)
        remote(sources[d], targets[o], send_sem, recv_sem, around[d]).start()


def both(ref, *at):
    return jnp.concatenate([ref[(*at, 0)], ref[(*at, 1)]], 1)


def distant(count):
    return sorted(range(count), key=lambda d: -min(d, count - d))


def turn(x, lanes):
    return pltpu.roll(x, lanes % 128, 1) if lanes % 128 else x


def pack_sides(first, last, quarter):
    left, right = first(0), turn(last(0), 32)
    for k in range(1, 4):
        left = jnp.where(quarter == k, turn(first(k), 32 * k), left)
        right = jnp.where(quarter == k, turn(last(k), 32 * k + 32), right)
    return left, right


def kernel(
    rows, cols, nyx,
    pos_in, obj_ref, probe_in, meas_in, table_in, perm_in,
    obj_out, probe_out,
    pos_ref, probe_ref, meas_ref, w_ref, perm_ref,
    win_a, win_b, pl_buf, pr_buf, hl, hr, hc,
    cut, mid, pad, seen,
    grad, gl, gr, gcl, gcr, gp_ref,
    theirs, ours, slots, mine, zslots, zpeak, xpeak, total_ref,
    rt, rb, rl, rr, corners,
    load_sem,
    send_halo, recv_halo, send_rim, recv_rim, send_pair, recv_pair, send_xy, recv_xy, send_z, recv_z,
    send_zm, recv_zm, send_xm, recv_xm, send_all, recv_all, send_back, recv_back,
):
    n = probe_ref.shape[-1]
    h = n // 2
    npos = cut.shape[0]
    ny, nx = nyx
    nxy = ny * nx
    nzl = cols // nxy
    nz = nzl * (rows // CORES)
    step = n // nxy
    r, c = place_of()
    core, zh = lax.rem(r, CORES), lax.div(r, CORES)
    zl, here = lax.div(c, nxy), lax.rem(c, nxy)
    y, x = lax.div(here, nx), lax.rem(here, nx)
    z = zh * nzl + zl
    partner = (zh * CORES + 1 - core, c)

    def peer(d):
        q = lax.rem(y + d // nx, ny) * nx + lax.rem(x + d % nx, nx)
        return q, (r, zl * nxy + q)

    def zpeer(d):
        k = lax.rem(z + d, nz)
        return lax.div(k, nzl) * CORES + core, lax.rem(k, nzl) * nxy + here

    def zother(d):
        k = lax.rem(z + d, nz)
        return lax.div(k, nzl) * CORES + 1 - core, lax.rem(k, nzl) * nxy + here

    far = distant(nz)[:-1]
    spread = [oy * nx + ox for oy in distant(ny) for ox in distant(nx)][:-1]

    around = neighbours(rows, cols)
    extra = [partner]
    extra += [peer(d)[1] for d in range(1, nxy)]
    extra += [zpeer(d) for d in range(1, nz)]
    extra += [zother(d) for d in range(1, nz)]
    greet(around + extra)
    above, below, before, after = r > 0, r < rows - 1, c > 0, c < cols - 1

    def only(ok, value):
        return jnp.where(ok, value, jnp.zeros_like(value))

    win = (win_a, win_b)
    inner = pl.ds(RIM, n)
    loads = [
        (obj_ref.at[pl.ds(2 * l, 2), :, pl.ds(128 * t, 128)], win[l].at[:, t + 1, inner, :])
        for l in (0, 1)
        for t in (0, 1)
    ]
    loads += [
        (meas_in, meas_ref),
        (perm_in, perm_ref),
        (probe_in, probe_ref),
        (table_in, w_ref),
        (pos_in, pos_ref),
    ]
    loads = [pltpu.make_async_copy(a, b, load_sem.at[i]) for i, (a, b) in enumerate(loads)]
    for load in loads:
        load.start()
    quarter = lax.div(lax.broadcasted_iota(jnp.int32, (h, 128), 1), 32)
    for l in (0, 1):
        loads[2 * l].wait()
        loads[2 * l + 1].wait()

        def piece(t, k, l=l):
            return win[l][k % 2, t, RIM + h * (k // 2) : RIM + h * (k // 2) + h, :]

        pl_buf[l], pr_buf[l] = pack_sides(lambda k: piece(1, k), lambda k: piece(2, k), quarter)
    pl.semaphore_wait(pltpu.get_barrier_semaphore(), len(around) + len(extra))

    def landed(ref, sem):
        remote(ref, ref, sem, sem, partner).wait_recv()

    def left(ref, sem):
        remote(ref, ref, sem, sem, partner).wait_send()

    wave = win[0].at[0, pl.ds(0, 2), :, :]

    ups, tops = pl.ds(0, RIM), pl.ds(RIM, RIM)
    lows, downs = pl.ds(n, RIM), pl.ds(n + RIM, RIM)
    lo, hi = pl.ds(0, RIM), pl.ds(h - RIM, RIM)
    halo = [
        (
            around,
            [
                win[l].at[:, 1:3, tops, :], win[l].at[:, 1:3, lows, :], pl_buf.at[l], pr_buf.at[l],
                pl_buf.at[l, lo, :], pr_buf.at[l, lo, :], pl_buf.at[l, hi, :], pr_buf.at[l, hi, :],
            ],
            [win[l].at[:, 1:3, ups, :], win[l].at[:, 1:3, downs, :], hl.at[l], hr.at[l]]
            + [hc.at[l, k] for k in range(4)],
            send_halo.at[l],
            recv_halo.at[l],
        )
        for l in (0, 1)
    ]
    swap_rims(*halo[0], CORNERS + STRAIGHT)
    swap_rims(*halo[1], CORNERS + STRAIGHT)

    zeros = jnp.zeros((64, 128), jnp.float32)
    for p in range(npos):
        for q in range(4):
            for t in (0, 1):
                pad[p, q, t, 0:64, :] = zeros
                pad[p, q, t, 64 + n :, :] = zeros
    loads[4].wait()
    loads[5].wait()
    for p in range(npos):
        for t in (0, 1):
            seen[p, t] = meas_ref[p, :, 128 * t : 128 * t + 128]
        meas = jnp.concatenate(
            [
                jnp.concatenate([seen[p, t, pl.ds(i, h, stride=2), :] for t in (0, 1)], 1)
                for i in (0, 1)
            ],
            0,
        )
        mh, ml = parts(meas)
        meas_ref[p] = dot(
            jnp.concatenate([mh, ml], 1), jnp.concatenate([perm_ref[...], perm_ref[...]], 0)
        )
    for load in loads[6:]:
        load.wait()
    offs = [(pos_ref[0, 0, p, 0], pos_ref[0, 0, p, 1]) for p in range(npos)]
    lane = lax.broadcasted_iota(jnp.int32, (RIM, 128), 1)
    chunk = 2 * RIM
    long_lane = lax.broadcasted_iota(jnp.int32, (chunk, 128), 1)

    def cut_slice(l):
        landed(wave, recv_halo.at[l])
        left(wave, send_halo.at[l])
        for a in (0, 1):
            for t in (1, 2):
                win[l][a, t, 0:RIM, :] = only(above, win[l][a, t, 0:RIM, :])
                win[l][a, t, RIM + n :, :] = only(below, win[l][a, t, RIM + n :, :])
            for k in (0, 1):
                at = slice(RIM + h * k, RIM + h * k + h)
                win[l][a, 0, at, :] = only(before, turn(hl[l], 96 - 32 * (2 * k + a)))
                win[l][a, 3, at, :] = only(after, turn(hr[l], -32 * (2 * k + a)))
            for k, (row, ok) in enumerate(((0, above), (RIM + n, below))):
                lane_of = 32 * (2 * (1 - k) + a)
                at = slice(row, row + RIM)
                win[l][a, 0, at, :] = only(
                    jnp.logical_and(ok, before), turn(hc[l, 2 * k], 96 - lane_of)
                )
                win[l][a, 3, at, :] = only(jnp.logical_and(ok, after), turn(hc[l, 2 * k + 1], -lane_of))

        def cut_rows(i, carry):
            for p in range(npos):
                dy, dx = offs[p]
                shift = lax.rem(128 - dx, 128)
                high, low = long_lane >= 128 - dx, long_lane < -dx
                for a in (0, 1):
                    at = pl.ds(RIM + dy + i * chunk, chunk)
                    t0, t1, t2, t3 = [pltpu.roll(win[l][a, t, at, :], shift, 1) for t in range(4)]
                    to = rows_at(i * chunk, chunk)
                    cut[p, 2 * l + a, 0, to, :] = jnp.where(high, t2, jnp.where(low, t0, t1))
                    cut[p, 2 * l + a, 1, to, :] = jnp.where(high, t3, jnp.where(low, t1, t2))
            return carry

        lax.fori_loop(0, n // chunk, cut_rows, 0)

    def keep(p, q, value):
        pad[p, q, 0, 64 : 64 + n, :] = value[:, :128]
        pad[p, q, 1, 64 : 64 + n, :] = value[:, 128:]

    quarter = lax.div(lane, 32)

    def window_rows(l, a, start):
        sums = None
        for p in range(npos):
            dy, dx = offs[p]
            shift = lax.rem(128 + dx, 128)
            low, high = lane < dx, lane >= 128 + dx
            at = pl.ds(RIM - dy + start, RIM)
            u, v = (pltpu.roll(pad[p, 2 * l + a, t, at, :], shift, 1) for t in (0, 1))
            o = jnp.zeros_like(u)
            got = [
                jnp.where(high, u, o),
                jnp.where(low, o, jnp.where(high, v, u)),
                jnp.where(low, u, jnp.where(high, o, v)),
                jnp.where(low, v, o),
            ]
            sums = got if sums is None else [e + f for e, f in zip(sums, got)]
        return sums

    def place(l, starts):
        got = [window_rows(l, a, start) for start in starts for a in (0, 1)]
        for k, four in enumerate(got):
            to = rows_at(starts[k // 2], RIM)
            grad[2 * l + k % 2, 0, to, :] = four[1]
            grad[2 * l + k % 2, 1, to, :] = four[2]
        right, left = pack_sides(lambda k: got[k][3], lambda k: got[k][0], quarter)
        return left, right

    def place_slice(l):
        gcl[l], gcr[l] = place(l, (0, RIM + n))
        swap_rims(*rims[l], CORNERS + ALONG)

        def go(i, carry):
            to = rows_at(i * RIM, RIM)
            gl[l, to, :], gr[l, to, :] = place(l, (i * RIM + RIM, i * RIM + RIM + h))
            return carry

        lax.fori_loop(0, h // RIM, go, 0)
        swap_rims(*rims[l], ACROSS)

    rims = [
        (
            around,
            [grad.at[pl.ds(2 * l, 2), :, ups, :], grad.at[pl.ds(2 * l, 2), :, downs, :], gl.at[l], gr.at[l]]
            + [gcl.at[l], gcr.at[l]] * 2,
            [rt.at[l], rb.at[l], rl.at[l], rr.at[l]] + [corners.at[l, k] for k in range(4)],
            send_rim.at[l],
            recv_rim.at[l],
        )
        for l in (0, 1)
    ]

    def first_pass(p):
        pr, pi = probe_ref[0], probe_ref[1]
        ar, ai = both(cut, p, 0), both(cut, p, 1)
        re, im = yield from sandwich(
            fold(pr * ar - pi * ai), fold(pr * ai + pi * ar), w_ref, *PROP
        )
        mid[p, 0], mid[p, 1] = unfold(re), unfold(im)

    def second_pass(p):
        qr, qi = mid[p, 0], mid[p, 1]
        br, bi = both(cut, p, 2), both(cut, p, 3)
        re, im = yield from sandwich(
            fold(qr * br - qi * bi), fold(qr * bi + qi * br), w_ref, *FORWARD
        )
        for i in (0, 1):
            for j in (0, 1):
                fr, fi = re[i][j], im[i][j]
                seen_at = meas_ref[p, i * h : (i + 1) * h, j * h : (j + 1) * h]
                ex = 2.0 * (fr * fr + fi * fi - seen_at)
                re[i][j], im[i][j] = ex * fr, ex * fi
        re, im = yield from sandwich(re, im, w_ref, *BACKWARD)
        hr_, hi_ = unfold(re), unfold(im)
        qr, qi = mid[p, 0], mid[p, 1]
        keep(p, 2, qr * hr_ + qi * hi_)
        keep(p, 3, qr * hi_ - qi * hr_)
        br, bi = both(cut, p, 2), both(cut, p, 3)
        mid[p, 0], mid[p, 1] = br * hr_ + bi * hi_, br * hi_ - bi * hr_

    def third_pass(p):
        re, im = yield from sandwich(fold(mid[p, 0]), fold(mid[p, 1]), w_ref, *PROP_CONJ)
        er, ei = unfold(re), unfold(im)
        pr, pi = probe_ref[0], probe_ref[1]
        keep(p, 0, pr * er + pi * ei)
        keep(p, 1, pr * ei - pi * er)
        ar, ai = both(cut, p, 0), both(cut, p, 1)
        if p == 0:
            gp_ref[0] = ar * er + ai * ei
            gp_ref[1] = ar * ei - ai * er
        else:
            gp_ref[0] += ar * er + ai * ei
            gp_ref[1] += ar * ei - ai * er

    cut_slice(0)
    staggered(*[first_pass(p) for p in range(npos)])
    cut_slice(1)
    staggered(*[second_pass(p) for p in range(npos)])
    place_slice(1)
    staggered(*[third_pass(p) for p in range(npos)])

    def band(q):
        return rows_at(q * step, step)

    def stripe(row):
        return rows_at(row * step * nx, step * nx)

    def pair(oy):
        at = stripe(lax.rem(y + oy, ny))
        return at, remote(gp_ref.at[1 - core, at, :], theirs.at[at, :], send_pair, recv_pair.at[oy], partner)

    for oy in distant(ny):
        pair(oy)[1].start()

    place_slice(0)

    for oy in distant(ny):
        at, copy = pair(oy)
        copy.wait_recv()
        ours[at, :] = gp_ref[core, at, :] + theirs[at, :]
        for ox in distant(nx):
            d = oy * nx + ox
            if d:
                q, where = peer(d)
                remote(ours.at[band(q), :], slots.at[d], send_xy, recv_xy, where).start()

    landed(slots.at[pl.ds(1, nxy - 1)], recv_xy)
    acc = ours[band(here), :]
    for d in range(1, nxy):
        acc = acc + slots[d]
    mine[...] = acc
    zslots[pl.ds(z, 1)] = acc[None]
    for d in far:
        remote(mine, zslots.at[z], send_z, recv_z, zpeer(d)).start()

    first_in = lane < jnp.where(before, 32, 0)
    final_in = lane >= jnp.where(after, 96, 128)
    zero = jnp.zeros((RIM, 128), jnp.float32)

    def rows_of(l, k, i):
        at, to = rows_at(i * RIM, RIM), rows_at(h * k + i * RIM + RIM, RIM)
        square = [None, None]
        for a in (0, 1):
            lane_of = 32 * (2 * k + a)
            ends = (
                jnp.where(first_in, turn(rl[l, at, :], -lane_of), zero),
                jnp.where(final_in, turn(rr[l, at, :], 96 - lane_of), zero),
            )
            for t in (0, 1):
                v = grad[2 * l + a, t, to, :] + ends[t]
                grad[2 * l + a, t, to, :] = v
                square[t] = v * v if square[t] is None else square[t] + v * v
        best = jnp.maximum(square[0], square[1])
        return functools.reduce(jnp.maximum, [best[8 * b : 8 * b + 8] for b in range(RIM // 8)])

    def add_edges(l):
        for edge, (strip, to, ok) in enumerate(((rt, RIM, above), (rb, n, below))):
            for a in (0, 1):
                lane_of = 32 * (2 * (1 - edge) + a)
                sides = (
                    jnp.where(first_in, turn(corners[l, 2 * edge], -lane_of), zero),
                    jnp.where(final_in, turn(corners[l, 2 * edge + 1], 96 - lane_of), zero),
                )
                for t in (0, 1):
                    grad[2 * l + a, t, to : to + RIM, :] += only(ok, strip[l, a, t] + sides[t])

    def finish_slice(l):
        landed(wave, recv_rim.at[l])
        left(wave, send_rim.at[l])
        add_edges(l)
        peak = jnp.zeros((8, 128), jnp.float32)
        for k in (0, 1):
            peak = lax.fori_loop(
                0, h // RIM, lambda i, m, k=k: jnp.maximum(m, rows_of(l, k, i)), peak
            )
        return peak

    xpeak[0] = jnp.maximum(finish_slice(1), finish_slice(0))
    for d in spread:
        remote(xpeak.at[0], xpeak.at[d], send_xm, recv_xm, peer(d)[1]).start()

    landed(zslots.at[pl.ds(0, nz - 1)], recv_z)
    acc = zslots[0]
    for k in range(1, nz):
        acc = acc + zslots[k]
    total_ref[pl.ds(core, 1), band(here), :] = acc[None]
    block = total_ref.at[core, band(here), :]
    for d in spread:
        remote(block, block, send_all, recv_all.at[d // nx], peer(d)[1]).start()

    landed(xpeak.at[pl.ds(1, nxy - 1)], recv_xm)
    peak = xpeak[0]
    for d in range(1, nxy):
        peak = jnp.maximum(peak, xpeak[d])
    zpeak[0] = peak
    for d in far:
        remote(zpeak.at[0], zpeak.at[d], send_zm, recv_zm, zpeer(d)).start()
        remote(zpeak.at[0], zpeak.at[nz + d], send_zm, recv_zm, zother(d)).start()
    remote(zpeak.at[0], zpeak.at[nz], send_zm, recv_zm, partner).start()

    def forward(oy):
        at = stripe(lax.rem(y + ny - oy, ny))
        block = total_ref.at[core, at, :]
        count = nx - 1 if oy == 0 else nx
        landed(total_ref.at[core, pl.ds(0, count * step), :], recv_all.at[oy])
        remote(block, block, send_back, recv_back, partner).start()

    for oy in reversed(distant(ny)):
        forward(oy)
    landed(zpeak.at[pl.ds(1, 2 * nz - 1)], recv_zm)
    peak = zpeak[0]
    for d in range(1, 2 * nz):
        peak = jnp.maximum(peak, zpeak[d])

    largest = jnp.max(peak, axis=(0, 1), keepdims=True)
    scale = jnp.broadcast_to(0.3 / (jnp.sqrt(largest) + 1e-06), (RIM, 128))

    def next_rows(i, carry):
        at = rows_at(i * RIM + RIM, RIM)
        for q in range(4):
            for t in (0, 1):
                obj_out[q, rows_at(i * RIM, RIM), 128 * t : 128 * t + 128] = (
                    win[q // 2][q % 2, t + 1, at, :] - scale * grad[q, t, at, :]
                )
        return carry

    lax.fori_loop(0, n // RIM, next_rows, 0)
    landed(total_ref.at[core], recv_back)
    probe_out[...] = probe_ref[...] - (2.0 / (rows * cols)) * total_ref[...]
    left(total_ref.at[core], send_back)
    left(total_ref.at[core], send_pair)
    left(slots.at[pl.ds(1, nxy - 1)], send_xy)
    left(slots.at[pl.ds(1, nxy - 1)], send_all)
    left(zslots.at[pl.ds(0, nz - 1)], send_z)
    left(zpeak.at[pl.ds(1, 2 * nz - 1)], send_zm)
    left(xpeak.at[pl.ds(1, nxy - 1)], send_xm)


def local(rows, cols, nyx, table, perm, object_in, probe_in, positions, intensity):
    n = probe_in.shape[-1]
    npos = positions.shape[2]
    f32 = jnp.float32
    hbm = pl.BlockSpec(memory_space=pltpu.HBM)
    vmem = pl.BlockSpec(memory_space=pltpu.VMEM)
    dma = pltpu.SemaphoreType.DMA
    nxy = nyx[0] * nyx[1]
    nz = rows * cols // (CORES * nxy)
    step = n // nxy
    wide = n + 2 * RIM
    buffers = [
        (2, n, n), (npos, n, n), table.shape, perm.shape,
        (2, 4, wide, 128), (2, 4, wide, 128), (2, n // 2, 128), (2, n // 2, 128), (2, n // 2, 128), (2, n // 2, 128),
        (2, 4, RIM, 128),
        (npos, 4, 2, n, 128), (npos, 2, n, n), (npos, 4, 2, n + 128, 128), (npos, 2, n, 128),
        (4, 2, wide, 128), (2, n // 2, 128), (2, n // 2, 128), (2, RIM, 128), (2, RIM, 128), (2, n, n),
        (n, n), (n, n), (nxy, step, n), (step, n), (nz, step, n),
        (2 * nz, 8, 128), (nxy, 8, 128), (2, n, n),
        (2, 2, 2, RIM, 128), (2, 2, 2, RIM, 128), (2, n // 2, 128), (2, n // 2, 128), (2, 4, RIM, 128),
    ]
    scratch = [pltpu.SMEM(positions.shape, jnp.int32)]
    scratch += [VMEM(shape, jnp.bfloat16 if i in (2, 3) else f32) for i, shape in enumerate(buffers)]
    scratch += [dma((9,)), dma((2,)), dma((2,)), dma((2,)), dma((2,))]
    scratch += [dma, dma((nyx[0],)), dma, dma, dma, dma]
    scratch += [dma] * 4 + [dma, dma((nyx[0],)), dma, dma]
    object_out, probe_out = pl.pallas_call(
        functools.partial(kernel, rows, cols, nyx),
        out_shape=(jax.ShapeDtypeStruct((4, n, n), f32), jax.ShapeDtypeStruct((2, n, n), f32)),
        in_specs=[hbm] * 6,
        out_specs=(vmem, vmem),
        scratch_shapes=scratch,
        compiler_params=pltpu.CompilerParams(
            collective_id=0, has_side_effects=True, vmem_limit_bytes=28 * 2**20
        ),
        name="step",
    )(
        *(
            pltpu.with_memory_space_constraint(a, pltpu.HBM)
            for a in (
                positions, object_in.reshape(4, n, n), probe_in, intensity.reshape(npos, n, n),
                jnp.asarray(table), jnp.asarray(perm),
            )
        )
    )
    return object_out.reshape(object_in.shape), probe_out


def solution(mesh):
    rows, cols = mesh.shape["row"], mesh.shape["col"]
    table, perm = weights(256)
    spec = (P(None, None, "row", "col"), P(), P("row", "col", None, None), P("row", "col", None, None, None))
    return jax.shard_map(
        functools.partial(local, rows, cols, NYX, table, perm),
        mesh=mesh,
        in_specs=spec,
        out_specs=(P(None, None, "row", "col"), P()),
        check_vma=False,
    )
```

```python
import functools
import math

import jax
import jax.numpy as jnp
import numpy as np
from jax import lax
from jax.experimental import pallas as pl
from jax.experimental.pallas import tpu as pltpu
from jax.sharding import PartitionSpec as P

RIM = 32
MESH = pl.DeviceIdType.MESH
VMEM = pltpu.VMEM
AROUND = ((-1, 0), (1, 0), (0, -1), (0, 1), (-1, -1), (-1, 1), (1, -1), (1, 1))
CORES = 2
NYX = (4, 4)


def split_of(matrix):
    high = matrix.astype(jnp.bfloat16)
    low = (matrix - high.astype(np.float64)).astype(jnp.bfloat16)
    return np.stack([np.asarray(high), np.asarray(low)])


def stacked(weight):
    real, imag = weight.real, weight.imag
    return np.block([[real, imag], [-imag, real]])


def weights(extent):
    half = extent // 2
    idx = np.arange(extent)
    freq = ((idx + half) % extent - half).astype(np.float64)
    turn = np.exp(-2j * np.pi * ((idx[:, None] * idx[None, :]) % extent) / extent)
    phase = np.exp(-8j * np.pi * freq**2 / extent**2)
    band = (np.conj(turn) * phase[None, :]) @ turn / extent
    left, right = band[:half, :half], band[:half, half:]
    even = turn[:half, 0::2] / math.sqrt(extent)
    odd = turn[:half, 1::2] / math.sqrt(extent)
    plus, minus = stacked((left + right) / 2), stacked((left - right) / 2)
    ev, od = stacked(even), stacked(odd)
    table = np.stack([split_of(m) for m in (plus, minus, ev, od, od.T)])
    order = np.concatenate([idx[0::2], idx[1::2]])
    perm = np.zeros((extent, extent), np.float32)
    perm[order, idx] = 1.0
    return table, perm.astype(jnp.bfloat16)


def parts(x):
    high = x.astype(jnp.bfloat16)
    return high, (x - high.astype(jnp.float32)).astype(jnp.bfloat16)


def dot(a, b):
    return jnp.dot(a, b, preferred_element_type=jnp.float32)


def times_right(split, w_ref, k):
    high, low = split
    wh, wl = w_ref[k, 0], w_ref[k, 1]
    rows = high.shape[0]
    y = dot(jnp.concatenate([high, low], 0), wh)
    return y[:rows] + (y[rows:] + dot(high, wl))


def times_left(split, w_ref, k):
    high, low = split
    wh, wl = w_ref[k, 0], w_ref[k, 1]
    rows = wh.shape[0]
    y = dot(jnp.concatenate([wh, wl], 0), high)
    return y[:rows] + (y[rows:] + dot(wh, low))


def fold(x):
    h = x.shape[0] // 2
    s, d = x[:h] + x[h:], x[:h] - x[h:]
    return [[s[:, :h] + s[:, h:], s[:, :h] - s[:, h:]], [d[:, :h] + d[:, h:], d[:, :h] - d[:, h:]]]


def unfold(b):
    top_s, top_d = b[0][0] + b[0][1], b[0][0] - b[0][1]
    bot_s, bot_d = b[1][0] + b[1][1], b[1][0] - b[1][1]
    s = jnp.concatenate([top_s, top_d], 1)
    d = jnp.concatenate([bot_s, bot_d], 1)
    return jnp.concatenate([s + d, s - d], 0)


def sandwich(re, im, w_ref, right, left):
    h = re[0][0].shape[0]
    split = []
    for j in (0, 1):
        first, second = (im, re) if right[j][1] else (re, im)
        x = jnp.concatenate(
            [jnp.concatenate([first[i][j], second[i][j]], 1) for i in (0, 1)], 0
        )
        split.append(parts(x))
    yield
    out = []
    for j in (0, 1):
        k, swap = right[j]
        y = times_right(split[j], w_ref, k)
        a, b = y[:, :h], y[:, h:]
        out.append((b, a) if swap else (a, b))
    yield
    split = []
    for i in (0, 1):
        rows = slice(i * h, (i + 1) * h)
        r = jnp.concatenate([out[0][0][rows], out[1][0][rows]], 1)
        m = jnp.concatenate([out[0][1][rows], out[1][1][rows]], 1)
        split.append(parts(jnp.concatenate([m, r] if left[i][1] else [r, m], 0)))
    yield
    res_re, res_im = [None, None], [None, None]
    for i in (0, 1):
        k, swap = left[i]
        y = times_left(split[i], w_ref, k)
        a, b = y[:h], y[h:]
        r, m = (b, a) if swap else (a, b)
        res_re[i] = [r[:, :h], r[:, h:]]
        res_im[i] = [m[:, :h], m[:, h:]]
    yield
    return res_re, res_im


def staggered(*runs):
    live = list(enumerate(runs))
    turn_of = 0
    while live:
        for item in list(live):
            lag, run = item
            if turn_of >= lag:
                try:
                    next(run)
                except StopIteration:
                    live.remove(item)
        turn_of += 1


PROP = (((0, False), (1, False)), ((0, True), (1, True)))
PROP_CONJ = (((0, True), (1, True)), ((0, False), (1, False)))
FORWARD = (((2, False), (3, False)), ((2, True), (4, False)))
BACKWARD = (((2, True), (4, False)), ((2, False), (3, False)))


def rows_at(start, size):
    if isinstance(start, int):
        return pl.ds(start, size)
    return pl.ds(pl.multiple_of(start, size), size)


def place_of():
    return lax.axis_index("row"), lax.axis_index("col")


def neighbours(rows, cols):
    r, c = place_of()
    return [(lax.rem(r + dr + rows, rows), lax.rem(c + dc + cols, cols)) for dr, dc in AROUND]


def opposite(d):
    dr, dc = AROUND[d]
    return AROUND.index((-dr, -dc))


def remote(src, dst, ssem, rsem, where):
    return pltpu.make_async_remote_copy(
        src_ref=src, dst_ref=dst, send_sem=ssem, recv_sem=rsem, device_id=where, device_id_type=MESH
    )


def greet(peers):
    for where in peers:
        pl.semaphore_signal(pltpu.get_barrier_semaphore(), inc=1, device_id=where, device_id_type=MESH)


CORNERS, STRAIGHT, ALONG, ACROSS = (4, 5, 6, 7), (0, 1, 2, 3), (0, 1), (2, 3)


def swap_rims(around, sources, targets, send_sem, recv_sem, these):
    for d in these:
        o = opposite(d)
        remote(sources[d], targets[o], send_sem, recv_sem, around[d]).start()


def both(ref, *at):
    return jnp.concatenate([ref[(*at, 0)], ref[(*at, 1)]], 1)


def distant(count):
    return sorted(range(count), key=lambda d: -min(d, count - d))


def turn(x, lanes):
    return pltpu.roll(x, lanes % 128, 1) if lanes % 128 else x


def pack_sides(first, last, quarter):
    left, right = first(0), turn(last(0), 32)
    for k in range(1, 4):
        left = jnp.where(quarter == k, turn(first(k), 32 * k), left)
        right = jnp.where(quarter == k, turn(last(k), 32 * k + 32), right)
    return left, right


def kernel(
    rows, cols, nyx,
    pos_in, obj_ref, probe_in, meas_in, table_in, perm_in,
    obj_out, probe_out,
    pos_ref, probe_ref, meas_ref, w_ref, perm_ref,
    win_a, win_b, pl_buf, pr_buf, hl, hr, hc,
    cut, mid, pad, seen,
    grad, gl, gr, gcl, gcr, gp_ref,
    theirs, ours, slots, mine, zslots, zpeak, xpeak, total_ref,
    rt, rb, rl, rr, corners,
    load_sem,
    send_halo, recv_halo, send_rim, recv_rim, send_pair, recv_pair, send_xy, recv_xy, send_z, recv_z,
    send_zm, recv_zm, send_xm, recv_xm, send_all, recv_all, send_back, recv_back,
):
    n = probe_ref.shape[-1]
    h = n // 2
    npos = cut.shape[0]
    ny, nx = nyx
    nxy = ny * nx
    nzl = cols // nxy
    nz = nzl * (rows // CORES)
    step = n // nxy
    r, c = place_of()
    core, zh = lax.rem(r, CORES), lax.div(r, CORES)
    zl, here = lax.div(c, nxy), lax.rem(c, nxy)
    y, x = lax.div(here, nx), lax.rem(here, nx)
    z = zh * nzl + zl
    partner = (zh * CORES + 1 - core, c)

    def peer(d):
        q = lax.rem(y + d // nx, ny) * nx + lax.rem(x + d % nx, nx)
        return q, (r, zl * nxy + q)

    def zpeer(d):
        k = lax.rem(z + d, nz)
        return lax.div(k, nzl) * CORES + core, lax.rem(k, nzl) * nxy + here

    def zother(d):
        k = lax.rem(z + d, nz)
        return lax.div(k, nzl) * CORES + 1 - core, lax.rem(k, nzl) * nxy + here

    far = distant(nz)[:-1]
    spread = sorted(range(1, nxy), key=lambda d: -min(d // nx, ny - d // nx) - min(d % nx, nx - d % nx))

    around = neighbours(rows, cols)
    extra = [partner]
    extra += [peer(d)[1] for d in range(1, nxy)]
    extra += [zpeer(d) for d in range(1, nz)]
    extra += [zother(d) for d in range(1, nz)]
    greet(extra[::-1] + around)
    above, below, before, after = r > 0, r < rows - 1, c > 0, c < cols - 1

    def only(ok, value):
        return jnp.where(ok, value, jnp.zeros_like(value))

    win = (win_a, win_b)
    inner = pl.ds(RIM, n)
    loads = [
        (obj_ref.at[pl.ds(2 * l, 2), :, pl.ds(128 * t, 128)], win[l].at[:, t + 1, inner, :])
        for l in (0, 1)
        for t in (0, 1)
    ]
    loads += [
        (meas_in, meas_ref),
        (perm_in, perm_ref),
        (probe_in, probe_ref),
        (table_in, w_ref),
        (pos_in, pos_ref),
    ]
    loads = [pltpu.make_async_copy(a, b, load_sem.at[i]) for i, (a, b) in enumerate(loads)]
    for load in loads:
        load.start()
    quarter = lax.div(lax.broadcasted_iota(jnp.int32, (h, 128), 1), 32)
    for l in (0, 1):
        loads[2 * l].wait()
        loads[2 * l + 1].wait()

        def piece(t, k, l=l):
            return win[l][k % 2, t, RIM + h * (k // 2) : RIM + h * (k // 2) + h, :]

        pl_buf[l], pr_buf[l] = pack_sides(lambda k: piece(1, k), lambda k: piece(2, k), quarter)
    pl.semaphore_wait(pltpu.get_barrier_semaphore(), len(around) + len(extra))

    def landed(ref, sem):
        remote(ref, ref, sem, sem, partner).wait_recv()

    def left(ref, sem):
        remote(ref, ref, sem, sem, partner).wait_send()

    wave = win[0].at[0, pl.ds(0, 2), :, :]

    ups, tops = pl.ds(0, RIM), pl.ds(RIM, RIM)
    lows, downs = pl.ds(n, RIM), pl.ds(n + RIM, RIM)
    lo, hi = pl.ds(0, RIM), pl.ds(h - RIM, RIM)
    halo = [
        (
            around,
            [
                win[l].at[:, 1:3, tops, :], win[l].at[:, 1:3, lows, :], pl_buf.at[l], pr_buf.at[l],
                pl_buf.at[l, lo, :], pr_buf.at[l, lo, :], pl_buf.at[l, hi, :], pr_buf.at[l, hi, :],
            ],
            [win[l].at[:, 1:3, ups, :], win[l].at[:, 1:3, downs, :], hl.at[l], hr.at[l]]
            + [hc.at[l, k] for k in range(4)],
            send_halo.at[l],
            recv_halo.at[l],
        )
        for l in (0, 1)
    ]
    swap_rims(*halo[0], CORNERS + STRAIGHT)
    swap_rims(*halo[1], CORNERS + STRAIGHT)

    zeros = jnp.zeros((64, 128), jnp.float32)
    for p in range(npos):
        for q in range(4):
            for t in (0, 1):
                pad[p, q, t, 0:64, :] = zeros
                pad[p, q, t, 64 + n :, :] = zeros
    loads[4].wait()
    loads[5].wait()
    for p in range(npos):
        for t in (0, 1):
            seen[p, t] = meas_ref[p, :, 128 * t : 128 * t + 128]
        meas = jnp.concatenate(
            [
                jnp.concatenate([seen[p, t, pl.ds(i, h, stride=2), :] for t in (0, 1)], 1)
                for i in (0, 1)
            ],
            0,
        )
        mh, ml = parts(meas)
        meas_ref[p] = dot(
            jnp.concatenate([mh, ml], 1), jnp.concatenate([perm_ref[...], perm_ref[...]], 0)
        )
    for load in loads[6:]:
        load.wait()
    offs = [(pos_ref[0, 0, p, 0], pos_ref[0, 0, p, 1]) for p in range(npos)]
    lane = lax.broadcasted_iota(jnp.int32, (RIM, 128), 1)
    chunk = 2 * RIM
    long_lane = lax.broadcasted_iota(jnp.int32, (chunk, 128), 1)

    def cut_slice(l):
        landed(wave, recv_halo.at[l])
        left(wave, send_halo.at[l])
        for a in (0, 1):
            for t in (1, 2):
                win[l][a, t, 0:RIM, :] = only(above, win[l][a, t, 0:RIM, :])
                win[l][a, t, RIM + n :, :] = only(below, win[l][a, t, RIM + n :, :])
            for k in (0, 1):
                at = slice(RIM + h * k, RIM + h * k + h)
                win[l][a, 0, at, :] = only(before, turn(hl[l], 96 - 32 * (2 * k + a)))
                win[l][a, 3, at, :] = only(after, turn(hr[l], -32 * (2 * k + a)))
            for k, (row, ok) in enumerate(((0, above), (RIM + n, below))):
                lane_of = 32 * (2 * (1 - k) + a)
                at = slice(row, row + RIM)
                win[l][a, 0, at, :] = only(
                    jnp.logical_and(ok, before), turn(hc[l, 2 * k], 96 - lane_of)
                )
                win[l][a, 3, at, :] = only(jnp.logical_and(ok, after), turn(hc[l, 2 * k + 1], -lane_of))

        def cut_rows(i, carry):
            for p in range(npos):
                dy, dx = offs[p]
                shift = lax.rem(128 - dx, 128)
                high, low = long_lane >= 128 - dx, long_lane < -dx
                for a in (0, 1):
                    at = pl.ds(RIM + dy + i * chunk, chunk)
                    t0, t1, t2, t3 = [pltpu.roll(win[l][a, t, at, :], shift, 1) for t in range(4)]
                    to = rows_at(i * chunk, chunk)
                    cut[p, 2 * l + a, 0, to, :] = jnp.where(high, t2, jnp.where(low, t0, t1))
                    cut[p, 2 * l + a, 1, to, :] = jnp.where(high, t3, jnp.where(low, t1, t2))
            return carry

        lax.fori_loop(0, n // chunk, cut_rows, 0)

    def keep(p, q, value):
        pad[p, q, 0, 64 : 64 + n, :] = value[:, :128]
        pad[p, q, 1, 64 : 64 + n, :] = value[:, 128:]

    quarter = lax.div(lane, 32)

    def window_rows(l, a, start):
        sums = None
        for p in range(npos):
            dy, dx = offs[p]
            shift = lax.rem(128 + dx, 128)
            low, high = lane < dx, lane >= 128 + dx
            at = pl.ds(RIM - dy + start, RIM)
            u, v = (pltpu.roll(pad[p, 2 * l + a, t, at, :], shift, 1) for t in (0, 1))
            o = jnp.zeros_like(u)
            got = [
                jnp.where(high, u, o),
                jnp.where(low, o, jnp.where(high, v, u)),
                jnp.where(low, u, jnp.where(high, o, v)),
                jnp.where(low, v, o),
            ]
            sums = got if sums is None else [e + f for e, f in zip(sums, got)]
        return sums

    def place(l, starts):
        got = [window_rows(l, a, start) for start in starts for a in (0, 1)]
        for k, four in enumerate(got):
            to = rows_at(starts[k // 2], RIM)
            grad[2 * l + k % 2, 0, to, :] = four[1]
            grad[2 * l + k % 2, 1, to, :] = four[2]
        right, left = pack_sides(lambda k: got[k][3], lambda k: got[k][0], quarter)
        return left, right

    def place_steps(l):
        gcl[l], gcr[l] = place(l, (0, RIM + n))
        swap_rims(*rims[l], CORNERS + ALONG)
        for i in range(h // RIM):
            yield
            to = pl.ds(i * RIM, RIM)
            gl[l, to, :], gr[l, to, :] = place(l, (i * RIM + RIM, i * RIM + RIM + h))
        swap_rims(*rims[l], ACROSS)

    def place_slice(l):
        gcl[l], gcr[l] = place(l, (0, RIM + n))
        swap_rims(*rims[l], CORNERS + ALONG)

        def go(i, carry):
            to = rows_at(i * RIM, RIM)
            gl[l, to, :], gr[l, to, :] = place(l, (i * RIM + RIM, i * RIM + RIM + h))
            return carry

        lax.fori_loop(0, h // RIM, go, 0)
        swap_rims(*rims[l], ACROSS)

    rims = [
        (
            around,
            [grad.at[pl.ds(2 * l, 2), :, ups, :], grad.at[pl.ds(2 * l, 2), :, downs, :], gl.at[l], gr.at[l]]
            + [gcl.at[l], gcr.at[l]] * 2,
            [rt.at[l], rb.at[l], rl.at[l], rr.at[l]] + [corners.at[l, k] for k in range(4)],
            send_rim.at[l],
            recv_rim.at[l],
        )
        for l in (0, 1)
    ]

    def first_pass(p):
        pr, pi = probe_ref[0], probe_ref[1]
        ar, ai = both(cut, p, 0), both(cut, p, 1)
        re, im = yield from sandwich(
            fold(pr * ar - pi * ai), fold(pr * ai + pi * ar), w_ref, *PROP
        )
        mid[p, 0], mid[p, 1] = unfold(re), unfold(im)

    def second_pass(p):
        qr, qi = mid[p, 0], mid[p, 1]
        br, bi = both(cut, p, 2), both(cut, p, 3)
        re, im = yield from sandwich(
            fold(qr * br - qi * bi), fold(qr * bi + qi * br), w_ref, *FORWARD
        )
        for i in (0, 1):
            for j in (0, 1):
                fr, fi = re[i][j], im[i][j]
                seen_at = meas_ref[p, i * h : (i + 1) * h, j * h : (j + 1) * h]
                ex = 2.0 * (fr * fr + fi * fi - seen_at)
                re[i][j], im[i][j] = ex * fr, ex * fi
        re, im = yield from sandwich(re, im, w_ref, *BACKWARD)
        hr_, hi_ = unfold(re), unfold(im)
        qr, qi = mid[p, 0], mid[p, 1]
        keep(p, 2, qr * hr_ + qi * hi_)
        keep(p, 3, qr * hi_ - qi * hr_)
        br, bi = both(cut, p, 2), both(cut, p, 3)
        mid[p, 0], mid[p, 1] = br * hr_ + bi * hi_, br * hi_ - bi * hr_

    def third_pass(p):
        re, im = yield from sandwich(fold(mid[p, 0]), fold(mid[p, 1]), w_ref, *PROP_CONJ)
        er, ei = unfold(re), unfold(im)
        pr, pi = probe_ref[0], probe_ref[1]
        keep(p, 0, pr * er + pi * ei)
        keep(p, 1, pr * ei - pi * er)
        ar, ai = both(cut, p, 0), both(cut, p, 1)
        if p == 0:
            gp_ref[0] = ar * er + ai * ei
            gp_ref[1] = ar * ei - ai * er
        else:
            gp_ref[0] += ar * er + ai * ei
            gp_ref[1] += ar * ei - ai * er

    cut_slice(0)
    staggered(*[first_pass(p) for p in range(npos)])
    cut_slice(1)
    staggered(*[second_pass(p) for p in range(npos)])
    staggered(*[third_pass(p) for p in range(npos)], place_steps(1))

    def band(q):
        return rows_at(q * step, step)

    def stripe(row):
        return rows_at(row * step * nx, step * nx)

    def pair(oy):
        at = stripe(lax.rem(y + oy, ny))
        return at, remote(gp_ref.at[1 - core, at, :], theirs.at[at, :], send_pair, recv_pair.at[oy], partner)

    for oy in distant(ny):
        pair(oy)[1].start()

    place_slice(0)

    for oy in distant(ny):
        at, copy = pair(oy)
        copy.wait_recv()
        ours[at, :] = gp_ref[core, at, :] + theirs[at, :]
        for ox in distant(nx):
            d = oy * nx + ox
            if d:
                q, where = peer(d)
                remote(ours.at[band(q), :], slots.at[d], send_xy, recv_xy, where).start()

    landed(slots.at[pl.ds(1, nxy - 1)], recv_xy)
    acc = ours[band(here), :]
    for d in range(1, nxy):
        acc = acc + slots[d]
    mine[...] = acc
    zslots[pl.ds(z, 1)] = acc[None]
    for d in far:
        remote(mine, zslots.at[z], send_z, recv_z, zpeer(d)).start()

    first_in = lane < jnp.where(before, 32, 0)
    final_in = lane >= jnp.where(after, 96, 128)
    zero = jnp.zeros((RIM, 128), jnp.float32)

    def rows_of(l, k, i):
        at, to = rows_at(i * RIM, RIM), rows_at(h * k + i * RIM + RIM, RIM)
        square = [None, None]
        for a in (0, 1):
            lane_of = 32 * (2 * k + a)
            ends = (
                jnp.where(first_in, turn(rl[l, at, :], -lane_of), zero),
                jnp.where(final_in, turn(rr[l, at, :], 96 - lane_of), zero),
            )
            for t in (0, 1):
                v = grad[2 * l + a, t, to, :] + ends[t]
                grad[2 * l + a, t, to, :] = v
                square[t] = v * v if square[t] is None else square[t] + v * v
        best = jnp.maximum(square[0], square[1])
        return functools.reduce(jnp.maximum, [best[8 * b : 8 * b + 8] for b in range(RIM // 8)])

    def add_edges(l):
        for edge, (strip, to, ok) in enumerate(((rt, RIM, above), (rb, n, below))):
            for a in (0, 1):
                lane_of = 32 * (2 * (1 - edge) + a)
                sides = (
                    jnp.where(first_in, turn(corners[l, 2 * edge], -lane_of), zero),
                    jnp.where(final_in, turn(corners[l, 2 * edge + 1], 96 - lane_of), zero),
                )
                for t in (0, 1):
                    grad[2 * l + a, t, to : to + RIM, :] += only(ok, strip[l, a, t] + sides[t])

    def finish_slice(l):
        landed(wave, recv_rim.at[l])
        left(wave, send_rim.at[l])
        add_edges(l)
        peak = jnp.zeros((8, 128), jnp.float32)
        for k in (0, 1):
            peak = lax.fori_loop(
                0, h // RIM, lambda i, m, k=k: jnp.maximum(m, rows_of(l, k, i)), peak, unroll=True
            )
        return peak

    xpeak[0] = jnp.maximum(finish_slice(1), finish_slice(0))
    for d in spread:
        remote(xpeak.at[0], xpeak.at[d], send_xm, recv_xm, peer(d)[1]).start()

    landed(zslots.at[pl.ds(0, nz - 1)], recv_z)
    acc = zslots[0]
    for k in range(1, nz):
        acc = acc + zslots[k]
    total_ref[pl.ds(core, 1), band(here), :] = acc[None]
    block = total_ref.at[core, band(here), :]
    for d in spread:
        remote(block, block, send_all, recv_all.at[d], peer(d)[1]).start()

    nearest = [0] + spread[::-1]
    forward_own = remote(block, block, send_back, recv_back, partner)
    forward_own.start()
    landed(xpeak.at[pl.ds(1, nxy - 1)], recv_xm)
    peak = xpeak[0]
    for d in range(1, nxy):
        peak = jnp.maximum(peak, xpeak[d])
    zpeak[0] = peak
    for d in far:
        remote(zpeak.at[0], zpeak.at[d], send_zm, recv_zm, zpeer(d)).start()
        remote(zpeak.at[0], zpeak.at[nz + d], send_zm, recv_zm, zother(d)).start()
    remote(zpeak.at[0], zpeak.at[nz], send_zm, recv_zm, partner).start()

    def forward(d):
        q = lax.rem(y + ny - d // nx, ny) * nx + lax.rem(x + nx - d % nx, nx)
        block = total_ref.at[core, band(q), :]
        landed(block, recv_all.at[d])
        remote(block, block, send_back, recv_back, partner).start()

    for d in nearest[1:]:
        forward(d)
    landed(zpeak.at[pl.ds(1, 2 * nz - 1)], recv_zm)
    peak = zpeak[0]
    for d in range(1, 2 * nz):
        peak = jnp.maximum(peak, zpeak[d])

    largest = jnp.max(peak, axis=(0, 1), keepdims=True)
    scale = jnp.broadcast_to(0.3 / (jnp.sqrt(largest) + 1e-06), (RIM, 128))

    def next_rows(i, carry):
        at = rows_at(i * RIM + RIM, RIM)
        for q in range(4):
            for t in (0, 1):
                obj_out[q, rows_at(i * RIM, RIM), 128 * t : 128 * t + 128] = (
                    win[q // 2][q % 2, t + 1, at, :] - scale * grad[q, t, at, :]
                )
        return carry

    lax.fori_loop(0, n // RIM, next_rows, 0, unroll=2)
    landed(total_ref.at[core], recv_back)
    probe_out[...] = probe_ref[...] - (2.0 / (rows * cols)) * total_ref[...]
    left(total_ref.at[core], send_back)
    left(total_ref.at[core], send_pair)
    left(slots.at[pl.ds(1, nxy - 1)], send_xy)
    left(slots.at[pl.ds(1, nxy - 1)], send_all)
    left(zslots.at[pl.ds(0, nz - 1)], send_z)
    left(zpeak.at[pl.ds(1, 2 * nz - 1)], send_zm)
    left(xpeak.at[pl.ds(1, nxy - 1)], send_xm)


def hand_out(object_ref, probe_ref, object_out, probe_out, sem):
    copies = [(object_ref.at[q], object_out.at[q]) for q in range(4)]
    copies += [(probe_ref.at[q], probe_out.at[q]) for q in range(2)]
    copies = [pltpu.make_async_copy(a, b, sem.at[i]) for i, (a, b) in enumerate(copies)]
    for copy in copies:
        copy.start()
    for copy in copies:
        copy.wait()


def local(rows, cols, nyx, table, perm, object_in, probe_in, positions, intensity):
    n = probe_in.shape[-1]
    npos = positions.shape[2]
    f32 = jnp.float32
    hbm = pl.BlockSpec(memory_space=pltpu.HBM)
    vmem = pl.BlockSpec(memory_space=pltpu.VMEM)
    dma = pltpu.SemaphoreType.DMA
    nxy = nyx[0] * nyx[1]
    nz = rows * cols // (CORES * nxy)
    step = n // nxy
    wide = n + 2 * RIM
    buffers = [
        (2, n, n), (npos, n, n), table.shape, perm.shape,
        (2, 4, wide, 128), (2, 4, wide, 128), (2, n // 2, 128), (2, n // 2, 128), (2, n // 2, 128), (2, n // 2, 128),
        (2, 4, RIM, 128),
        (npos, 4, 2, n, 128), (npos, 2, n, n), (npos, 4, 2, n + 128, 128), (npos, 2, n, 128),
        (4, 2, wide, 128), (2, n // 2, 128), (2, n // 2, 128), (2, RIM, 128), (2, RIM, 128), (2, n, n),
        (n, n), (n, n), (nxy, step, n), (step, n), (nz, step, n),
        (2 * nz, 8, 128), (nxy, 8, 128), (2, n, n),
        (2, 2, 2, RIM, 128), (2, 2, 2, RIM, 128), (2, n // 2, 128), (2, n // 2, 128), (2, 4, RIM, 128),
    ]
    scratch = [pltpu.SMEM(positions.shape, jnp.int32)]
    scratch += [VMEM(shape, jnp.bfloat16 if i in (2, 3) else f32) for i, shape in enumerate(buffers)]
    scratch += [dma((9,)), dma((2,)), dma((2,)), dma((2,)), dma((2,))]
    scratch += [dma, dma((nyx[0],)), dma, dma, dma, dma]
    scratch += [dma] * 4 + [dma, dma((nxy,)), dma, dma]
    object_out, probe_out = pl.pallas_call(
        functools.partial(kernel, rows, cols, nyx),
        out_shape=(jax.ShapeDtypeStruct((4, n, n), f32), jax.ShapeDtypeStruct((2, n, n), f32)),
        in_specs=[hbm] * 6,
        out_specs=(vmem, vmem),
        scratch_shapes=scratch,
        compiler_params=pltpu.CompilerParams(
            collective_id=0, has_side_effects=True, vmem_limit_bytes=28 * 2**20
        ),
        name="step",
    )(
        *(
            pltpu.with_memory_space_constraint(a, pltpu.HBM)
            for a in (
                positions, object_in.reshape(4, n, n), probe_in, intensity.reshape(npos, n, n),
                jnp.asarray(table), jnp.asarray(perm),
            )
        )
    )
    object_out, probe_out = pl.pallas_call(
        hand_out,
        out_shape=(jax.ShapeDtypeStruct((4, n, n), f32), jax.ShapeDtypeStruct((2, n, n), f32)),
        in_specs=[vmem, vmem],
        out_specs=(hbm, hbm),
        scratch_shapes=[dma((6,))],
        compiler_params=pltpu.CompilerParams(vmem_limit_bytes=2**20),
        name="hand_out",
    )(object_out, probe_out)
    return object_out.reshape(object_in.shape), probe_out


def solution(mesh):
    rows, cols = mesh.shape["row"], mesh.shape["col"]
    table, perm = weights(256)
    spec = (P(None, None, "row", "col"), P(), P("row", "col", None, None), P("row", "col", None, None, None))
    return jax.shard_map(
        functools.partial(local, rows, cols, NYX, table, perm),
        mesh=mesh,
        in_specs=spec,
        out_specs=(P(None, None, "row", "col"), P()),
        check_vma=False,
    )
```

```python
import functools
import math

import jax
import jax.numpy as jnp
import numpy as np
from jax import lax
from jax.experimental import pallas as pl
from jax.experimental.pallas import tpu as pltpu
from jax.sharding import PartitionSpec as P

RIM = 32
MESH = pl.DeviceIdType.MESH
VMEM = pltpu.VMEM
AROUND = ((-1, 0), (1, 0), (0, -1), (0, 1), (-1, -1), (-1, 1), (1, -1), (1, 1))
CORES = 2
NYX = (4, 4)


def split_of(matrix):
    high = matrix.astype(jnp.bfloat16)
    low = (matrix - high.astype(np.float64)).astype(jnp.bfloat16)
    return np.stack([np.asarray(high), np.asarray(low)])


def stacked(weight):
    real, imag = weight.real, weight.imag
    return np.block([[real, imag], [-imag, real]])


def weights(extent):
    half = extent // 2
    idx = np.arange(extent)
    freq = ((idx + half) % extent - half).astype(np.float64)
    turn = np.exp(-2j * np.pi * ((idx[:, None] * idx[None, :]) % extent) / extent)
    phase = np.exp(-8j * np.pi * freq**2 / extent**2)
    band = (np.conj(turn) * phase[None, :]) @ turn / extent
    left, right = band[:half, :half], band[:half, half:]
    even = turn[:half, 0::2] / math.sqrt(extent)
    odd = turn[:half, 1::2] / math.sqrt(extent)
    plus, minus = stacked((left + right) / 2), stacked((left - right) / 2)
    ev, od = stacked(even), stacked(odd)
    table = np.stack([split_of(m) for m in (plus, minus, ev, od, od.T)])
    order = np.concatenate([idx[0::2], idx[1::2]])
    perm = np.zeros((extent, extent), np.float32)
    perm[order, idx] = 1.0
    return table, perm.astype(jnp.bfloat16)


def parts(x):
    high = x.astype(jnp.bfloat16)
    return high, (x - high.astype(jnp.float32)).astype(jnp.bfloat16)


def dot(a, b):
    return jnp.dot(a, b, preferred_element_type=jnp.float32)


def times_right(split, w_ref, k):
    high, low = split
    wh, wl = w_ref[k, 0], w_ref[k, 1]
    rows = high.shape[0]
    y = dot(jnp.concatenate([high, low], 0), wh)
    return y[:rows] + (y[rows:] + dot(high, wl))


def times_left(split, w_ref, k):
    high, low = split
    wh, wl = w_ref[k, 0], w_ref[k, 1]
    rows = wh.shape[0]
    y = dot(jnp.concatenate([wh, wl], 0), high)
    return y[:rows] + (y[rows:] + dot(wh, low))


def fold(x):
    h = x.shape[0] // 2
    s, d = x[:h] + x[h:], x[:h] - x[h:]
    return [[s[:, :h] + s[:, h:], s[:, :h] - s[:, h:]], [d[:, :h] + d[:, h:], d[:, :h] - d[:, h:]]]


def unfold(b):
    top_s, top_d = b[0][0] + b[0][1], b[0][0] - b[0][1]
    bot_s, bot_d = b[1][0] + b[1][1], b[1][0] - b[1][1]
    s = jnp.concatenate([top_s, top_d], 1)
    d = jnp.concatenate([bot_s, bot_d], 1)
    return jnp.concatenate([s + d, s - d], 0)


def sandwich(re, im, w_ref, right, left):
    h = re[0][0].shape[0]
    split = []
    for j in (0, 1):
        first, second = (im, re) if right[j][1] else (re, im)
        x = jnp.concatenate(
            [jnp.concatenate([first[i][j], second[i][j]], 1) for i in (0, 1)], 0
        )
        split.append(parts(x))
    yield
    out = []
    for j in (0, 1):
        k, swap = right[j]
        y = times_right(split[j], w_ref, k)
        a, b = y[:, :h], y[:, h:]
        out.append((b, a) if swap else (a, b))
    yield
    split = []
    for i in (0, 1):
        rows = slice(i * h, (i + 1) * h)
        r = jnp.concatenate([out[0][0][rows], out[1][0][rows]], 1)
        m = jnp.concatenate([out[0][1][rows], out[1][1][rows]], 1)
        split.append(parts(jnp.concatenate([m, r] if left[i][1] else [r, m], 0)))
    yield
    res_re, res_im = [None, None], [None, None]
    for i in (0, 1):
        k, swap = left[i]
        y = times_left(split[i], w_ref, k)
        a, b = y[:h], y[h:]
        r, m = (b, a) if swap else (a, b)
        res_re[i] = [r[:, :h], r[:, h:]]
        res_im[i] = [m[:, :h], m[:, h:]]
    yield
    return res_re, res_im


def staggered(*runs):
    live = list(enumerate(runs))
    turn_of = 0
    while live:
        for item in list(live):
            lag, run = item
            if turn_of >= lag:
                try:
                    next(run)
                except StopIteration:
                    live.remove(item)
        turn_of += 1


PROP = (((0, False), (1, False)), ((0, True), (1, True)))
PROP_CONJ = (((0, True), (1, True)), ((0, False), (1, False)))
FORWARD = (((2, False), (3, False)), ((2, True), (4, False)))
BACKWARD = (((2, True), (4, False)), ((2, False), (3, False)))


def rows_at(start, size):
    if isinstance(start, int):
        return pl.ds(start, size)
    return pl.ds(pl.multiple_of(start, size), size)


def place_of():
    return lax.axis_index("row"), lax.axis_index("col")


def neighbours(rows, cols):
    r, c = place_of()
    return [(lax.rem(r + dr + rows, rows), lax.rem(c + dc + cols, cols)) for dr, dc in AROUND]


def opposite(d):
    dr, dc = AROUND[d]
    return AROUND.index((-dr, -dc))


def remote(src, dst, ssem, rsem, where):
    return pltpu.make_async_remote_copy(
        src_ref=src, dst_ref=dst, send_sem=ssem, recv_sem=rsem, device_id=where, device_id_type=MESH
    )


def greet(peers):
    for where in peers:
        pl.semaphore_signal(pltpu.get_barrier_semaphore(), inc=1, device_id=where, device_id_type=MESH)


CORNERS, STRAIGHT, ALONG, ACROSS = (4, 5, 6, 7), (0, 1, 2, 3), (0, 1), (2, 3)


def swap_rims(around, sources, targets, send_sem, recv_sem, these):
    for d in these:
        o = opposite(d)
        remote(sources[d], targets[o], send_sem, recv_sem, around[d]).start()


def both(ref, *at):
    return jnp.concatenate([ref[(*at, 0)], ref[(*at, 1)]], 1)


def distant(count):
    return sorted(range(count), key=lambda d: -min(d, count - d))


def turn(x, lanes):
    return pltpu.roll(x, lanes % 128, 1) if lanes % 128 else x


def pack_sides(first, last, quarter):
    left, right = first(0), turn(last(0), 32)
    for k in range(1, 4):
        left = jnp.where(quarter == k, turn(first(k), 32 * k), left)
        right = jnp.where(quarter == k, turn(last(k), 32 * k + 32), right)
    return left, right


def kernel(
    rows, cols, nyx,
    pos_in, obj_ref, probe_in, meas_in, table_in, perm_in,
    obj_out, probe_out,
    pos_ref, probe_ref, meas_ref, w_ref, perm_ref,
    win_a, win_b, pl_buf, pr_buf, hl, hr, hc,
    cut, mid, pad, seen,
    grad, gl, gr, gcl, gcr, gp_ref,
    theirs, ours, slots, mine, zslots, zpeak, xpeak, total_ref,
    rt, rb, rl, rr, corners,
    load_sem,
    send_halo, recv_halo, send_rim, recv_rim, send_pair, recv_pair, send_xy, recv_xy, send_z, recv_z,
    send_zm, recv_zm, send_xm, recv_xm, send_all, recv_all, send_back, recv_back,
):
    n = probe_ref.shape[-1]
    h = n // 2
    npos = cut.shape[0]
    ny, nx = nyx
    nxy = ny * nx
    nzl = cols // nxy
    nz = nzl * (rows // CORES)
    step = n // nxy
    r, c = place_of()
    core, zh = lax.rem(r, CORES), lax.div(r, CORES)
    zl, here = lax.div(c, nxy), lax.rem(c, nxy)
    y, x = lax.div(here, nx), lax.rem(here, nx)
    z = zh * nzl + zl
    partner = (zh * CORES + 1 - core, c)

    def peer(d):
        q = lax.rem(y + d // nx, ny) * nx + lax.rem(x + d % nx, nx)
        return q, (r, zl * nxy + q)

    def zpeer(d):
        k = lax.rem(z + d, nz)
        return lax.div(k, nzl) * CORES + core, lax.rem(k, nzl) * nxy + here

    def zother(d):
        k = lax.rem(z + d, nz)
        return lax.div(k, nzl) * CORES + 1 - core, lax.rem(k, nzl) * nxy + here

    far = distant(nz)[:-1]
    spread = sorted(range(1, nxy), key=lambda d: -min(d // nx, ny - d // nx) - min(d % nx, nx - d % nx))

    around = neighbours(rows, cols)
    extra = [partner]
    extra += [peer(d)[1] for d in range(1, nxy)]
    extra += [zpeer(d) for d in range(1, nz)]
    extra += [zother(d) for d in range(1, nz)]
    greet(extra[::-1] + around)
    above, below, before, after = r > 0, r < rows - 1, c > 0, c < cols - 1

    def only(ok, value):
        return jnp.where(ok, value, jnp.zeros_like(value))

    win = (win_a, win_b)
    inner = pl.ds(RIM, n)
    loads = [
        (obj_ref.at[pl.ds(2 * l, 2), :, pl.ds(128 * t, 128)], win[l].at[:, t + 1, inner, :])
        for l in (0, 1)
        for t in (0, 1)
    ]
    loads += [
        (meas_in, meas_ref),
        (perm_in, perm_ref),
        (probe_in, probe_ref),
        (table_in, w_ref),
        (pos_in, pos_ref),
    ]
    loads = [pltpu.make_async_copy(a, b, load_sem.at[i]) for i, (a, b) in enumerate(loads)]
    for load in loads:
        load.start()
    quarter = lax.div(lax.broadcasted_iota(jnp.int32, (h, 128), 1), 32)
    for l in (0, 1):
        loads[2 * l].wait()
        loads[2 * l + 1].wait()

        def piece(t, k, l=l):
            return win[l][k % 2, t, RIM + h * (k // 2) : RIM + h * (k // 2) + h, :]

        pl_buf[l], pr_buf[l] = pack_sides(lambda k: piece(1, k), lambda k: piece(2, k), quarter)
    pl.semaphore_wait(pltpu.get_barrier_semaphore(), len(around) + len(extra))

    def landed(ref, sem):
        remote(ref, ref, sem, sem, partner).wait_recv()

    def left(ref, sem):
        remote(ref, ref, sem, sem, partner).wait_send()

    wave = win[0].at[0, pl.ds(0, 2), :, :]

    ups, tops = pl.ds(0, RIM), pl.ds(RIM, RIM)
    lows, downs = pl.ds(n, RIM), pl.ds(n + RIM, RIM)
    lo, hi = pl.ds(0, RIM), pl.ds(h - RIM, RIM)
    halo = [
        (
            around,
            [
                win[l].at[:, 1:3, tops, :], win[l].at[:, 1:3, lows, :], pl_buf.at[l], pr_buf.at[l],
                pl_buf.at[l, lo, :], pr_buf.at[l, lo, :], pl_buf.at[l, hi, :], pr_buf.at[l, hi, :],
            ],
            [win[l].at[:, 1:3, ups, :], win[l].at[:, 1:3, downs, :], hl.at[l], hr.at[l]]
            + [hc.at[l, k] for k in range(4)],
            send_halo.at[l],
            recv_halo.at[l],
        )
        for l in (0, 1)
    ]
    swap_rims(*halo[0], CORNERS + STRAIGHT)
    swap_rims(*halo[1], CORNERS + STRAIGHT)

    zeros = jnp.zeros((64, 128), jnp.float32)
    for p in range(npos):
        for q in range(4):
            for t in (0, 1):
                pad[p, q, t, 0:64, :] = zeros
                pad[p, q, t, 64 + n :, :] = zeros
    loads[4].wait()
    loads[5].wait()
    for p in range(npos):
        for t in (0, 1):
            seen[p, t] = meas_ref[p, :, 128 * t : 128 * t + 128]
        meas = jnp.concatenate(
            [
                jnp.concatenate([seen[p, t, pl.ds(i, h, stride=2), :] for t in (0, 1)], 1)
                for i in (0, 1)
            ],
            0,
        )
        mh, ml = parts(meas)
        meas_ref[p] = dot(
            jnp.concatenate([mh, ml], 1), jnp.concatenate([perm_ref[...], perm_ref[...]], 0)
        )
    for load in loads[6:]:
        load.wait()
    offs = [(pos_ref[0, 0, p, 0], pos_ref[0, 0, p, 1]) for p in range(npos)]
    lane = lax.broadcasted_iota(jnp.int32, (RIM, 128), 1)
    chunk = 2 * RIM
    long_lane = lax.broadcasted_iota(jnp.int32, (chunk, 128), 1)

    def cut_slice(l):
        landed(wave, recv_halo.at[l])
        left(wave, send_halo.at[l])
        for a in (0, 1):
            for t in (1, 2):
                win[l][a, t, 0:RIM, :] = only(above, win[l][a, t, 0:RIM, :])
                win[l][a, t, RIM + n :, :] = only(below, win[l][a, t, RIM + n :, :])
            for k in (0, 1):
                at = slice(RIM + h * k, RIM + h * k + h)
                win[l][a, 0, at, :] = only(before, turn(hl[l], 96 - 32 * (2 * k + a)))
                win[l][a, 3, at, :] = only(after, turn(hr[l], -32 * (2 * k + a)))
            for k, (row, ok) in enumerate(((0, above), (RIM + n, below))):
                lane_of = 32 * (2 * (1 - k) + a)
                at = slice(row, row + RIM)
                win[l][a, 0, at, :] = only(
                    jnp.logical_and(ok, before), turn(hc[l, 2 * k], 96 - lane_of)
                )
                win[l][a, 3, at, :] = only(jnp.logical_and(ok, after), turn(hc[l, 2 * k + 1], -lane_of))

        def cut_rows(i, carry):
            for p in range(npos):
                dy, dx = offs[p]
                shift = lax.rem(128 - dx, 128)
                high, low = long_lane >= 128 - dx, long_lane < -dx
                for a in (0, 1):
                    at = pl.ds(RIM + dy + i * chunk, chunk)
                    t0, t1, t2, t3 = [pltpu.roll(win[l][a, t, at, :], shift, 1) for t in range(4)]
                    to = rows_at(i * chunk, chunk)
                    cut[p, 2 * l + a, 0, to, :] = jnp.where(high, t2, jnp.where(low, t0, t1))
                    cut[p, 2 * l + a, 1, to, :] = jnp.where(high, t3, jnp.where(low, t1, t2))
            return carry

        lax.fori_loop(0, n // chunk, cut_rows, 0, unroll=True)

    def keep(p, q, value):
        pad[p, q, 0, 64 : 64 + n, :] = value[:, :128]
        pad[p, q, 1, 64 : 64 + n, :] = value[:, 128:]

    quarter = lax.div(lane, 32)

    def window_rows(l, a, start):
        sums = None
        for p in range(npos):
            dy, dx = offs[p]
            shift = lax.rem(128 + dx, 128)
            low, high = lane < dx, lane >= 128 + dx
            at = pl.ds(RIM - dy + start, RIM)
            u, v = (pltpu.roll(pad[p, 2 * l + a, t, at, :], shift, 1) for t in (0, 1))
            o = jnp.zeros_like(u)
            got = [
                jnp.where(high, u, o),
                jnp.where(low, o, jnp.where(high, v, u)),
                jnp.where(low, u, jnp.where(high, o, v)),
                jnp.where(low, v, o),
            ]
            sums = got if sums is None else [e + f for e, f in zip(sums, got)]
        return sums

    def place(l, starts):
        got = [window_rows(l, a, start) for start in starts for a in (0, 1)]
        for k, four in enumerate(got):
            to = rows_at(starts[k // 2], RIM)
            grad[2 * l + k % 2, 0, to, :] = four[1]
            grad[2 * l + k % 2, 1, to, :] = four[2]
        right, left = pack_sides(lambda k: got[k][3], lambda k: got[k][0], quarter)
        return left, right

    def place_steps(l):
        gcl[l], gcr[l] = place(l, (0, RIM + n))
        swap_rims(*rims[l], CORNERS + ALONG)
        for i in range(h // RIM):
            yield
            to = pl.ds(i * RIM, RIM)
            gl[l, to, :], gr[l, to, :] = place(l, (i * RIM + RIM, i * RIM + RIM + h))
        swap_rims(*rims[l], ACROSS)

    rims = [
        (
            around,
            [grad.at[pl.ds(2 * l, 2), :, ups, :], grad.at[pl.ds(2 * l, 2), :, downs, :], gl.at[l], gr.at[l]]
            + [gcl.at[l], gcr.at[l]] * 2,
            [rt.at[l], rb.at[l], rl.at[l], rr.at[l]] + [corners.at[l, k] for k in range(4)],
            send_rim.at[l],
            recv_rim.at[l],
        )
        for l in (0, 1)
    ]

    def first_pass(p):
        pr, pi = probe_ref[0], probe_ref[1]
        ar, ai = both(cut, p, 0), both(cut, p, 1)
        re, im = yield from sandwich(
            fold(pr * ar - pi * ai), fold(pr * ai + pi * ar), w_ref, *PROP
        )
        mid[p, 0], mid[p, 1] = unfold(re), unfold(im)

    def second_pass(p):
        qr, qi = mid[p, 0], mid[p, 1]
        br, bi = both(cut, p, 2), both(cut, p, 3)
        re, im = yield from sandwich(
            fold(qr * br - qi * bi), fold(qr * bi + qi * br), w_ref, *FORWARD
        )
        for i in (0, 1):
            for j in (0, 1):
                fr, fi = re[i][j], im[i][j]
                seen_at = meas_ref[p, i * h : (i + 1) * h, j * h : (j + 1) * h]
                ex = 2.0 * (fr * fr + fi * fi - seen_at)
                re[i][j], im[i][j] = ex * fr, ex * fi
        re, im = yield from sandwich(re, im, w_ref, *BACKWARD)
        hr_, hi_ = unfold(re), unfold(im)
        qr, qi = mid[p, 0], mid[p, 1]
        keep(p, 2, qr * hr_ + qi * hi_)
        keep(p, 3, qr * hi_ - qi * hr_)
        br, bi = both(cut, p, 2), both(cut, p, 3)
        mid[p, 0], mid[p, 1] = br * hr_ + bi * hi_, br * hi_ - bi * hr_

    def third_pass(p):
        re, im = yield from sandwich(fold(mid[p, 0]), fold(mid[p, 1]), w_ref, *PROP_CONJ)
        er, ei = unfold(re), unfold(im)
        pr, pi = probe_ref[0], probe_ref[1]
        keep(p, 0, pr * er + pi * ei)
        keep(p, 1, pr * ei - pi * er)
        ar, ai = both(cut, p, 0), both(cut, p, 1)
        if p == 0:
            gp_ref[0] = ar * er + ai * ei
            gp_ref[1] = ar * ei - ai * er
        else:
            gp_ref[0] += ar * er + ai * ei
            gp_ref[1] += ar * ei - ai * er

    cut_slice(0)
    staggered(*[first_pass(p) for p in range(npos)])
    cut_slice(1)
    staggered(*[second_pass(p) for p in range(npos)])
    staggered(*[third_pass(p) for p in range(npos)], place_steps(1))

    def band(q):
        return rows_at(q * step, step)

    def stripe(row):
        return rows_at(row * step * nx, step * nx)

    def pair(oy):
        at = stripe(lax.rem(y + oy, ny))
        return at, remote(gp_ref.at[1 - core, at, :], theirs.at[at, :], send_pair, recv_pair.at[oy], partner)

    for oy in distant(ny):
        pair(oy)[1].start()

    staggered(place_steps(0))

    for oy in distant(ny):
        at, copy = pair(oy)
        copy.wait_recv()
        ours[at, :] = gp_ref[core, at, :] + theirs[at, :]
        for ox in distant(nx):
            d = oy * nx + ox
            if d:
                q, where = peer(d)
                remote(ours.at[band(q), :], slots.at[d], send_xy, recv_xy, where).start()

    landed(slots.at[pl.ds(1, nxy - 1)], recv_xy)
    acc = ours[band(here), :]
    for d in range(1, nxy):
        acc = acc + slots[d]
    mine[...] = acc
    zslots[pl.ds(z, 1)] = acc[None]
    for d in far:
        remote(mine, zslots.at[z], send_z, recv_z, zpeer(d)).start()

    first_in = lane < jnp.where(before, 32, 0)
    final_in = lane >= jnp.where(after, 96, 128)
    zero = jnp.zeros((RIM, 128), jnp.float32)

    def rows_of(l, k, i):
        at, to = rows_at(i * RIM, RIM), rows_at(h * k + i * RIM + RIM, RIM)
        square = [None, None]
        for a in (0, 1):
            lane_of = 32 * (2 * k + a)
            ends = (
                jnp.where(first_in, turn(rl[l, at, :], -lane_of), zero),
                jnp.where(final_in, turn(rr[l, at, :], 96 - lane_of), zero),
            )
            for t in (0, 1):
                v = grad[2 * l + a, t, to, :] + ends[t]
                grad[2 * l + a, t, to, :] = v
                square[t] = v * v if square[t] is None else square[t] + v * v
        best = jnp.maximum(square[0], square[1])
        return functools.reduce(jnp.maximum, [best[8 * b : 8 * b + 8] for b in range(RIM // 8)])

    def add_edges(l):
        for edge, (strip, to, ok) in enumerate(((rt, RIM, above), (rb, n, below))):
            for a in (0, 1):
                lane_of = 32 * (2 * (1 - edge) + a)
                sides = (
                    jnp.where(first_in, turn(corners[l, 2 * edge], -lane_of), zero),
                    jnp.where(final_in, turn(corners[l, 2 * edge + 1], 96 - lane_of), zero),
                )
                for t in (0, 1):
                    grad[2 * l + a, t, to : to + RIM, :] += only(ok, strip[l, a, t] + sides[t])

    def finish_slice(l):
        landed(wave, recv_rim.at[l])
        left(wave, send_rim.at[l])
        add_edges(l)
        peak = jnp.zeros((8, 128), jnp.float32)
        for k in (0, 1):
            peak = lax.fori_loop(
                0, h // RIM, lambda i, m, k=k: jnp.maximum(m, rows_of(l, k, i)), peak, unroll=True
            )
        return peak

    xpeak[0] = jnp.maximum(finish_slice(1), finish_slice(0))
    for d in spread:
        remote(xpeak.at[0], xpeak.at[d], send_xm, recv_xm, peer(d)[1]).start()

    landed(zslots.at[pl.ds(0, nz - 1)], recv_z)
    acc = zslots[0]
    for k in range(1, nz):
        acc = acc + zslots[k]
    total_ref[pl.ds(core, 1), band(here), :] = acc[None]
    block = total_ref.at[core, band(here), :]
    for d in spread:
        remote(block, block, send_all, recv_all.at[d], peer(d)[1]).start()

    nearest = [0] + spread[::-1]
    forward_own = remote(block, block, send_back, recv_back, partner)
    forward_own.start()
    landed(xpeak.at[pl.ds(1, nxy - 1)], recv_xm)
    peak = xpeak[0]
    for d in range(1, nxy):
        peak = jnp.maximum(peak, xpeak[d])
    zpeak[0] = peak
    for d in far:
        remote(zpeak.at[0], zpeak.at[d], send_zm, recv_zm, zpeer(d)).start()
        remote(zpeak.at[0], zpeak.at[nz + d], send_zm, recv_zm, zother(d)).start()
    remote(zpeak.at[0], zpeak.at[nz], send_zm, recv_zm, partner).start()

    def forward(d):
        q = lax.rem(y + ny - d // nx, ny) * nx + lax.rem(x + nx - d % nx, nx)
        block = total_ref.at[core, band(q), :]
        landed(block, recv_all.at[d])
        remote(block, block, send_back, recv_back, partner).start()

    for d in nearest[1:]:
        forward(d)
    landed(zpeak.at[pl.ds(1, 2 * nz - 1)], recv_zm)
    peak = zpeak[0]
    for d in range(1, 2 * nz):
        peak = jnp.maximum(peak, zpeak[d])

    largest = jnp.max(peak, axis=(0, 1), keepdims=True)
    scale = jnp.broadcast_to(0.3 / (jnp.sqrt(largest) + 1e-06), (RIM, 128))

    def next_rows(i, carry):
        at = rows_at(i * RIM + RIM, RIM)
        for q in range(4):
            for t in (0, 1):
                obj_out[q, rows_at(i * RIM, RIM), 128 * t : 128 * t + 128] = (
                    win[q // 2][q % 2, t + 1, at, :] - scale * grad[q, t, at, :]
                )
        return carry

    lax.fori_loop(0, n // RIM, next_rows, 0, unroll=2)
    landed(total_ref.at[core], recv_back)
    probe_out[...] = probe_ref[...] - (2.0 / (rows * cols)) * total_ref[...]
    left(total_ref.at[core], send_back)
    left(total_ref.at[core], send_pair)
    left(slots.at[pl.ds(1, nxy - 1)], send_xy)
    left(slots.at[pl.ds(1, nxy - 1)], send_all)
    left(zslots.at[pl.ds(0, nz - 1)], send_z)
    left(zpeak.at[pl.ds(1, 2 * nz - 1)], send_zm)
    left(xpeak.at[pl.ds(1, nxy - 1)], send_xm)


def hand_out(object_ref, probe_ref, object_out, probe_out, sem):
    copies = [(object_ref.at[q], object_out.at[q]) for q in range(4)]
    copies += [(probe_ref.at[q], probe_out.at[q]) for q in range(2)]
    copies = [pltpu.make_async_copy(a, b, sem.at[i]) for i, (a, b) in enumerate(copies)]
    for copy in copies:
        copy.start()
    for copy in copies:
        copy.wait()


def local(rows, cols, nyx, table, perm, object_in, probe_in, positions, intensity):
    n = probe_in.shape[-1]
    npos = positions.shape[2]
    f32 = jnp.float32
    hbm = pl.BlockSpec(memory_space=pltpu.HBM)
    vmem = pl.BlockSpec(memory_space=pltpu.VMEM)
    dma = pltpu.SemaphoreType.DMA
    nxy = nyx[0] * nyx[1]
    nz = rows * cols // (CORES * nxy)
    step = n // nxy
    wide = n + 2 * RIM
    buffers = [
        (2, n, n), (npos, n, n), table.shape, perm.shape,
        (2, 4, wide, 128), (2, 4, wide, 128), (2, n // 2, 128), (2, n // 2, 128), (2, n // 2, 128), (2, n // 2, 128),
        (2, 4, RIM, 128),
        (npos, 4, 2, n, 128), (npos, 2, n, n), (npos, 4, 2, n + 128, 128), (npos, 2, n, 128),
        (4, 2, wide, 128), (2, n // 2, 128), (2, n // 2, 128), (2, RIM, 128), (2, RIM, 128), (2, n, n),
        (n, n), (n, n), (nxy, step, n), (step, n), (nz, step, n),
        (2 * nz, 8, 128), (nxy, 8, 128), (2, n, n),
        (2, 2, 2, RIM, 128), (2, 2, 2, RIM, 128), (2, n // 2, 128), (2, n // 2, 128), (2, 4, RIM, 128),
    ]
    scratch = [pltpu.SMEM(positions.shape, jnp.int32)]
    scratch += [VMEM(shape, jnp.bfloat16 if i in (2, 3) else f32) for i, shape in enumerate(buffers)]
    scratch += [dma((9,)), dma((2,)), dma((2,)), dma((2,)), dma((2,))]
    scratch += [dma, dma((nyx[0],)), dma, dma, dma, dma]
    scratch += [dma] * 4 + [dma, dma((nxy,)), dma, dma]
    object_out, probe_out = pl.pallas_call(
        functools.partial(kernel, rows, cols, nyx),
        out_shape=(jax.ShapeDtypeStruct((4, n, n), f32), jax.ShapeDtypeStruct((2, n, n), f32)),
        in_specs=[hbm] * 6,
        out_specs=(vmem, vmem),
        scratch_shapes=scratch,
        compiler_params=pltpu.CompilerParams(
            collective_id=0, has_side_effects=True, vmem_limit_bytes=28 * 2**20
        ),
        name="step",
    )(
        *(
            pltpu.with_memory_space_constraint(a, pltpu.HBM)
            for a in (
                positions, object_in.reshape(4, n, n), probe_in, intensity.reshape(npos, n, n),
                jnp.asarray(table), jnp.asarray(perm),
            )
        )
    )
    object_out, probe_out = pl.pallas_call(
        hand_out,
        out_shape=(jax.ShapeDtypeStruct((4, n, n), f32), jax.ShapeDtypeStruct((2, n, n), f32)),
        in_specs=[vmem, vmem],
        out_specs=(hbm, hbm),
        scratch_shapes=[dma((6,))],
        compiler_params=pltpu.CompilerParams(vmem_limit_bytes=2**20),
        name="hand_out",
    )(object_out, probe_out)
    return object_out.reshape(object_in.shape), probe_out


def solution(mesh):
    rows, cols = mesh.shape["row"], mesh.shape["col"]
    table, perm = weights(256)
    spec = (P(None, None, "row", "col"), P(), P("row", "col", None, None), P("row", "col", None, None, None))
    return jax.shard_map(
        functools.partial(local, rows, cols, NYX, table, perm),
        mesh=mesh,
        in_specs=spec,
        out_specs=(P(None, None, "row", "col"), P()),
        check_vma=False,
    )
```

```python
import functools
import math

import jax
import jax.numpy as jnp
import numpy as np
from jax import lax
from jax.experimental import pallas as pl
from jax.experimental.pallas import tpu as pltpu
from jax.sharding import PartitionSpec as P

RIM = 32
MESH = pl.DeviceIdType.MESH
VMEM = pltpu.VMEM
AROUND = ((-1, 0), (1, 0), (0, -1), (0, 1), (-1, -1), (-1, 1), (1, -1), (1, 1))
CORES = 2
NYX = (4, 4)


def split_of(matrix):
    high = matrix.astype(jnp.bfloat16)
    low = (matrix - high.astype(np.float64)).astype(jnp.bfloat16)
    return np.stack([np.asarray(high), np.asarray(low)])


def stacked(weight):
    real, imag = weight.real, weight.imag
    return np.block([[real, imag], [-imag, real]])


def weights(extent):
    half = extent // 2
    idx = np.arange(extent)
    freq = ((idx + half) % extent - half).astype(np.float64)
    turn = np.exp(-2j * np.pi * ((idx[:, None] * idx[None, :]) % extent) / extent)
    phase = np.exp(-8j * np.pi * freq**2 / extent**2)
    band = (np.conj(turn) * phase[None, :]) @ turn / extent
    left, right = band[:half, :half], band[:half, half:]
    even = turn[:half, 0::2] / math.sqrt(extent)
    odd = turn[:half, 1::2] / math.sqrt(extent)
    plus, minus = stacked((left + right) / 2), stacked((left - right) / 2)
    ev, od = stacked(even), stacked(odd)
    table = np.stack([split_of(m) for m in (plus, minus, ev, od, od.T)])
    order = np.concatenate([idx[0::2], idx[1::2]])
    perm = np.zeros((extent, extent), np.float32)
    perm[order, idx] = 1.0
    return table, perm.astype(jnp.bfloat16)


def parts(x):
    high = x.astype(jnp.bfloat16)
    return high, (x - high.astype(jnp.float32)).astype(jnp.bfloat16)


def dot(a, b):
    return jnp.dot(a, b, preferred_element_type=jnp.float32)


def times_right(split, w_ref, k):
    high, low = split
    wh, wl = w_ref[k, 0], w_ref[k, 1]
    rows = high.shape[0]
    y = dot(jnp.concatenate([high, low], 0), wh)
    return y[:rows] + (y[rows:] + dot(high, wl))


def times_left(split, w_ref, k):
    high, low = split
    wh, wl = w_ref[k, 0], w_ref[k, 1]
    rows = wh.shape[0]
    y = dot(jnp.concatenate([wh, wl], 0), high)
    return y[:rows] + (y[rows:] + dot(wh, low))


def fold(x):
    h = x.shape[0] // 2
    s, d = x[:h] + x[h:], x[:h] - x[h:]
    return [[s[:, :h] + s[:, h:], s[:, :h] - s[:, h:]], [d[:, :h] + d[:, h:], d[:, :h] - d[:, h:]]]


def unfold(b):
    top_s, top_d = b[0][0] + b[0][1], b[0][0] - b[0][1]
    bot_s, bot_d = b[1][0] + b[1][1], b[1][0] - b[1][1]
    s = jnp.concatenate([top_s, top_d], 1)
    d = jnp.concatenate([bot_s, bot_d], 1)
    return jnp.concatenate([s + d, s - d], 0)


def sandwich(re, im, w_ref, right, left):
    h = re[0][0].shape[0]
    split = []
    for j in (0, 1):
        first, second = (im, re) if right[j][1] else (re, im)
        x = jnp.concatenate(
            [jnp.concatenate([first[i][j], second[i][j]], 1) for i in (0, 1)], 0
        )
        split.append(parts(x))
    yield
    out = []
    for j in (0, 1):
        k, swap = right[j]
        y = times_right(split[j], w_ref, k)
        a, b = y[:, :h], y[:, h:]
        out.append((b, a) if swap else (a, b))
    yield
    split = []
    for i in (0, 1):
        rows = slice(i * h, (i + 1) * h)
        r = jnp.concatenate([out[0][0][rows], out[1][0][rows]], 1)
        m = jnp.concatenate([out[0][1][rows], out[1][1][rows]], 1)
        split.append(parts(jnp.concatenate([m, r] if left[i][1] else [r, m], 0)))
    yield
    res_re, res_im = [None, None], [None, None]
    for i in (0, 1):
        k, swap = left[i]
        y = times_left(split[i], w_ref, k)
        a, b = y[:h], y[h:]
        r, m = (b, a) if swap else (a, b)
        res_re[i] = [r[:, :h], r[:, h:]]
        res_im[i] = [m[:, :h], m[:, h:]]
    yield
    return res_re, res_im


def staggered(*runs):
    live = list(enumerate(runs))
    turn_of = 0
    while live:
        for item in list(live):
            lag, run = item
            if turn_of >= lag:
                try:
                    next(run)
                except StopIteration:
                    live.remove(item)
        turn_of += 1


PROP = (((0, False), (1, False)), ((0, True), (1, True)))
PROP_CONJ = (((0, True), (1, True)), ((0, False), (1, False)))
FORWARD = (((2, False), (3, False)), ((2, True), (4, False)))
BACKWARD = (((2, True), (4, False)), ((2, False), (3, False)))


def rows_at(start, size):
    if isinstance(start, int):
        return pl.ds(start, size)
    return pl.ds(pl.multiple_of(start, size), size)


def place_of():
    return lax.axis_index("row"), lax.axis_index("col")


def neighbours(rows, cols):
    r, c = place_of()
    return [(lax.rem(r + dr + rows, rows), lax.rem(c + dc + cols, cols)) for dr, dc in AROUND]


def opposite(d):
    dr, dc = AROUND[d]
    return AROUND.index((-dr, -dc))


def remote(src, dst, ssem, rsem, where):
    return pltpu.make_async_remote_copy(
        src_ref=src, dst_ref=dst, send_sem=ssem, recv_sem=rsem, device_id=where, device_id_type=MESH
    )


def greet(peers):
    for where in peers:
        pl.semaphore_signal(pltpu.get_barrier_semaphore(), inc=1, device_id=where, device_id_type=MESH)


CORNERS, STRAIGHT, ALONG, ACROSS = (4, 5, 6, 7), (0, 1, 2, 3), (0, 1), (2, 3)


def swap_rims(around, sources, targets, send_sem, recv_sem, these):
    for d in these:
        o = opposite(d)
        remote(sources[d], targets[o], send_sem, recv_sem, around[d]).start()


def both(ref, *at):
    return jnp.concatenate([ref[(*at, 0)], ref[(*at, 1)]], 1)


def distant(count):
    return sorted(range(count), key=lambda d: -min(d, count - d))


def turn(x, lanes):
    return pltpu.roll(x, lanes % 128, 1) if lanes % 128 else x


def pack_sides(first, last, quarter):
    left, right = first(0), turn(last(0), 32)
    for k in range(1, 4):
        left = jnp.where(quarter == k, turn(first(k), 32 * k), left)
        right = jnp.where(quarter == k, turn(last(k), 32 * k + 32), right)
    return left, right


def kernel(
    rows, cols, nyx,
    pos_in, obj_ref, probe_in, meas_in, table_in, perm_in,
    obj_out, probe_out,
    pos_ref, probe_ref, meas_ref, w_ref, perm_ref,
    win_a, win_b, pl_buf, pr_buf, hl, hr, hc,
    cut, mid, pad, seen,
    grad, gl, gr, gcl, gcr, gp_ref,
    theirs, ours, slots, mine, zslots, zpeak, xpeak, total_ref,
    rt, rb, rl, rr, corners,
    load_sem,
    send_halo, recv_halo, send_rim, recv_rim, send_pair, recv_pair, send_xy, recv_xy, send_z, recv_z,
    send_zm, recv_zm, send_xm, recv_xm, send_all, recv_all, send_back, recv_back,
):
    n = probe_ref.shape[-1]
    h = n // 2
    npos = cut.shape[0]
    ny, nx = nyx
    nxy = ny * nx
    nzl = cols // nxy
    nz = nzl * (rows // CORES)
    step = n // nxy
    r, c = place_of()
    core, zh = lax.rem(r, CORES), lax.div(r, CORES)
    zl, here = lax.div(c, nxy), lax.rem(c, nxy)
    y, x = lax.div(here, nx), lax.rem(here, nx)
    z = zh * nzl + zl
    partner = (zh * CORES + 1 - core, c)

    def peer(d):
        q = lax.rem(y + d // nx, ny) * nx + lax.rem(x + d % nx, nx)
        return q, (r, zl * nxy + q)

    def zpeer(d):
        k = lax.rem(z + d, nz)
        return lax.div(k, nzl) * CORES + core, lax.rem(k, nzl) * nxy + here

    def zother(d):
        k = lax.rem(z + d, nz)
        return lax.div(k, nzl) * CORES + 1 - core, lax.rem(k, nzl) * nxy + here

    far = distant(nz)[:-1]
    spread = sorted(range(1, nxy), key=lambda d: -min(d // nx, ny - d // nx) - min(d % nx, nx - d % nx))

    around = neighbours(rows, cols)
    extra = [partner]
    extra += [peer(d)[1] for d in range(1, nxy)]
    extra += [zpeer(d) for d in range(1, nz)]
    extra += [zother(d) for d in range(1, nz)]
    greet(extra[::-1] + around)
    above, below, before, after = r > 0, r < rows - 1, c > 0, c < cols - 1

    def only(ok, value):
        return jnp.where(ok, value, jnp.zeros_like(value))

    win = (win_a, win_b)
    inner = pl.ds(RIM, n)
    loads = [
        (obj_ref.at[pl.ds(2 * l, 2), :, pl.ds(128 * t, 128)], win[l].at[:, t + 1, inner, :])
        for l in (0, 1)
        for t in (0, 1)
    ]
    loads += [
        (meas_in, meas_ref),
        (perm_in, perm_ref),
        (probe_in, probe_ref),
        (table_in, w_ref),
        (pos_in, pos_ref),
    ]
    loads = [pltpu.make_async_copy(a, b, load_sem.at[i]) for i, (a, b) in enumerate(loads)]
    for load in loads:
        load.start()
    quarter = lax.div(lax.broadcasted_iota(jnp.int32, (h, 128), 1), 32)
    for l in (0, 1):
        loads[2 * l].wait()
        loads[2 * l + 1].wait()

        def piece(t, k, l=l):
            return win[l][k % 2, t, RIM + h * (k // 2) : RIM + h * (k // 2) + h, :]

        pl_buf[l], pr_buf[l] = pack_sides(lambda k: piece(1, k), lambda k: piece(2, k), quarter)
    pl.semaphore_wait(pltpu.get_barrier_semaphore(), len(around) + len(extra))

    def landed(ref, sem):
        remote(ref, ref, sem, sem, partner).wait_recv()

    def left(ref, sem):
        remote(ref, ref, sem, sem, partner).wait_send()

    wave = win[0].at[0, pl.ds(0, 2), :, :]

    ups, tops = pl.ds(0, RIM), pl.ds(RIM, RIM)
    lows, downs = pl.ds(n, RIM), pl.ds(n + RIM, RIM)
    lo, hi = pl.ds(0, RIM), pl.ds(h - RIM, RIM)
    halo = [
        (
            around,
            [
                win[l].at[:, 1:3, tops, :], win[l].at[:, 1:3, lows, :], pl_buf.at[l], pr_buf.at[l],
                pl_buf.at[l, lo, :], pr_buf.at[l, lo, :], pl_buf.at[l, hi, :], pr_buf.at[l, hi, :],
            ],
            [win[l].at[:, 1:3, ups, :], win[l].at[:, 1:3, downs, :], hl.at[l], hr.at[l]]
            + [hc.at[l, k] for k in range(4)],
            send_halo.at[l],
            recv_halo.at[l],
        )
        for l in (0, 1)
    ]
    swap_rims(*halo[0], CORNERS + STRAIGHT)
    swap_rims(*halo[1], CORNERS + STRAIGHT)

    zeros = jnp.zeros((64, 128), jnp.float32)
    for p in range(npos):
        for q in range(4):
            for t in (0, 1):
                pad[p, q, t, 0:64, :] = zeros
                pad[p, q, t, 64 + n :, :] = zeros
    loads[4].wait()
    loads[5].wait()
    for p in range(npos):
        for t in (0, 1):
            seen[p, t] = meas_ref[p, :, 128 * t : 128 * t + 128]
        meas = jnp.concatenate(
            [
                jnp.concatenate([seen[p, t, pl.ds(i, h, stride=2), :] for t in (0, 1)], 1)
                for i in (0, 1)
            ],
            0,
        )
        mh, ml = parts(meas)
        meas_ref[p] = dot(
            jnp.concatenate([mh, ml], 1), jnp.concatenate([perm_ref[...], perm_ref[...]], 0)
        )
    for load in loads[6:]:
        load.wait()
    offs = [(pos_ref[0, 0, p, 0], pos_ref[0, 0, p, 1]) for p in range(npos)]
    lane = lax.broadcasted_iota(jnp.int32, (RIM, 128), 1)
    chunk = 2 * RIM
    long_lane = lax.broadcasted_iota(jnp.int32, (chunk, 128), 1)

    def cut_slice(l):
        landed(wave, recv_halo.at[l])
        left(wave, send_halo.at[l])
        for a in (0, 1):
            for t in (1, 2):
                win[l][a, t, 0:RIM, :] = only(above, win[l][a, t, 0:RIM, :])
                win[l][a, t, RIM + n :, :] = only(below, win[l][a, t, RIM + n :, :])
            for k in (0, 1):
                at = slice(RIM + h * k, RIM + h * k + h)
                win[l][a, 0, at, :] = only(before, turn(hl[l], 96 - 32 * (2 * k + a)))
                win[l][a, 3, at, :] = only(after, turn(hr[l], -32 * (2 * k + a)))
            for k, (row, ok) in enumerate(((0, above), (RIM + n, below))):
                lane_of = 32 * (2 * (1 - k) + a)
                at = slice(row, row + RIM)
                win[l][a, 0, at, :] = only(
                    jnp.logical_and(ok, before), turn(hc[l, 2 * k], 96 - lane_of)
                )
                win[l][a, 3, at, :] = only(jnp.logical_and(ok, after), turn(hc[l, 2 * k + 1], -lane_of))

        def cut_rows(i, carry):
            for p in range(npos):
                dy, dx = offs[p]
                shift = lax.rem(128 - dx, 128)
                high, low = long_lane >= 128 - dx, long_lane < -dx
                for a in (0, 1):
                    at = pl.ds(RIM + dy + i * chunk, chunk)
                    t0, t1, t2, t3 = [pltpu.roll(win[l][a, t, at, :], shift, 1) for t in range(4)]
                    to = rows_at(i * chunk, chunk)
                    cut[p, 2 * l + a, 0, to, :] = jnp.where(high, t2, jnp.where(low, t0, t1))
                    cut[p, 2 * l + a, 1, to, :] = jnp.where(high, t3, jnp.where(low, t1, t2))
            return carry

        lax.fori_loop(0, n // chunk, cut_rows, 0, unroll=True)

    def keep(p, q, value):
        pad[p, q, 0, 64 : 64 + n, :] = value[:, :128]
        pad[p, q, 1, 64 : 64 + n, :] = value[:, 128:]

    quarter = lax.div(lane, 32)

    def window_rows(l, a, start):
        sums = None
        for p in range(npos):
            dy, dx = offs[p]
            shift = lax.rem(128 + dx, 128)
            low, high = lane < dx, lane >= 128 + dx
            at = pl.ds(RIM - dy + start, RIM)
            u, v = (pltpu.roll(pad[p, 2 * l + a, t, at, :], shift, 1) for t in (0, 1))
            o = jnp.zeros_like(u)
            got = [
                jnp.where(high, u, o),
                jnp.where(low, o, jnp.where(high, v, u)),
                jnp.where(low, u, jnp.where(high, o, v)),
                jnp.where(low, v, o),
            ]
            sums = got if sums is None else [e + f for e, f in zip(sums, got)]
        return sums

    def place(l, starts):
        got = [window_rows(l, a, start) for start in starts for a in (0, 1)]
        for k, four in enumerate(got):
            to = rows_at(starts[k // 2], RIM)
            grad[2 * l + k % 2, 0, to, :] = four[1]
            grad[2 * l + k % 2, 1, to, :] = four[2]
        right, left = pack_sides(lambda k: got[k][3], lambda k: got[k][0], quarter)
        return left, right

    def place_steps(l):
        gcl[l], gcr[l] = place(l, (0, RIM + n))
        swap_rims(*rims[l], CORNERS + ALONG)
        for i in range(h // RIM):
            yield
            to = pl.ds(i * RIM, RIM)
            gl[l, to, :], gr[l, to, :] = place(l, (i * RIM + RIM, i * RIM + RIM + h))
        swap_rims(*rims[l], ACROSS)

    rims = [
        (
            around,
            [grad.at[pl.ds(2 * l, 2), :, ups, :], grad.at[pl.ds(2 * l, 2), :, downs, :], gl.at[l], gr.at[l]]
            + [gcl.at[l], gcr.at[l]] * 2,
            [rt.at[l], rb.at[l], rl.at[l], rr.at[l]] + [corners.at[l, k] for k in range(4)],
            send_rim.at[l],
            recv_rim.at[l],
        )
        for l in (0, 1)
    ]

    def first_pass(p):
        pr, pi = probe_ref[0], probe_ref[1]
        ar, ai = both(cut, p, 0), both(cut, p, 1)
        re, im = yield from sandwich(
            fold(pr * ar - pi * ai), fold(pr * ai + pi * ar), w_ref, *PROP
        )
        mid[p, 0], mid[p, 1] = unfold(re), unfold(im)

    def second_pass(p):
        qr, qi = mid[p, 0], mid[p, 1]
        br, bi = both(cut, p, 2), both(cut, p, 3)
        re, im = yield from sandwich(
            fold(qr * br - qi * bi), fold(qr * bi + qi * br), w_ref, *FORWARD
        )
        for i in (0, 1):
            for j in (0, 1):
                fr, fi = re[i][j], im[i][j]
                seen_at = meas_ref[p, i * h : (i + 1) * h, j * h : (j + 1) * h]
                ex = 2.0 * (fr * fr + fi * fi - seen_at)
                re[i][j], im[i][j] = ex * fr, ex * fi
        re, im = yield from sandwich(re, im, w_ref, *BACKWARD)
        hr_, hi_ = unfold(re), unfold(im)
        qr, qi = mid[p, 0], mid[p, 1]
        keep(p, 2, qr * hr_ + qi * hi_)
        keep(p, 3, qr * hi_ - qi * hr_)
        br, bi = both(cut, p, 2), both(cut, p, 3)
        mid[p, 0], mid[p, 1] = br * hr_ + bi * hi_, br * hi_ - bi * hr_

    def third_pass(p):
        re, im = yield from sandwich(fold(mid[p, 0]), fold(mid[p, 1]), w_ref, *PROP_CONJ)
        er, ei = unfold(re), unfold(im)
        pr, pi = probe_ref[0], probe_ref[1]
        keep(p, 0, pr * er + pi * ei)
        keep(p, 1, pr * ei - pi * er)
        ar, ai = both(cut, p, 0), both(cut, p, 1)
        if p == 0:
            gp_ref[0] = ar * er + ai * ei
            gp_ref[1] = ar * ei - ai * er
        else:
            gp_ref[0] += ar * er + ai * ei
            gp_ref[1] += ar * ei - ai * er

    cut_slice(0)
    staggered(*[first_pass(p) for p in range(npos)])
    cut_slice(1)
    staggered(*[second_pass(p) for p in range(npos)])
    staggered(*[third_pass(p) for p in range(npos)], place_steps(1))

    def band(q):
        return rows_at(q * step, step)

    def stripe(row):
        return rows_at(row * step * nx, step * nx)

    def pair(oy):
        at = stripe(lax.rem(y + oy, ny))
        return at, remote(gp_ref.at[1 - core, at, :], theirs.at[at, :], send_pair, recv_pair.at[oy], partner)

    for oy in distant(ny):
        pair(oy)[1].start()

    staggered(place_steps(0))

    for oy in distant(ny):
        at, copy = pair(oy)
        copy.wait_recv()
        ours[at, :] = gp_ref[core, at, :] + theirs[at, :]
        for ox in distant(nx):
            d = oy * nx + ox
            if d:
                q, where = peer(d)
                remote(ours.at[band(q), :], slots.at[d], send_xy, recv_xy, where).start()

    first_in = lane < jnp.where(before, 32, 0)
    final_in = lane >= jnp.where(after, 96, 128)
    zero = jnp.zeros((RIM, 128), jnp.float32)

    def rows_of(l, k, i):
        at, to = rows_at(i * RIM, RIM), rows_at(h * k + i * RIM + RIM, RIM)
        square = [None, None]
        for a in (0, 1):
            lane_of = 32 * (2 * k + a)
            ends = (
                jnp.where(first_in, turn(rl[l, at, :], -lane_of), zero),
                jnp.where(final_in, turn(rr[l, at, :], 96 - lane_of), zero),
            )
            for t in (0, 1):
                v = grad[2 * l + a, t, to, :] + ends[t]
                grad[2 * l + a, t, to, :] = v
                square[t] = v * v if square[t] is None else square[t] + v * v
        best = jnp.maximum(square[0], square[1])
        return functools.reduce(jnp.maximum, [best[8 * b : 8 * b + 8] for b in range(RIM // 8)])

    def add_edges(l):
        for edge, (strip, to, ok) in enumerate(((rt, RIM, above), (rb, n, below))):
            for a in (0, 1):
                lane_of = 32 * (2 * (1 - edge) + a)
                sides = (
                    jnp.where(first_in, turn(corners[l, 2 * edge], -lane_of), zero),
                    jnp.where(final_in, turn(corners[l, 2 * edge + 1], 96 - lane_of), zero),
                )
                for t in (0, 1):
                    grad[2 * l + a, t, to : to + RIM, :] += only(ok, strip[l, a, t] + sides[t])

    def finish_slice(l):
        landed(wave, recv_rim.at[l])
        left(wave, send_rim.at[l])
        add_edges(l)
        peak = jnp.zeros((8, 128), jnp.float32)
        for k in (0, 1):
            peak = lax.fori_loop(
                0, h // RIM, lambda i, m, k=k: jnp.maximum(m, rows_of(l, k, i)), peak, unroll=True
            )
        return peak

    early = finish_slice(1)

    landed(slots.at[pl.ds(1, nxy - 1)], recv_xy)
    acc = ours[band(here), :]
    for d in range(1, nxy):
        acc = acc + slots[d]
    mine[...] = acc
    zslots[pl.ds(z, 1)] = acc[None]
    for d in far:
        remote(mine, zslots.at[z], send_z, recv_z, zpeer(d)).start()

    xpeak[0] = jnp.maximum(early, finish_slice(0))
    for d in spread:
        remote(xpeak.at[0], xpeak.at[d], send_xm, recv_xm, peer(d)[1]).start()

    landed(zslots.at[pl.ds(0, nz - 1)], recv_z)
    acc = zslots[0]
    for k in range(1, nz):
        acc = acc + zslots[k]
    total_ref[pl.ds(core, 1), band(here), :] = acc[None]
    block = total_ref.at[core, band(here), :]
    for d in spread:
        remote(block, block, send_all, recv_all.at[d], peer(d)[1]).start()

    nearest = [0] + spread[::-1]
    forward_own = remote(block, block, send_back, recv_back, partner)
    forward_own.start()
    landed(xpeak.at[pl.ds(1, nxy - 1)], recv_xm)
    peak = xpeak[0]
    for d in range(1, nxy):
        peak = jnp.maximum(peak, xpeak[d])
    zpeak[0] = peak
    for d in far:
        remote(zpeak.at[0], zpeak.at[d], send_zm, recv_zm, zpeer(d)).start()
        remote(zpeak.at[0], zpeak.at[nz + d], send_zm, recv_zm, zother(d)).start()
    remote(zpeak.at[0], zpeak.at[nz], send_zm, recv_zm, partner).start()

    def forward(d):
        q = lax.rem(y + ny - d // nx, ny) * nx + lax.rem(x + nx - d % nx, nx)
        block = total_ref.at[core, band(q), :]
        landed(block, recv_all.at[d])
        remote(block, block, send_back, recv_back, partner).start()

    for d in nearest[1:]:
        forward(d)
    landed(zpeak.at[pl.ds(1, 2 * nz - 1)], recv_zm)
    peak = zpeak[0]
    for d in range(1, 2 * nz):
        peak = jnp.maximum(peak, zpeak[d])

    largest = jnp.max(peak, axis=(0, 1), keepdims=True)
    scale = jnp.broadcast_to(0.3 / (jnp.sqrt(largest) + 1e-06), (RIM, 128))

    def next_rows(i, carry):
        at = rows_at(i * RIM + RIM, RIM)
        for q in range(4):
            for t in (0, 1):
                obj_out[q, rows_at(i * RIM, RIM), 128 * t : 128 * t + 128] = (
                    win[q // 2][q % 2, t + 1, at, :] - scale * grad[q, t, at, :]
                )
        return carry

    lax.fori_loop(0, n // RIM, next_rows, 0, unroll=2)
    landed(total_ref.at[core], recv_back)
    probe_out[...] = probe_ref[...] - (2.0 / (rows * cols)) * total_ref[...]
    left(total_ref.at[core], send_back)
    left(total_ref.at[core], send_pair)
    left(slots.at[pl.ds(1, nxy - 1)], send_xy)
    left(slots.at[pl.ds(1, nxy - 1)], send_all)
    left(zslots.at[pl.ds(0, nz - 1)], send_z)
    left(zpeak.at[pl.ds(1, 2 * nz - 1)], send_zm)
    left(xpeak.at[pl.ds(1, nxy - 1)], send_xm)


def hand_out(object_ref, probe_ref, object_out, probe_out, sem):
    copies = [(object_ref.at[q], object_out.at[q]) for q in range(4)]
    copies += [(probe_ref.at[q], probe_out.at[q]) for q in range(2)]
    copies = [pltpu.make_async_copy(a, b, sem.at[i]) for i, (a, b) in enumerate(copies)]
    for copy in copies:
        copy.start()
    for copy in copies:
        copy.wait()


def local(rows, cols, nyx, table, perm, object_in, probe_in, positions, intensity):
    n = probe_in.shape[-1]
    npos = positions.shape[2]
    f32 = jnp.float32
    hbm = pl.BlockSpec(memory_space=pltpu.HBM)
    vmem = pl.BlockSpec(memory_space=pltpu.VMEM)
    dma = pltpu.SemaphoreType.DMA
    nxy = nyx[0] * nyx[1]
    nz = rows * cols // (CORES * nxy)
    step = n // nxy
    wide = n + 2 * RIM
    buffers = [
        (2, n, n), (npos, n, n), table.shape, perm.shape,
        (2, 4, wide, 128), (2, 4, wide, 128), (2, n // 2, 128), (2, n // 2, 128), (2, n // 2, 128), (2, n // 2, 128),
        (2, 4, RIM, 128),
        (npos, 4, 2, n, 128), (npos, 2, n, n), (npos, 4, 2, n + 128, 128), (npos, 2, n, 128),
        (4, 2, wide, 128), (2, n // 2, 128), (2, n // 2, 128), (2, RIM, 128), (2, RIM, 128), (2, n, n),
        (n, n), (n, n), (nxy, step, n), (step, n), (nz, step, n),
        (2 * nz, 8, 128), (nxy, 8, 128), (2, n, n),
        (2, 2, 2, RIM, 128), (2, 2, 2, RIM, 128), (2, n // 2, 128), (2, n // 2, 128), (2, 4, RIM, 128),
    ]
    scratch = [pltpu.SMEM(positions.shape, jnp.int32)]
    scratch += [VMEM(shape, jnp.bfloat16 if i in (2, 3) else f32) for i, shape in enumerate(buffers)]
    scratch += [dma((9,)), dma((2,)), dma((2,)), dma((2,)), dma((2,))]
    scratch += [dma, dma((nyx[0],)), dma, dma, dma, dma]
    scratch += [dma] * 4 + [dma, dma((nxy,)), dma, dma]
    object_out, probe_out = pl.pallas_call(
        functools.partial(kernel, rows, cols, nyx),
        out_shape=(jax.ShapeDtypeStruct((4, n, n), f32), jax.ShapeDtypeStruct((2, n, n), f32)),
        in_specs=[hbm] * 6,
        out_specs=(vmem, vmem),
        scratch_shapes=scratch,
        compiler_params=pltpu.CompilerParams(
            collective_id=0, has_side_effects=True, vmem_limit_bytes=28 * 2**20
        ),
        name="step",
    )(
        *(
            pltpu.with_memory_space_constraint(a, pltpu.HBM)
            for a in (
                positions, object_in.reshape(4, n, n), probe_in, intensity.reshape(npos, n, n),
                jnp.asarray(table), jnp.asarray(perm),
            )
        )
    )
    object_out, probe_out = pl.pallas_call(
        hand_out,
        out_shape=(jax.ShapeDtypeStruct((4, n, n), f32), jax.ShapeDtypeStruct((2, n, n), f32)),
        in_specs=[vmem, vmem],
        out_specs=(hbm, hbm),
        scratch_shapes=[dma((6,))],
        compiler_params=pltpu.CompilerParams(vmem_limit_bytes=2**20),
        name="hand_out",
    )(object_out, probe_out)
    return object_out.reshape(object_in.shape), probe_out


def solution(mesh):
    rows, cols = mesh.shape["row"], mesh.shape["col"]
    table, perm = weights(256)
    spec = (P(None, None, "row", "col"), P(), P("row", "col", None, None), P("row", "col", None, None, None))
    return jax.shard_map(
        functools.partial(local, rows, cols, NYX, table, perm),
        mesh=mesh,
        in_specs=spec,
        out_specs=(P(None, None, "row", "col"), P()),
        check_vma=False,
    )
```
